32 devices in a mesh: ctx: 8 (over z, y), head: 4 (over x, core).
Axes of the slice: x: 2, y: 2, z: 4, core: 2. Of those that a mesh axis runs over, the one named last changes fastest.
Arguments:
- queries: bfloat16 [8192, 1024], P('ctx', 'head'), may hold values from -6 to 6
- keys: bfloat16 [8192, 1024], P('ctx', 'head'), may hold values from -1.7 to 1.7
- values: bfloat16 [8192, 1024], P('ctx', 'head'), may hold values from -6 to 6
- w_out: bfloat16 [1024, 2048], P('head'), may hold values from -0.1875 to 0.1875
- cotangent: bfloat16 [8192, 2048], P('ctx', 'head'), may hold values from -6 to 6
Outputs:
- layer_out: bfloat16 [8192, 2048], P('ctx', 'head')
- grad_queries: bfloat16 [8192, 1024], P('ctx', 'head')
- grad_keys: bfloat16 [8192, 1024], P('ctx', 'head')
- grad_values: bfloat16 [8192, 1024], P('ctx', 'head')
- grad_weight: float32 [1024, 2048], P('head', 'ctx')
The draws below stay inside these ranges and needn't reach their ends.
All inputs are finite; a program needn't handle non-finite values.
Results may differ from the reference program's by a relative error of at most 0.014.
Values may be sent and summed in bfloat16 or wider, within the bound.
No kernel may reach another device: no remote copies, remote signals or barrier semaphores. Data moves between devices by JAX's collectives and lax.ppermute only.
A program may use at most 128 MiB of HBM per device.

```python
import jax
import jax.numpy as jnp
from jax import lax

HDIM = 128
D = 2048
SPAN = 256
NEWTON = 8
HEADS = 8
TOKENS = 8192


def draw_keys(key, part):
    scale_key, entry_key = jax.random.split(jax.random.fold_in(key, 11))
    columns = HEADS * HDIM
    spread = jax.random.uniform(scale_key, (columns,), jnp.float32, -2.5, 2.5)
    entries = jax.random.truncated_normal(entry_key, -6.0, 6.0, (TOKENS, columns), jnp.float32)
    return (0.023 * jnp.exp(spread)[None, :] * entries).astype(jnp.bfloat16)


def block_scale(rng, shape, cuts, least, top_value):
    level = 1.0
    for position, blocks in cuts:
        draws = jax.random.uniform(jax.random.fold_in(jax.random.fold_in(rng, 6), position), (blocks,), jnp.float32, least / len(cuts), top_value / len(cuts))
        level = level * jnp.repeat(jnp.exp(draws), shape[position] // blocks).reshape((-1,) + (1,) * (len(shape) - 1 - position))
    return level


def centred(stream_key, shape, width, limit, cuts=(), kind=jnp.bfloat16):
    result = width * jax.random.normal(stream_key, shape, jnp.float32)
    if cuts:
        result = result * block_scale(stream_key, shape, cuts, -0.22, 0.18)
    return jnp.clip(result, -limit, limit).astype(kind)


def setup_inputs(seed: int = 0) -> dict:
    streams_of = jax.random.split(jax.random.key(seed), 6)
    return {
        "queries": centred(streams_of[0], (TOKENS, HEADS * HDIM), 1.0, 6.0, ((0, 8), (1, 4))),
        "keys": draw_keys(jax.random.fold_in(streams_of[5], 71), 0),
        "values": centred(streams_of[2], (TOKENS, HEADS * HDIM), 1.0, 6.0, ((0, 8), (1, 4))),
        "w_out": centred(streams_of[3], (HEADS * HDIM, D), (HEADS * HDIM) ** -0.5, 0.1875, ((0, 4),)),
        "cotangent": centred(streams_of[4], (TOKENS, D), 1.0, 6.0, ((0, 8), (1, 4))),
    }


RIDGE = 1.0
HIGH = lax.Precision.HIGHEST

def newton_inverse(matrix):
    size = matrix.shape[0]
    unit_matrix = jnp.eye(size, dtype=jnp.float32)
    approx = unit_matrix / jnp.sqrt(jnp.sum(matrix * matrix))
    for step in range(NEWTON):
        product = jnp.dot(matrix, approx, precision=HIGH)
        approx = jnp.dot(approx, 2.0 * unit_matrix - product, precision=HIGH)
    return approx

def block_output(block_q, block_k, block_v, gram, memory):
    size = gram.shape[0]
    ridged = gram + RIDGE * jnp.eye(size, dtype=jnp.float32)
    inverse = newton_inverse(ridged)
    solved = jnp.dot(block_q, inverse, precision=HIGH)
    scores = jnp.dot(solved, block_k.T, precision=HIGH)
    length = scores.shape[0]
    causal = jnp.arange(length)[:, None] >= jnp.arange(length)[None, :]
    scores = jnp.where(causal, scores, jnp.zeros_like(scores))
    return jnp.dot(scores, block_v, precision=HIGH) + jnp.dot(solved, memory.T, precision=HIGH)

def exclusive_forward(blocks):
    running = jnp.cumsum(blocks, axis=0)
    return jnp.concatenate([jnp.zeros_like(blocks[:1]), running[:-1]], axis=0)

def exclusive_backward(blocks):
    running = jnp.cumsum(blocks[::-1], axis=0)[::-1]
    return jnp.concatenate([running[1:], jnp.zeros_like(blocks[:1])], axis=0)

def head_pass(stacked):
    head_q, head_k, head_v, head_grad = stacked
    blocks = head_q.shape[0] // SPAN
    q_float = head_q.astype(jnp.float32).reshape(blocks, SPAN, HDIM)
    k_float = head_k.astype(jnp.float32).reshape(blocks, SPAN, HDIM)
    v_float = head_v.astype(jnp.float32).reshape(blocks, SPAN, HDIM)
    grams = jnp.einsum('cti,ctj->cij', k_float, k_float, precision=HIGH)
    pairs = jnp.einsum('cti,ctj->cij', v_float, k_float, precision=HIGH)
    gram_prefix = exclusive_forward(grams)
    pair_prefix = exclusive_forward(pairs)
    outputs, pullback = jax.vjp(jax.vmap(block_output), q_float, k_float, v_float, gram_prefix, pair_prefix)
    grad_out = head_grad.astype(jnp.float32).reshape(blocks, SPAN, HDIM)
    d_query, d_key, d_value, d_gram, d_pair = pullback(grad_out)
    gram_suffix = exclusive_backward(d_gram)
    pair_suffix = exclusive_backward(d_pair)
    symmetric = gram_suffix + jnp.swapaxes(gram_suffix, 1, 2)
    d_key = d_key + jnp.einsum('cti,cij->ctj', k_float, symmetric, precision=HIGH)
    d_key = d_key + jnp.einsum('cti,cij->ctj', v_float, pair_suffix, precision=HIGH)
    d_value = d_value + jnp.einsum('ctj,cij->cti', k_float, pair_suffix, precision=HIGH)
    shape = (blocks * SPAN, HDIM)
    return (outputs.reshape(shape).astype(jnp.bfloat16), d_query.reshape(shape).astype(jnp.bfloat16), d_key.reshape(shape).astype(jnp.bfloat16), d_value.reshape(shape).astype(jnp.bfloat16))

def by_head(array):
    return array.reshape(TOKENS, HEADS, HDIM).transpose(1, 0, 2)

def from_head(array):
    return array.transpose(1, 0, 2).reshape(TOKENS, HEADS * HDIM)

def reference(queries, keys, values, w_out, cotangent):
    grad_heads = jnp.dot(cotangent, w_out.T, preferred_element_type=jnp.float32).astype(jnp.bfloat16)
    results = lax.map(head_pass, (by_head(queries), by_head(keys), by_head(values), by_head(grad_heads)))
    heads_out = from_head(results[0])
    layer_out = jnp.dot(heads_out, w_out, preferred_element_type=jnp.float32).astype(jnp.bfloat16)
    grad_weight = jnp.dot(heads_out.T, cotangent, preferred_element_type=jnp.float32)
    return (layer_out, from_head(results[1]), from_head(results[2]), from_head(results[3]), grad_weight)
```

```python
import functools

import jax
import jax.numpy as jnp
from jax import lax
from jax.experimental import pallas as pl
from jax.experimental.pallas import tpu as pltpu
from jax.sharding import PartitionSpec as P

HDIM = 128
SPAN = 256
NEWTON = 8
RIDGE = 1.0
F32 = jnp.float32
BF16 = jnp.bfloat16
VMEM_SPEC = pl.BlockSpec(memory_space=pltpu.VMEM)
SMEM_SPEC = pl.BlockSpec(memory_space=pltpu.SMEM)


def dot(left, right, axes=(1, 0)):
    return lax.dot_general(
        left, right, (((axes[0],), (axes[1],)), ((), ())), preferred_element_type=F32
    )


def split(value):
    high = value.astype(BF16)
    return high, (value - high.astype(F32)).astype(BF16)


def cat(parts, axis):
    return jnp.concatenate(parts, axis=axis)


def params(limit=60):
    return pltpu.CompilerParams(vmem_limit_bytes=limit * 1024 * 1024)


def cost(flops, size):
    return pl.CostEstimate(flops=flops, bytes_accessed=size, transcendentals=0)


def shape(dims, dtype=F32):
    return jax.ShapeDtypeStruct(dims, dtype)


def unit():
    rows = lax.broadcasted_iota(jnp.int32, (HDIM, HDIM), 0)
    cols = lax.broadcasted_iota(jnp.int32, (HDIM, HDIM), 1)
    return rows == cols


def causal():
    rows = lax.broadcasted_iota(jnp.int32, (SPAN, SPAN), 0)
    cols = lax.broadcasted_iota(jnp.int32, (SPAN, SPAN), 1)
    return rows >= cols


def totals_kernel(k_ref, v_ref, g_ref, n_ref):
    for h in range(g_ref.shape[0]):
        cols = slice(h * HDIM, (h + 1) * HDIM)
        k = k_ref[:, cols]
        both = dot(k, cat([k, v_ref[:, cols]], 1), (0, 0))
        g_ref[h] = both[:, :HDIM]
        n_ref[h] = both[:, HDIM:]


def totals(keys, values, heads):
    state = shape((heads, HDIM, HDIM))
    return pl.pallas_call(
        totals_kernel,
        out_shape=(state, state),
        in_specs=[VMEM_SPEC] * 2,
        out_specs=(VMEM_SPEC, VMEM_SPEC),
        compiler_params=params(),
        cost_estimate=cost(2 * 2 * keys.size * HDIM, 4 * keys.size),
    )(keys, values)


def primal_kernel(
    q_ref, k_ref, v_ref, g_ref, n_ref, out_ref, e_ref, x_ref, last_ref, a_ref, pre_ref, es, xs
):
    blocks = a_ref.shape[1]
    eye = unit()
    gram, pair = g_ref[0], n_ref[0]
    for b in range(blocks):
        rows = slice(b * SPAN, (b + 1) * SPAN)
        ridged = gram + jnp.where(eye, RIDGE, 0.0)
        scale = 1.0 / jnp.sqrt(jnp.sum(ridged * ridged, keepdims=True))
        a_ref[0, b] = ridged
        pre_ref[0, b] = pair
        es[b] = ridged * scale
        xs[b] = jnp.where(eye, scale, 0.0)
        if b < blocks - 1:
            k = k_ref[rows, :]
            both = dot(k, cat([k, v_ref[rows, :]], 1), (0, 0))
            gram = gram + both[:, :HDIM]
            pair = pair + both[:, HDIM:]
    nil = jnp.zeros((HDIM, HDIM), BF16)

    def step(j, carry):
        for b in range(blocks):
            e, x = es[b], xs[b]
            eh, el = split(e)
            xh, xl = split(x)
            e_ref[0, j, b] = eh
            x_ref[0, j, b] = xh
            left = cat([cat([eh, el], 1), cat([xh, xl], 1)], 0)
            right = cat([cat([eh, el], 1), cat([eh, nil], 1)], 0)
            both = dot(left, right)
            both = both[:, :HDIM] + both[:, HDIM:]
            es[b] = 2.0 * e - both[:HDIM]
            xs[b] = 2.0 * x - both[HDIM:]
        return carry

    lax.fori_loop(0, NEWTON, step, 0)
    keep = causal()
    for b in range(blocks):
        rows = slice(b * SPAN, (b + 1) * SPAN)
        q, k, v = q_ref[rows, :], k_ref[rows, :], v_ref[rows, :]
        x = xs[b]
        last_ref[0, b] = x
        xh, xl = split(x)
        sh, sl = split(dot(cat([q, q], 1), cat([xh, xl], 0)))
        scores = dot(cat([sh, sl], 1), cat([k, k], 1), (1, 1))
        scores = jnp.where(keep, scores, 0.0).astype(BF16)
        nh, nl = split(pre_ref[0, b])
        out = dot(scores, v) + dot(cat([sh, sl], 1), cat([nh, nh], 0)) + dot(sh, nl)
        out_ref[rows, :] = out.astype(BF16)


def column(tok, index=0):
    return pl.BlockSpec((tok, HDIM), lambda h: (0, h))


def per_head(*dims):
    return pl.BlockSpec((1,) + dims, lambda h: (h,) + (0,) * len(dims))


def primal(queries, keys, values, gram, pair, heads, blocks):
    tok = queries.shape[0]
    stash = shape((heads, NEWTON, blocks, HDIM, HDIM), BF16)
    state = shape((heads, blocks, HDIM, HDIM))
    return pl.pallas_call(
        primal_kernel,
        grid=(heads,),
        out_shape=(shape(queries.shape, BF16), stash, stash, state, state, state),
        in_specs=[column(tok)] * 3 + [per_head(HDIM, HDIM)] * 2,
        out_specs=(column(tok),)
        + (per_head(NEWTON, blocks, HDIM, HDIM),) * 2
        + (per_head(blocks, HDIM, HDIM),) * 3,
        scratch_shapes=[pltpu.VMEM((blocks, HDIM, HDIM), F32)] * 2,
        compiler_params=params(),
        cost_estimate=cost(4_000_000_000, 8_000_000),
    )(queries, keys, values, gram, pair)


def tangent_kernel(
    q_ref, k_ref, v_ref, do_ref, e_ref, x_ref, last_ref, a_ref, pre_ref,
    dq_ref, dk_ref, dv_ref, da_ref, dn_ref, ga_ref, gn_ref, des, dxs, first,
):
    blocks = a_ref.shape[1]
    keep = causal()
    nil = jnp.zeros((HDIM, HDIM), BF16)
    for b in range(blocks):
        rows = slice(b * SPAN, (b + 1) * SPAN)
        q, k, v, do = q_ref[rows, :], k_ref[rows, :], v_ref[rows, :], do_ref[rows, :]
        weights = jnp.where(keep, dot(do, v, (1, 1)), 0.0).astype(BF16)
        nh, nl = split(pre_ref[0, b])
        ds = dot(weights, k) + dot(cat([do, do], 1), cat([nh, nl], 1), (1, 1))
        ds = ds.astype(BF16)
        xh, xl = split(last_ref[0, b])
        inverse = cat([xh, xl], 0)
        sh, sl = split(dot(cat([q, q], 1), inverse))
        scores = dot(cat([sh, sl], 1), cat([k, k], 1), (1, 1))
        scores = jnp.where(keep, scores, 0.0).astype(BF16)
        dv_ref[rows, :] = dot(scores, do, (0, 0))
        dk_ref[rows, :] = dot(weights, sh, (0, 0))
        dn_ref[0, b] = dot(sh, do, (0, 0)) + dot(sl, do, (0, 0))
        dq_ref[rows, :] = dot(cat([ds, ds], 1), inverse).astype(BF16)
        bar = dot(q, ds, (0, 0))
        bar = bar + bar.T
        ridged = a_ref[0, b]
        scale = 1.0 / jnp.sqrt(jnp.sum(ridged * ridged, keepdims=True))
        first[b] = bar
        des[b] = bar * scale
        dxs[b] = jnp.zeros((HDIM, HDIM), F32)

    def step(j, carry):
        for b in range(blocks):
            e, x = e_ref[0, j, b], x_ref[0, j, b]
            de, dx = des[b], dxs[b]
            left = cat([cat([dx.astype(BF16), x], 1), cat([nil, e], 1)], 0)
            both = dot(left, cat([e, de.astype(BF16)], 0))
            turned = both[HDIM:]
            dxs[b] = 2.0 * dx - both[:HDIM]
            des[b] = 2.0 * de - (turned + turned.T)
        return carry

    lax.fori_loop(0, NEWTON, step, 0)
    sum_a = jnp.zeros((HDIM, HDIM), F32)
    sum_n = jnp.zeros((HDIM, HDIM), F32)
    for b in range(blocks):
        ridged, dx = a_ref[0, b], dxs[b]
        square = jnp.sum(ridged * ridged, keepdims=True)
        along = jnp.sum(first[b] * last_ref[0, b] + dx * ridged, keepdims=True)
        da = dx - (along / square) * ridged
        da_ref[0, b] = da
        sum_a = sum_a + da
        sum_n = sum_n + dn_ref[0, b]
    ga_ref[0] = sum_a
    gn_ref[0] = sum_n


def tangent(queries, keys, values, grads, stash, heads, blocks):
    tok = queries.shape[0]
    state = shape((heads, blocks, HDIM, HDIM))
    total = shape((heads, HDIM, HDIM))
    wide = shape(queries.shape)
    return pl.pallas_call(
        tangent_kernel,
        grid=(heads,),
        out_shape=(shape(queries.shape, BF16), wide, wide, state, state, total, total),
        in_specs=[column(tok)] * 4
        + [per_head(NEWTON, blocks, HDIM, HDIM)] * 2
        + [per_head(blocks, HDIM, HDIM)] * 3,
        out_specs=(column(tok),) * 3
        + (per_head(blocks, HDIM, HDIM),) * 2
        + (per_head(HDIM, HDIM),) * 2,
        scratch_shapes=[pltpu.VMEM((blocks, HDIM, HDIM), F32)] * 3,
        compiler_params=params(),
        cost_estimate=cost(4_000_000_000, 8_000_000),
    )(queries, keys, values, grads, *stash)


def finish_kernel(k_ref, v_ref, dk_ref, dv_ref, da_ref, dn_ref, sa_ref, sn_ref, gk_ref, gv_ref):
    blocks = da_ref.shape[1]
    sa, sn = sa_ref[0], sn_ref[0]
    for b in reversed(range(blocks)):
        rows = slice(b * SPAN, (b + 1) * SPAN)
        k, v = k_ref[rows, :], v_ref[rows, :]
        nh, nl = split(sn)
        grad_k = dk_ref[rows, :] + dot(k, sa.astype(BF16)) + dot(cat([v, v], 1), cat([nh, nl], 1), (1, 1))
        grad_v = dv_ref[rows, :] + dot(cat([k, k], 1), cat([nh, nl], 0))
        gk_ref[rows, :] = grad_k.astype(BF16)
        gv_ref[rows, :] = grad_v.astype(BF16)
        if b:
            sa = sa + da_ref[0, b]
            sn = sn + dn_ref[0, b]


def finish(keys, values, dk, dv, da, dn, sa, sn, heads, blocks):
    tok = keys.shape[0]
    return pl.pallas_call(
        finish_kernel,
        grid=(heads,),
        out_shape=(shape(keys.shape, BF16),) * 2,
        in_specs=[column(tok)] * 4
        + [per_head(blocks, HDIM, HDIM)] * 2
        + [per_head(HDIM, HDIM)] * 2,
        out_specs=(column(tok),) * 2,
        compiler_params=params(),
        cost_estimate=cost(1_000_000_000, 6_000_000),
    )(keys, values, dk, dv, da, dn, sa, sn)


def grads_kernel(me_ref, w_ref, *refs):
    parts, out_ref = refs[:-1], refs[-1]
    me = me_ref[0]
    width = parts[0].shape[1]
    total = None
    for s, part in enumerate(parts):
        cols = pl.ds(pl.multiple_of((me ^ s) * width, width), width)
        term = dot(part[...], w_ref[:, cols], (1, 1))
        total = term if total is None else total + term
    out_ref[...] = total.astype(BF16)


def head_grads(me, w_out, parts):
    rows = parts[0].shape[0]
    return pl.pallas_call(
        grads_kernel,
        out_shape=shape((rows, w_out.shape[0]), BF16),
        in_specs=[SMEM_SPEC] + [VMEM_SPEC] * (1 + len(parts)),
        out_specs=VMEM_SPEC,
        compiler_params=params(),
        cost_estimate=cost(2 * rows * w_out.size, 6_000_000),
    )(me, w_out, *parts)


def weights_kernel(count, me_ref, h_ref, *refs):
    parts, out_ref = refs[:-1], refs[-1]
    me, mine = me_ref[0], me_ref[1]
    width = out_ref.shape[2]
    fold = parts[0].shape[1] // width
    for s, part in enumerate(parts):
        for f in range(fold):
            target = (me ^ s) * fold + f
            term = dot(h_ref[...], part[:, f * width : (f + 1) * width], (0, 0))
            out_ref[target ^ mine] = term.astype(BF16)


def weight_terms(me, heads_out, parts, count):
    feats = sum(part.shape[1] for part in parts)
    return pl.pallas_call(
        functools.partial(weights_kernel, count),
        out_shape=shape((count, heads_out.shape[1], feats // count), BF16),
        in_specs=[SMEM_SPEC] + [VMEM_SPEC] * (1 + len(parts)),
        out_specs=VMEM_SPEC,
        compiler_params=params(),
        cost_estimate=cost(2 * heads_out.size * feats, 6_000_000),
    )(me, heads_out, *parts)


def layer_kernel(*refs):
    count = (len(refs) - 1) // 2
    total = None
    for s in range(count):
        term = dot(refs[s][...], refs[count + s][...])
        total = term if total is None else total + term
    refs[-1][...] = total.astype(BF16)


def layer(parts, blocks):
    rows, cols = parts[0].shape[0], blocks[0].shape[1]
    return pl.pallas_call(
        layer_kernel,
        out_shape=shape((rows, cols), BF16),
        in_specs=[VMEM_SPEC] * (len(parts) + len(blocks)),
        out_specs=VMEM_SPEC,
        compiler_params=params(),
        cost_estimate=cost(2 * rows * cols * sum(p.shape[1] for p in parts), 6_000_000),
    )(*parts, *blocks)


def swap(value, axis, distance):
    count = lax.axis_size(axis)
    return lax.ppermute(value, axis, [(i, i ^ distance) for i in range(count)])


def gather_relative(value, axis):
    count = lax.axis_size(axis)
    near = {s: value if s == 0 else swap(value, axis, s) for s in range(0, count, 2)}
    out = []
    for s in range(0, count, 2):
        out += [near[s], swap(near[s], axis, 1)]
    return out


def before(value, axis, backward):
    count, mine = lax.axis_size(axis), lax.axis_index(axis)
    prefix = jax.tree.map(jnp.zeros_like, value)
    distance = 1
    while distance < count:
        other = jax.tree.map(lambda part: swap(part, axis, distance), value)
        upper = (mine & distance) != 0
        take = jnp.logical_not(upper) if backward else upper
        prefix = jax.tree.map(lambda p, o: p + jnp.where(take, o, 0.0), prefix, other)
        value = jax.tree.map(jnp.add, value, other)
        distance *= 2
    return prefix


def scatter_sum(terms, axis):
    count = lax.axis_size(axis)
    pairs = terms.reshape((count // 2, 2) + terms.shape[1:])
    other = swap(pairs[:, 1], axis, 1)
    half = pairs[:, 0].astype(F32) + other.astype(F32)
    total = half[0]
    for u in range(1, count // 2):
        total = total + swap(half[u].astype(BF16), axis, 2 * u).astype(F32)
    return total


def shards(queries, keys, values, w_out, cotangent):
    heads = queries.shape[1] // HDIM
    blocks = queries.shape[0] // SPAN
    head_count, ctx_count = lax.axis_size("head"), lax.axis_size("ctx")
    me_head, me_ctx = lax.axis_index("head"), lax.axis_index("ctx")
    me = jnp.stack([me_head, me_ctx]).astype(jnp.int32)

    grad_parts = gather_relative(cotangent, "head")
    gram, pair = totals(keys, values, heads)
    gram, pair = before((gram, pair), "ctx", False)
    heads_out, *stash = primal(queries, keys, values, gram, pair, heads, blocks)
    grads = head_grads(me, w_out, grad_parts)
    grad_queries, dk, dv, da, dn, sum_a, sum_n = tangent(
        queries, keys, values, grads, stash, heads, blocks
    )
    sum_a, sum_n = before((sum_a, sum_n), "ctx", True)
    grad_keys, grad_values = finish(keys, values, dk, dv, da, dn, sum_a, sum_n, heads, blocks)

    terms = weight_terms(me, heads_out, grad_parts, ctx_count)
    grad_weight = scatter_sum(terms, "ctx")

    width = w_out.shape[1] // head_count
    columns = []
    for s in range(head_count):
        mine = lax.dynamic_slice_in_dim(w_out, (me_head ^ s) * width, width, axis=1)
        columns.append(swap(mine, "head", s) if s else mine)
    layer_out = layer(gather_relative(heads_out, "head"), columns)
    return (layer_out, grad_queries, grad_keys, grad_values, grad_weight)


def solution(mesh):
    in_specs = (
        P("ctx", "head"),
        P("ctx", "head"),
        P("ctx", "head"),
        P("head", None),
        P("ctx", "head"),
    )
    out_specs = (
        P("ctx", "head"),
        P("ctx", "head"),
        P("ctx", "head"),
        P("ctx", "head"),
        P("head", "ctx"),
    )
    return jax.shard_map(shards, mesh=mesh, in_specs=in_specs, out_specs=out_specs, check_vma=False)
```

```python
import functools

import jax
import jax.numpy as jnp
from jax import lax
from jax.experimental import pallas as pl
from jax.experimental.pallas import tpu as pltpu
from jax.sharding import PartitionSpec as P

HDIM = 128
SPAN = 256
NEWTON = 8
RIDGE = 1.0
F32 = jnp.float32
BF16 = jnp.bfloat16
VMEM_SPEC = pl.BlockSpec(memory_space=pltpu.VMEM)
SMEM_SPEC = pl.BlockSpec(memory_space=pltpu.SMEM)


def dot(left, right, axes=(1, 0)):
    return lax.dot_general(
        left, right, (((axes[0],), (axes[1],)), ((), ())), preferred_element_type=F32
    )


def split(value):
    high = value.astype(BF16)
    return high, (value - high.astype(F32)).astype(BF16)


def cat(parts, axis):
    return jnp.concatenate(parts, axis=axis)


def params(limit=16):
    return pltpu.CompilerParams(vmem_limit_bytes=limit * 1024 * 1024)


def cost(flops, size):
    return pl.CostEstimate(flops=flops, bytes_accessed=size, transcendentals=0)


def shape(dims, dtype=F32):
    return jax.ShapeDtypeStruct(dims, dtype)


def unit():
    rows = lax.broadcasted_iota(jnp.int32, (HDIM, HDIM), 0)
    cols = lax.broadcasted_iota(jnp.int32, (HDIM, HDIM), 1)
    return rows == cols


def causal():
    rows = lax.broadcasted_iota(jnp.int32, (SPAN, SPAN), 0)
    cols = lax.broadcasted_iota(jnp.int32, (SPAN, SPAN), 1)
    return rows >= cols


def corner():
    rows = lax.broadcasted_iota(jnp.int32, (HDIM, HDIM), 0)
    cols = lax.broadcasted_iota(jnp.int32, (HDIM, HDIM), 1)
    return rows, cols


def fold(one, two):
    rows, cols = corner()
    both = jnp.where(rows <= cols, one, two)
    line = jnp.sum(jnp.where(rows == cols, two, 0.0), axis=0, keepdims=True)
    return both, jnp.broadcast_to(line, (8, HDIM))


def unfold(both, line):
    rows, cols = corner()
    turned = both.T
    one = jnp.where(rows <= cols, both, turned)
    two = jnp.where(rows > cols, both, turned)
    two = jnp.where(rows == cols, line[:1], two)
    return one, two


def folded(heads):
    return (heads + 1) // 2


def fold_into(ref, mats, base=0):
    for i in range(folded(len(mats))):
        one, two = mats[2 * i], mats[min(2 * i + 1, len(mats) - 1)]
        both, line = fold(one, two)
        top = base + i * (HDIM + 8)
        ref[top : top + HDIM, :] = both
        ref[top + HDIM : top + HDIM + 8, :] = line


def unfold_from(ref, heads, base=0):
    mats = []
    for i in range(folded(heads)):
        top = base + i * (HDIM + 8)
        mats += unfold(ref[top : top + HDIM, :], ref[top + HDIM : top + HDIM + 8, :])
    return mats[:heads]


def totals_kernel(k_ref, v_ref, g_ref, n_ref):
    grams = []
    for h in range(k_ref.shape[1] // HDIM):
        cols = slice(h * HDIM, (h + 1) * HDIM)
        k = k_ref[:, cols]
        both = dot(k, cat([k, v_ref[:, cols]], 1), (0, 0))
        grams.append(both[:, :HDIM])
        n_ref[cols, :] = both[:, HDIM:]
    fold_into(g_ref, grams)


def totals(keys, values, heads):
    return pl.pallas_call(
        totals_kernel,
        out_shape=(shape((folded(heads) * (HDIM + 8), HDIM)), shape((heads * HDIM, HDIM))),
        in_specs=[VMEM_SPEC] * 2,
        out_specs=(VMEM_SPEC, VMEM_SPEC),
        compiler_params=params(),
        cost_estimate=cost(2 * 2 * keys.size * HDIM, 4 * keys.size),
    )(keys, values)


def places(q_ref, heads):
    blocks = q_ref.shape[0] // SPAN
    for h in range(heads):
        for b in range(blocks):
            yield h, b, h * blocks + b, slice(b * SPAN, (b + 1) * SPAN), slice(h * HDIM, (h + 1) * HDIM)


def primal_kernel(
    q_ref, k_ref, v_ref, g_ref, n_ref, out_ref, e_ref, x_ref, last_ref, a_ref, pre_ref, es, xs
):
    heads = q_ref.shape[1] // HDIM
    eye = unit()
    grams = unfold_from(g_ref, heads)
    pairs = [n_ref[h * HDIM : (h + 1) * HDIM, :] for h in range(heads)]
    for h, b, i, rows, cols in places(q_ref, heads):
        ridged = grams[h] + jnp.where(eye, RIDGE, 0.0)
        scale = 1.0 / jnp.sqrt(jnp.sum(ridged * ridged, keepdims=True))
        a_ref[i] = ridged
        pre_ref[i] = pairs[h]
        es[i] = ridged * scale
        xs[i] = jnp.where(eye, scale, 0.0)
        k = k_ref[rows, cols]
        both = dot(k, cat([k, v_ref[rows, cols]], 1), (0, 0))
        grams[h] = grams[h] + both[:, :HDIM]
        pairs[h] = pairs[h] + both[:, HDIM:]
    nil = jnp.zeros((HDIM, HDIM), BF16)

    def step(j, carry):
        for i in range(es.shape[0]):
            e, x = es[i], xs[i]
            eh, el = split(e)
            xh, xl = split(x)
            e_ref[j, i] = eh
            x_ref[j, i] = xh
            left = cat([cat([eh, el], 1), cat([xh, xl], 1)], 0)
            right = cat([cat([eh, el], 1), cat([eh, nil], 1)], 0)
            both = dot(left, right)
            both = both[:, :HDIM] + both[:, HDIM:]
            es[i] = 2.0 * e - both[:HDIM]
            xs[i] = 2.0 * x - both[HDIM:]
        return carry

    lax.fori_loop(0, NEWTON, step, 0)
    keep = causal()
    for h, b, i, rows, cols in places(q_ref, heads):
        q, k, v = q_ref[rows, cols], k_ref[rows, cols], v_ref[rows, cols]
        x = xs[i]
        last_ref[i] = x
        xh, xl = split(x)
        sh, sl = split(dot(cat([q, q], 1), cat([xh, xl], 0)))
        both = cat([sh, sl], 1)
        scores = dot(both, cat([k, k], 1), (1, 1))
        scores = jnp.where(keep, scores, 0.0).astype(BF16)
        nh, nl = split(pre_ref[i])
        state = dot(both, cat([cat([nh, nl], 1), cat([nh, nil], 1)], 0))
        out = dot(scores, v) + state[:, :HDIM] + state[:, HDIM:]
        out_ref[rows, cols] = out.astype(BF16)


def primal(queries, keys, values, gram, pair, heads, blocks):
    count = heads * blocks
    stash = shape((NEWTON, count, HDIM, HDIM), BF16)
    state = shape((count, HDIM, HDIM))
    return pl.pallas_call(
        primal_kernel,
        out_shape=(shape(queries.shape, BF16), stash, stash, state, state, state),
        in_specs=[VMEM_SPEC] * 5,
        out_specs=(VMEM_SPEC,) * 6,
        scratch_shapes=[pltpu.VMEM((count, HDIM, HDIM), F32)] * 2,
        compiler_params=params(24),
        cost_estimate=cost(4_000_000_000, 8_000_000),
    )(queries, keys, values, gram, pair)


def tangent_kernel(
    q_ref, k_ref, v_ref, do_ref, e_ref, x_ref, last_ref, a_ref, pre_ref,
    dq_ref, dk_ref, dv_ref, da_ref, dn_ref, sum_ref, des, dxs, first,
):
    heads = q_ref.shape[1] // HDIM
    keep = causal()
    nil = jnp.zeros((HDIM, HDIM), BF16)
    for h, b, i, rows, cols in places(q_ref, heads):
        q, k, v, do = q_ref[rows, cols], k_ref[rows, cols], v_ref[rows, cols], do_ref[rows, cols]
        weights = jnp.where(keep, dot(do, v, (1, 1)), 0.0).astype(BF16)
        nh, nl = split(pre_ref[i])
        ds = dot(weights, k) + dot(cat([do, do], 1), cat([nh, nl], 1), (1, 1))
        ds = ds.astype(BF16)
        xh, xl = split(last_ref[i])
        inverse = cat([xh, xl], 0)
        sh, sl = split(dot(cat([q, q], 1), inverse))
        both = cat([sh, sl], 1)
        scores = dot(both, cat([k, k], 1), (1, 1))
        scores = jnp.where(keep, scores, 0.0).astype(BF16)
        dv_ref[rows, cols] = dot(scores, do, (0, 0))
        dk_ref[rows, cols] = dot(weights, sh, (0, 0))
        state = dot(both, do, (0, 0))
        dn_ref[i] = state[:HDIM] + state[HDIM:]
        dq_ref[rows, cols] = dot(cat([ds, ds], 1), inverse).astype(BF16)
        bar = dot(q, ds, (0, 0))
        bar = bar + bar.T
        ridged = a_ref[i]
        scale = 1.0 / jnp.sqrt(jnp.sum(ridged * ridged, keepdims=True))
        first[i] = bar
        des[i] = bar * scale
        dxs[i] = jnp.zeros((HDIM, HDIM), F32)

    def step(j, carry):
        for i in range(des.shape[0]):
            e, x = e_ref[j, i], x_ref[j, i]
            de, dx = des[i], dxs[i]
            left = cat([cat([dx.astype(BF16), x], 1), cat([nil, e], 1)], 0)
            both = dot(left, cat([e, de.astype(BF16)], 0))
            turned = both[HDIM:]
            dxs[i] = 2.0 * dx - both[:HDIM]
            des[i] = 2.0 * de - (turned + turned.T)
        return carry

    lax.fori_loop(0, NEWTON, step, 0)
    sum_a = [jnp.zeros((HDIM, HDIM), F32) for _ in range(heads)]
    sum_n = [jnp.zeros((HDIM, HDIM), F32) for _ in range(heads)]
    for h, b, i, rows, cols in places(q_ref, heads):
        ridged, dx = a_ref[i], dxs[i]
        square = jnp.sum(ridged * ridged, keepdims=True)
        along = jnp.sum(first[i] * last_ref[i] + dx * ridged, keepdims=True)
        da = dx - (along / square) * ridged
        da_ref[i] = da
        sum_a[h] = sum_a[h] + da
        sum_n[h] = sum_n[h] + dn_ref[i]
    for h in range(heads):
        sum_ref[h * HDIM : (h + 1) * HDIM, :] = sum_n[h]
    fold_into(sum_ref, sum_a, heads * HDIM)


def tangent(queries, keys, values, grads, stash, heads, blocks):
    count = heads * blocks
    state = shape((count, HDIM, HDIM))
    wide = shape(queries.shape)
    rows = heads * HDIM + folded(heads) * (HDIM + 8)
    return pl.pallas_call(
        tangent_kernel,
        out_shape=(shape(queries.shape, BF16), wide, wide, state, state, shape((rows, HDIM))),
        in_specs=[VMEM_SPEC] * 9,
        out_specs=(VMEM_SPEC,) * 6,
        scratch_shapes=[pltpu.VMEM((count, HDIM, HDIM), F32)] * 3,
        compiler_params=params(24),
        cost_estimate=cost(4_000_000_000, 8_000_000),
    )(queries, keys, values, grads, *stash)


def finish_kernel(k_ref, v_ref, dk_ref, dv_ref, da_ref, dn_ref, sum_ref, gk_ref, gv_ref):
    heads = k_ref.shape[1] // HDIM
    sa = unfold_from(sum_ref, heads, heads * HDIM)
    sn = [sum_ref[h * HDIM : (h + 1) * HDIM, :] for h in range(heads)]
    for h, b, i, rows, cols in reversed(list(places(k_ref, heads))):
        k, v = k_ref[rows, cols], v_ref[rows, cols]
        nh, nl = split(sn[h])
        grad_k = dk_ref[rows, cols] + dot(k, sa[h].astype(BF16))
        grad_k = grad_k + dot(cat([v, v], 1), cat([nh, nl], 1), (1, 1))
        grad_v = dv_ref[rows, cols] + dot(cat([k, k], 1), cat([nh, nl], 0))
        gk_ref[rows, cols] = grad_k.astype(BF16)
        gv_ref[rows, cols] = grad_v.astype(BF16)
        sa[h] = sa[h] + da_ref[i]
        sn[h] = sn[h] + dn_ref[i]


def finish(keys, values, dk, dv, da, dn, sums):
    return pl.pallas_call(
        finish_kernel,
        out_shape=(shape(keys.shape, BF16),) * 2,
        in_specs=[VMEM_SPEC] * 7,
        out_specs=(VMEM_SPEC,) * 2,
        compiler_params=params(),
        cost_estimate=cost(1_000_000_000, 6_000_000),
    )(keys, values, dk, dv, da, dn, sums)


def grads_kernel(first, me_ref, w_ref, *refs):
    out_ref = refs[-1]
    me = me_ref[0]
    rest = refs[:-1]
    total = None
    if first:
        total, rest = rest[0][...], rest[1:]
    for s, part in enumerate(rest):
        width = part.shape[1]
        cols = pl.ds(pl.multiple_of((me ^ (first + s)) * width, width), width)
        term = dot(part[...], w_ref[:, cols], (1, 1))
        total = term if total is None else total + term
    out_ref[...] = total.astype(out_ref.dtype)


def head_grads(me, w_out, parts, first, begun=None):
    rows = parts[0].shape[0]
    begun = [] if begun is None else [begun]
    return pl.pallas_call(
        functools.partial(grads_kernel, first),
        out_shape=shape((rows, w_out.shape[0]), BF16 if begun else F32),
        in_specs=[SMEM_SPEC] + [VMEM_SPEC] * (1 + len(parts) + len(begun)),
        out_specs=VMEM_SPEC,
        compiler_params=params(),
        cost_estimate=cost(rows * w_out.size, 4_000_000),
    )(me, w_out, *begun, *parts)


def weights_kernel(count, me_ref, h_ref, *refs):
    parts, out_ref = refs[:-1], refs[-1]
    me, mine = me_ref[0], me_ref[1]
    width = out_ref.shape[2]
    fold = parts[0].shape[1] // width
    for s, part in enumerate(parts):
        for f in range(fold):
            target = (me ^ s) * fold + f
            term = dot(h_ref[...], part[:, f * width : (f + 1) * width], (0, 0))
            out_ref[target ^ mine] = term.astype(BF16)


def weight_terms(me, heads_out, parts, count):
    feats = sum(part.shape[1] for part in parts)
    return pl.pallas_call(
        functools.partial(weights_kernel, count),
        out_shape=shape((count, heads_out.shape[1], feats // count), BF16),
        in_specs=[SMEM_SPEC] + [VMEM_SPEC] * (1 + len(parts)),
        out_specs=VMEM_SPEC,
        compiler_params=params(),
        cost_estimate=cost(2 * heads_out.size * feats, 6_000_000),
    )(me, heads_out, *parts)


def layer_kernel(*refs):
    count = (len(refs) - 1) // 2
    total = None
    for s in range(count):
        term = dot(refs[s][...], refs[count + s][...])
        total = term if total is None else total + term
    refs[-1][...] = total.astype(BF16)


def layer(parts, blocks):
    rows, cols = parts[0].shape[0], blocks[0].shape[1]
    return pl.pallas_call(
        layer_kernel,
        out_shape=shape((rows, cols), BF16),
        in_specs=[VMEM_SPEC] * (len(parts) + len(blocks)),
        out_specs=VMEM_SPEC,
        compiler_params=params(),
        cost_estimate=cost(2 * rows * cols * sum(p.shape[1] for p in parts), 6_000_000),
    )(*parts, *blocks)


def swap(value, axis, distance):
    count = lax.axis_size(axis)
    return lax.ppermute(value, axis, [(i, i ^ distance) for i in range(count)])


def after(value, *others):
    return lax.optimization_barrier((value,) + others)[0]


def before(value, axis, backward, kind):
    count, mine = lax.axis_size(axis), lax.axis_index(axis)
    prefix = jnp.zeros_like(value)
    distance = 1
    while distance < count:
        other = swap(value.astype(kind), axis, distance).astype(F32)
        upper = (mine & distance) != 0
        take = jnp.logical_not(upper) if backward else upper
        prefix = prefix + jnp.where(take, other, 0.0)
        value = value + other
        distance *= 2
    return prefix


def shards(queries, keys, values, w_out, cotangent):
    heads = queries.shape[1] // HDIM
    blocks = queries.shape[0] // SPAN
    head_count, ctx_count = lax.axis_size("head"), lax.axis_size("ctx")
    me_head, me_ctx = lax.axis_index("head"), lax.axis_index("ctx")
    me = jnp.stack([me_head, me_ctx]).astype(jnp.int32)
    evens = range(2, head_count, 2)

    far = [swap(cotangent, "head", s) for s in evens]
    near = swap(cotangent, "head", 1)
    gram, pair = totals(keys, values, heads)
    gram = before(gram, "ctx", False, F32)
    pair = before(pair, "ctx", False, F32)
    begun = head_grads(me, w_out, [cotangent, near], 0)
    gram = after(gram, begun)
    heads_out, *stash = primal(queries, keys, values, gram, pair, heads, blocks)
    grad_parts = [cotangent, near]
    for part in far:
        grad_parts += [part, swap(part, "head", 1)]
    begun = after(begun, heads_out)
    grads = head_grads(me, w_out, grad_parts[2:], 2, begun)

    outs_far = [swap(after(heads_out, grads), "head", s) for s in evens]
    outs_near = swap(after(heads_out, grads), "head", 1)
    terms = weight_terms(me, after(heads_out, grads), grad_parts, ctx_count)
    pairs = terms.reshape((ctx_count // 2, 2) + terms.shape[1:])
    other = swap(pairs[:, 1], "ctx", 1)

    width = w_out.shape[1] // head_count
    late = after(w_out, terms)
    columns = []
    for s in range(head_count):
        mine = lax.dynamic_slice_in_dim(late, (me_head ^ s) * width, width, axis=1)
        columns.append(swap(mine, "head", s) if s else mine)

    grad_queries, dk, dv, da, dn, sums = tangent(
        queries, keys, values, after(grads, terms), stash, heads, blocks
    )
    sums = before(sums, "ctx", True, BF16)

    half = pairs[:, 0].astype(F32) + after(other, grad_queries).astype(F32)
    grad_weight = half[0]
    for u in range(1, ctx_count // 2):
        grad_weight = grad_weight + swap(half[u].astype(BF16), "ctx", 2 * u).astype(F32)

    outs = [heads_out, outs_near]
    for part in outs_far:
        outs += [part, swap(after(part, grad_queries), "head", 1)]
    layer_out = layer(outs, columns)
    grad_keys, grad_values = finish(keys, values, dk, dv, da, dn, sums)
    return (layer_out, grad_queries, grad_keys, grad_values, grad_weight)


def solution(mesh):
    in_specs = (
        P("ctx", "head"),
        P("ctx", "head"),
        P("ctx", "head"),
        P("head", None),
        P("ctx", "head"),
    )
    out_specs = (
        P("ctx", "head"),
        P("ctx", "head"),
        P("ctx", "head"),
        P("ctx", "head"),
        P("head", "ctx"),
    )
    return jax.shard_map(shards, mesh=mesh, in_specs=in_specs, out_specs=out_specs, check_vma=False)
```

```python
import functools

import jax
import jax.numpy as jnp
from jax import lax
from jax.experimental import pallas as pl
from jax.experimental.pallas import tpu as pltpu
from jax.sharding import PartitionSpec as P


HDIM = 128
SPAN = 256
NEWTON = 8
RIDGE = 1.0
F32 = jnp.float32
BF16 = jnp.bfloat16
VMEM_SPEC = pl.BlockSpec(memory_space=pltpu.VMEM)
SMEM_SPEC = pl.BlockSpec(memory_space=pltpu.SMEM)


def dot(left, right, axes=(1, 0)):
    return lax.dot_general(
        left, right, (((axes[0],), (axes[1],)), ((), ())), preferred_element_type=F32
    )


def split(value):
    high = value.astype(BF16)
    return high, (value - high.astype(F32)).astype(BF16)


def cat(parts, axis):
    return jnp.concatenate(parts, axis=axis)


def params(limit=16):
    return pltpu.CompilerParams(vmem_limit_bytes=limit * 1024 * 1024)


def cost(flops, size):
    return pl.CostEstimate(flops=flops, bytes_accessed=size, transcendentals=0)


def shape(dims, dtype=F32):
    return jax.ShapeDtypeStruct(dims, dtype)


def unit():
    rows = lax.broadcasted_iota(jnp.int32, (HDIM, HDIM), 0)
    cols = lax.broadcasted_iota(jnp.int32, (HDIM, HDIM), 1)
    return rows == cols


def causal():
    rows = lax.broadcasted_iota(jnp.int32, (SPAN, SPAN), 0)
    cols = lax.broadcasted_iota(jnp.int32, (SPAN, SPAN), 1)
    return rows >= cols


def corner():
    rows = lax.broadcasted_iota(jnp.int32, (HDIM, HDIM), 0)
    cols = lax.broadcasted_iota(jnp.int32, (HDIM, HDIM), 1)
    return rows, cols


def fold(one, two):
    rows, cols = corner()
    both = jnp.where(rows <= cols, one, two)
    line = jnp.sum(jnp.where(rows == cols, two, 0.0), axis=0, keepdims=True)
    return both, jnp.broadcast_to(line, (8, HDIM))


def unfold(both, line):
    rows, cols = corner()
    turned = both.T
    one = jnp.where(rows <= cols, both, turned)
    two = jnp.where(rows > cols, both, turned)
    two = jnp.where(rows == cols, line[:1], two)
    return one, two


def folded(heads):
    return (heads + 1) // 2


def fold_into(ref, mats, base=0):
    for i in range(folded(len(mats))):
        one, two = mats[2 * i], mats[min(2 * i + 1, len(mats) - 1)]
        both, line = fold(one, two)
        top = base + i * (HDIM + 8)
        ref[top : top + HDIM, :] = both
        ref[top + HDIM : top + HDIM + 8, :] = line


def unfold_from(ref, heads, base=0):
    mats = []
    for i in range(folded(heads)):
        top = base + i * (HDIM + 8)
        mats += unfold(ref[top : top + HDIM, :], ref[top + HDIM : top + HDIM + 8, :])
    return mats[:heads]


def totals_kernel(k_ref, v_ref, g_ref, n_ref):
    grams = []
    for h in range(k_ref.shape[1] // HDIM):
        cols = slice(h * HDIM, (h + 1) * HDIM)
        k = k_ref[:, cols]
        both = dot(k, cat([k, v_ref[:, cols]], 1), (0, 0))
        grams.append(both[:, :HDIM])
        n_ref[cols, :] = both[:, HDIM:]
    fold_into(g_ref, grams)


def totals(keys, values, heads):
    return pl.pallas_call(
        totals_kernel,
        out_shape=(shape((folded(heads) * (HDIM + 8), HDIM)), shape((heads * HDIM, HDIM))),
        in_specs=[VMEM_SPEC] * 2,
        out_specs=(VMEM_SPEC, VMEM_SPEC),
        compiler_params=params(),
        cost_estimate=cost(2 * 2 * keys.size * HDIM, 4 * keys.size),
    )(keys, values)


def places(q_ref, heads):
    blocks = q_ref.shape[0] // SPAN
    for h in range(heads):
        for b in range(blocks):
            yield h, b, h * blocks + b, slice(b * SPAN, (b + 1) * SPAN), slice(h * HDIM, (h + 1) * HDIM)


def inverse_kernel(k_ref, g_ref, e_ref, x_ref, last_ref, a_ref, es, xs):
    heads = k_ref.shape[1] // HDIM
    eye = unit()
    grams = unfold_from(g_ref, heads)
    for h, b, i, rows, cols in places(k_ref, heads):
        ridged = grams[h] + jnp.where(eye, RIDGE, 0.0)
        scale = 1.0 / jnp.sqrt(jnp.sum(ridged * ridged, keepdims=True))
        a_ref[i] = ridged
        es[i] = ridged * scale
        xs[i] = jnp.where(eye, scale, 0.0)
        k = k_ref[rows, cols]
        grams[h] = grams[h] + dot(k, k, (0, 0))
    nil = jnp.zeros((HDIM, HDIM), BF16)

    def step(j, carry):
        for i in range(es.shape[0]):
            e, x = es[i], xs[i]
            eh, el = split(e)
            xh, xl = split(x)
            e_ref[j, i] = eh
            x_ref[j, i] = xh
            left = cat([cat([eh, el], 1), cat([xh, xl], 1)], 0)
            right = cat([cat([eh, el], 1), cat([eh, nil], 1)], 0)
            both = dot(left, right)
            both = both[:, :HDIM] + both[:, HDIM:]
            es[i] = 2.0 * e - both[:HDIM]
            xs[i] = 2.0 * x - both[HDIM:]
        return carry

    lax.fori_loop(0, NEWTON, step, 0)
    for i in range(xs.shape[0]):
        last_ref[i] = xs[i]


def inverses(keys, gram, count):
    stash = shape((NEWTON, count, HDIM, HDIM), BF16)
    state = shape((count, HDIM, HDIM))
    return pl.pallas_call(
        inverse_kernel,
        out_shape=(stash, stash, state, state),
        in_specs=[VMEM_SPEC] * 2,
        out_specs=(VMEM_SPEC,) * 4,
        scratch_shapes=[pltpu.VMEM((count, HDIM, HDIM), F32)] * 2,
        compiler_params=params(),
        cost_estimate=cost(2_000_000_000, 8_000_000),
    )(keys, gram)


def outputs_kernel(q_ref, k_ref, v_ref, n_ref, last_ref, out_ref, pre_ref, s_ref, w_ref):
    heads = q_ref.shape[1] // HDIM
    keep = causal()
    nil = jnp.zeros((HDIM, HDIM), BF16)
    pairs = [n_ref[h * HDIM : (h + 1) * HDIM, :] for h in range(heads)]
    for h, b, i, rows, cols in places(q_ref, heads):
        q, k, v = q_ref[rows, cols], k_ref[rows, cols], v_ref[rows, cols]
        xh, xl = split(last_ref[i])
        sh, sl = split(dot(cat([q, q], 1), cat([xh, xl], 0)))
        both = cat([sh, sl], 1)
        s_ref[i] = both
        scores = dot(both, cat([k, k], 1), (1, 1))
        scores = jnp.where(keep, scores, 0.0).astype(BF16)
        w_ref[i] = scores
        nh, nl = split(pairs[h])
        pre_ref[i] = cat([nh, nl], 1)
        state = dot(both, cat([cat([nh, nl], 1), cat([nh, nil], 1)], 0))
        out = dot(scores, v) + state[:, :HDIM] + state[:, HDIM:]
        out_ref[rows, cols] = out.astype(BF16)
        pairs[h] = pairs[h] + dot(k, v, (0, 0))


def outputs(queries, keys, values, pair, last):
    count = last.shape[0]
    return pl.pallas_call(
        outputs_kernel,
        out_shape=(
            shape(queries.shape, BF16),
            shape((count, HDIM, 2 * HDIM), BF16),
            shape((count, SPAN, 2 * HDIM), BF16),
            shape((count, SPAN, SPAN), BF16),
        ),
        in_specs=[VMEM_SPEC] * 5,
        out_specs=(VMEM_SPEC,) * 4,
        compiler_params=params(),
        cost_estimate=cost(2_000_000_000, 8_000_000),
    )(queries, keys, values, pair, last)


def tangent_kernel(
    q_ref, k_ref, v_ref, do_ref, e_ref, x_ref, last_ref, a_ref, pre_ref, s_ref, w_ref,
    dq_ref, dk_ref, dv_ref, da_ref, dn_ref, sum_ref, des, dxs, first,
):
    heads = q_ref.shape[1] // HDIM
    keep = causal()
    nil = jnp.zeros((HDIM, HDIM), BF16)
    for h, b, i, rows, cols in places(q_ref, heads):
        q, k, v, do = q_ref[rows, cols], k_ref[rows, cols], v_ref[rows, cols], do_ref[rows, cols]
        weights = jnp.where(keep, dot(do, v, (1, 1)), 0.0).astype(BF16)
        ds = dot(weights, k) + dot(cat([do, do], 1), pre_ref[i], (1, 1))
        ds = ds.astype(BF16)
        xh, xl = split(last_ref[i])
        inverse = cat([xh, xl], 0)
        both = s_ref[i]
        sh = both[:, :HDIM]
        scores = w_ref[i]
        dv_ref[rows, cols] = dot(scores, do, (0, 0))
        dk_ref[rows, cols] = dot(weights, sh, (0, 0))
        state = dot(both, do, (0, 0))
        dn_ref[i] = state[:HDIM] + state[HDIM:]
        dq_ref[rows, cols] = dot(cat([ds, ds], 1), inverse).astype(BF16)
        bar = dot(q, ds, (0, 0))
        bar = bar + bar.T
        ridged = a_ref[i]
        scale = 1.0 / jnp.sqrt(jnp.sum(ridged * ridged, keepdims=True))
        first[i] = bar
        des[i] = bar * scale
        dxs[i] = jnp.zeros((HDIM, HDIM), F32)

    def step(j, carry):
        for i in range(des.shape[0]):
            e, x = e_ref[j, i], x_ref[j, i]
            de, dx = des[i], dxs[i]
            left = cat([cat([dx.astype(BF16), x], 1), cat([nil, e], 1)], 0)
            both = dot(left, cat([e, de.astype(BF16)], 0))
            turned = both[HDIM:]
            dxs[i] = 2.0 * dx - both[:HDIM]
            des[i] = 2.0 * de - (turned + turned.T)
        return carry

    lax.fori_loop(0, NEWTON, step, 0)
    sum_a = [jnp.zeros((HDIM, HDIM), F32) for _ in range(heads)]
    sum_n = [jnp.zeros((HDIM, HDIM), F32) for _ in range(heads)]
    for h, b, i, rows, cols in places(q_ref, heads):
        ridged, dx = a_ref[i], dxs[i]
        square = jnp.sum(ridged * ridged, keepdims=True)
        along = jnp.sum(first[i] * last_ref[i] + dx * ridged, keepdims=True)
        da = dx - (along / square) * ridged
        da_ref[i] = da
        sum_a[h] = sum_a[h] + da
        sum_n[h] = sum_n[h] + dn_ref[i]
    for h in range(heads):
        sum_ref[h * HDIM : (h + 1) * HDIM, :] = sum_n[h]
    fold_into(sum_ref, sum_a, heads * HDIM)


def tangent(queries, keys, values, grads, stash):
    heads = queries.shape[1] // HDIM
    count = stash[-1].shape[0]
    state = shape((count, HDIM, HDIM))
    wide = shape(queries.shape)
    rows = heads * HDIM + folded(heads) * (HDIM + 8)
    return pl.pallas_call(
        tangent_kernel,
        out_shape=(shape(queries.shape, BF16), wide, wide, state, state, shape((rows, HDIM))),
        in_specs=[VMEM_SPEC] * 11,
        out_specs=(VMEM_SPEC,) * 6,
        scratch_shapes=[pltpu.VMEM((count, HDIM, HDIM), F32)] * 3,
        compiler_params=params(24),
        cost_estimate=cost(4_000_000_000, 8_000_000),
    )(queries, keys, values, grads, *stash)


def finish_kernel(k_ref, v_ref, dk_ref, dv_ref, da_ref, dn_ref, sum_ref, gk_ref, gv_ref):
    heads = k_ref.shape[1] // HDIM
    sa = unfold_from(sum_ref, heads, heads * HDIM)
    sn = [sum_ref[h * HDIM : (h + 1) * HDIM, :] for h in range(heads)]
    for h, b, i, rows, cols in reversed(list(places(k_ref, heads))):
        k, v = k_ref[rows, cols], v_ref[rows, cols]
        nh, nl = split(sn[h])
        grad_k = dk_ref[rows, cols] + dot(k, sa[h].astype(BF16))
        grad_k = grad_k + dot(cat([v, v], 1), cat([nh, nl], 1), (1, 1))
        grad_v = dv_ref[rows, cols] + dot(cat([k, k], 1), cat([nh, nl], 0))
        gk_ref[rows, cols] = grad_k.astype(BF16)
        gv_ref[rows, cols] = grad_v.astype(BF16)
        sa[h] = sa[h] + da_ref[i]
        sn[h] = sn[h] + dn_ref[i]


def finish(keys, values, dk, dv, da, dn, sums):
    return pl.pallas_call(
        finish_kernel,
        out_shape=(shape(keys.shape, BF16),) * 2,
        in_specs=[VMEM_SPEC] * 7,
        out_specs=(VMEM_SPEC,) * 2,
        compiler_params=params(),
        cost_estimate=cost(1_000_000_000, 6_000_000),
    )(keys, values, dk, dv, da, dn, sums)


def spans(pieces):
    out, top = [], 0
    for piece in pieces:
        out.append(slice(top, top + piece.shape[0]))
        top += piece.shape[0]
    return out


def groups(refs, cuts):
    out, at = [], 0
    for cut in cuts:
        out.append(refs[at : at + cut])
        at += cut
    return out


def grads_kernel(first, cuts, me_ref, w_ref, *refs):
    out_ref = refs[-1]
    me = me_ref[0]
    parts = groups(refs[1:-1] if first else refs[:-1], cuts)
    for c, rows in enumerate(spans(parts[0])):
        total = refs[0][rows, :] if first else None
        for s, part in enumerate(parts):
            width = part[c].shape[1]
            cols = pl.ds(pl.multiple_of((me ^ (first + s)) * width, width), width)
            term = dot(part[c][...], w_ref[:, cols], (1, 1))
            total = term if total is None else total + term
        out_ref[rows, :] = total.astype(out_ref.dtype)


def head_grads(me, w_out, parts, first, begun=None):
    flat = [piece for part in parts for piece in part]
    rows = sum(piece.shape[0] for piece in parts[0])
    begun = [] if begun is None else [begun]
    return pl.pallas_call(
        functools.partial(grads_kernel, first, [len(part) for part in parts]),
        out_shape=shape((rows, w_out.shape[0]), BF16 if begun else F32),
        in_specs=[SMEM_SPEC] + [VMEM_SPEC] * (1 + len(flat) + len(begun)),
        out_specs=VMEM_SPEC,
        compiler_params=params(),
        cost_estimate=cost(rows * w_out.size, 4_000_000),
    )(me, w_out, *begun, *flat)


def weights_kernel(cuts, me_ref, h_ref, *refs):
    parts, out_ref = groups(refs[:-1], cuts), refs[-1]
    me, mine = me_ref[0], me_ref[1]
    width = out_ref.shape[2]
    fold = parts[0][0].shape[1] // width
    for s, part in enumerate(parts):
        for f in range(fold):
            target = (me ^ s) * fold + f
            cols = slice(f * width, (f + 1) * width)
            total = None
            for piece, rows in zip(part, spans(part)):
                term = dot(h_ref[rows, :], piece[:, cols], (0, 0))
                total = term if total is None else total + term
            out_ref[target ^ mine] = total.astype(BF16)


def weight_terms(me, heads_out, parts, count):
    flat = [piece for part in parts for piece in part]
    feats = sum(part[0].shape[1] for part in parts)
    return pl.pallas_call(
        functools.partial(weights_kernel, [len(part) for part in parts]),
        out_shape=shape((count, heads_out.shape[1], feats // count), BF16),
        in_specs=[SMEM_SPEC] + [VMEM_SPEC] * (1 + len(flat)),
        out_specs=VMEM_SPEC,
        compiler_params=params(),
        cost_estimate=cost(2 * heads_out.size * feats, 6_000_000),
    )(me, heads_out, *flat)


def layer_kernel(*refs):
    count = (len(refs) - 1) // 2
    total = None
    for s in range(count):
        term = dot(refs[s][...], refs[count + s][...])
        total = term if total is None else total + term
    refs[-1][...] = total.astype(BF16)


def layer(parts, blocks):
    rows, cols = parts[0].shape[0], blocks[0].shape[1]
    return pl.pallas_call(
        layer_kernel,
        out_shape=shape((rows, cols), BF16),
        in_specs=[VMEM_SPEC] * (len(parts) + len(blocks)),
        out_specs=VMEM_SPEC,
        compiler_params=params(),
        cost_estimate=cost(2 * rows * cols * sum(p.shape[1] for p in parts), 6_000_000),
    )(*parts, *blocks)


def swap(value, axis, distance):
    count = lax.axis_size(axis)
    return lax.ppermute(value, axis, [(i, i ^ distance) for i in range(count)])


def after(value, *others):
    return lax.optimization_barrier((value,) + others)[0]


def take(prefix, other, axis, distance, backward):
    upper = (lax.axis_index(axis) & distance) != 0
    wanted = jnp.logical_not(upper) if backward else upper
    return prefix + jnp.where(wanted, other, 0.0)


def doublings(axis):
    return [1 << i for i in range((lax.axis_size(axis) - 1).bit_length())]


def shards(queries, keys, values, w_out, cotangent):
    heads = queries.shape[1] // HDIM
    count = heads * (queries.shape[0] // SPAN)
    head_count, ctx_count = lax.axis_size("head"), lax.axis_size("ctx")
    me_head, me_ctx = lax.axis_index("head"), lax.axis_index("ctx")
    me = jnp.stack([me_head, me_ctx]).astype(jnp.int32)
    evens = range(2, head_count, 2)
    middle = cotangent.shape[0] // 2

    gram, pair = totals(keys, values, heads)
    cot = after(cotangent, gram, pair)
    pieces = (cot[:middle], cot[middle:])
    far = {s: [swap(p, "head", s) for p in pieces] for s in evens}
    near = swap(cot, "head", 1)

    grams, pairs = jnp.zeros_like(gram), jnp.zeros_like(pair)
    begun = None
    crossed = {s: [] for s in evens}
    for distance in doublings("ctx"):
        if distance == ctx_count // 2:
            gram = after(gram, begun)
            for s in evens:
                crossed[s].append(swap(after(far[s][0], gram), "head", 1))
        other_gram = swap(gram, "ctx", distance)
        other_pair = swap(pair, "ctx", distance)
        grams = take(grams, other_gram, "ctx", distance, False)
        pairs = take(pairs, other_pair, "ctx", distance, False)
        if begun is None:
            begun = head_grads(me, w_out, [[cotangent], [after(near, grams)]], 0)
        gram, pair = gram + other_gram, pair + other_pair
    *stash, last, ridged = inverses(keys, grams, count)
    pairs = after(pairs, last)
    for s in evens:
        crossed[s].append(swap(after(far[s][1], pairs), "head", 1))
    heads_out, states, solved, scores = outputs(queries, keys, values, pairs, last)

    parts = []
    for s in evens:
        parts += [far[s], crossed[s]]
    grads = head_grads(me, w_out, parts, 2, after(begun, heads_out))
    parts = [[cotangent], [near]] + parts

    terms = weight_terms(me, after(heads_out, grads), parts, ctx_count)
    halves = terms.reshape((ctx_count // 2, 2) + terms.shape[1:])
    cut = ctx_count // 4
    sent = [swap(halves[cut:, 1], "ctx", 1), swap(halves[:cut, 1], "ctx", 1)]

    width = w_out.shape[1] // head_count
    late = after(w_out, terms)
    columns = []
    for s in range(head_count):
        mine = lax.dynamic_slice_in_dim(late, (me_head ^ s) * width, width, axis=1)
        columns.append(swap(mine, "head", s) if s else mine)
    outs_out = after(heads_out, terms)
    outs_far = [swap(outs_out, "head", s) for s in evens]
    outs_near = swap(outs_out, "head", 1)

    grad_queries, dk, dv, da, dn, sums = tangent(
        queries, keys, values, after(grads, terms), [*stash, last, ridged, states, solved, scores]
    )

    sent = after(sent[0], grad_queries), sent[1]
    high = halves[cut:, 0].astype(F32) + sent[0].astype(F32)
    moved = [swap(high[u].astype(BF16), "ctx", 2 * (cut + u)) for u in range(high.shape[0])]

    later = jnp.zeros_like(sums)
    for distance in doublings("ctx"):
        other = swap(sums.astype(BF16), "ctx", distance).astype(F32)
        later = take(later, other, "ctx", distance, True)
        sums = sums + other

    low = halves[:cut, 0].astype(F32) + after(sent[1], grad_queries).astype(F32)
    moved += [swap(low[u].astype(BF16), "ctx", 2 * u) for u in range(1, cut)]
    grad_weight = low[0]
    for part in moved:
        grad_weight = grad_weight + part.astype(F32)

    outs = [heads_out, outs_near]
    for part in outs_far:
        outs += [part, swap(after(part, grad_queries), "head", 1)]
    layer_out = layer(outs, columns)
    grad_keys, grad_values = finish(keys, values, dk, dv, da, dn, later)
    return (layer_out, grad_queries, grad_keys, grad_values, grad_weight)


def solution(mesh):
    in_specs = (
        P("ctx", "head"),
        P("ctx", "head"),
        P("ctx", "head"),
        P("head", None),
        P("ctx", "head"),
    )
    out_specs = (
        P("ctx", "head"),
        P("ctx", "head"),
        P("ctx", "head"),
        P("ctx", "head"),
        P("head", "ctx"),
    )
    return jax.shard_map(shards, mesh=mesh, in_specs=in_specs, out_specs=out_specs, check_vma=False)
```

```python
import functools

import jax
import jax.numpy as jnp
from jax import lax
from jax.experimental import pallas as pl
from jax.experimental.pallas import tpu as pltpu
from jax.sharding import PartitionSpec as P


HDIM = 128
SPAN = 256
NEWTON = 8
RIDGE = 1.0
F32 = jnp.float32
BF16 = jnp.bfloat16
VMEM_SPEC = pl.BlockSpec(memory_space=pltpu.VMEM)
HBM_SPEC = pl.BlockSpec(memory_space=pltpu.HBM)
SMEM_SPEC = pl.BlockSpec(memory_space=pltpu.SMEM)


def dot(left, right, axes=(1, 0)):
    return lax.dot_general(
        left, right, (((axes[0],), (axes[1],)), ((), ())), preferred_element_type=F32
    )


def split(value):
    high = value.astype(BF16)
    return high, (value - high.astype(F32)).astype(BF16)


def cat(parts, axis):
    return jnp.concatenate(parts, axis=axis)


def params(limit=8):
    return pltpu.CompilerParams(vmem_limit_bytes=limit * 1024 * 1024)


def cost(flops, size):
    return pl.CostEstimate(flops=flops, bytes_accessed=size, transcendentals=0)


def shape(dims, dtype=F32):
    return jax.ShapeDtypeStruct(dims, dtype)


def unit():
    rows = lax.broadcasted_iota(jnp.int32, (HDIM, HDIM), 0)
    cols = lax.broadcasted_iota(jnp.int32, (HDIM, HDIM), 1)
    return rows == cols


def causal():
    rows = lax.broadcasted_iota(jnp.int32, (SPAN, SPAN), 0)
    cols = lax.broadcasted_iota(jnp.int32, (SPAN, SPAN), 1)
    return rows >= cols


def corner():
    rows = lax.broadcasted_iota(jnp.int32, (HDIM, HDIM), 0)
    cols = lax.broadcasted_iota(jnp.int32, (HDIM, HDIM), 1)
    return rows, cols


def fold(one, two):
    rows, cols = corner()
    both = jnp.where(rows <= cols, one, two)
    line = jnp.sum(jnp.where(rows == cols, two, 0.0), axis=0, keepdims=True)
    return both, jnp.broadcast_to(line, (8, HDIM))


def unfold(both, line):
    rows, cols = corner()
    turned = both.T
    one = jnp.where(rows <= cols, both, turned)
    two = jnp.where(rows > cols, both, turned)
    two = jnp.where(rows == cols, line[:1], two)
    return one, two


def folded(heads):
    return (heads + 1) // 2


def fold_into(ref, mats, base=0):
    for i in range(folded(len(mats))):
        one, two = mats[2 * i], mats[min(2 * i + 1, len(mats) - 1)]
        both, line = fold(one, two)
        top = base + i * (HDIM + 8)
        ref[top : top + HDIM, :] = both
        ref[top + HDIM : top + HDIM + 8, :] = line


def unfold_from(ref, heads, base=0):
    mats = []
    for i in range(folded(heads)):
        top = base + i * (HDIM + 8)
        mats += unfold(ref[top : top + HDIM, :], ref[top + HDIM : top + HDIM + 8, :])
    return mats[:heads]


def totals_kernel(me_ref, k_hbm, v_hbm, g_ref, n_ref, k_ref, v_ref, sem):
    copies = [
        pltpu.make_async_copy(k_hbm, k_ref, sem.at[0]),
        pltpu.make_async_copy(v_hbm, v_ref, sem.at[1]),
    ]
    for copy in copies:
        copy.start()
    for copy in copies:
        copy.wait()
    grams = []
    for h in range(k_ref.shape[1] // HDIM):
        cols = slice(h * HDIM, (h + 1) * HDIM)
        k = k_ref[:, cols]
        both = dot(k, cat([k, v_ref[:, cols]], 1), (0, 0))
        grams.append(both[:, :HDIM])
        n_ref[cols, :] = both[:, HDIM:]
    fold_into(g_ref, grams)


def totals(me, keys, values, heads):
    return pl.pallas_call(
        totals_kernel,
        out_shape=(shape((folded(heads) * (HDIM + 8), HDIM)), shape((heads * HDIM, HDIM))),
        in_specs=[SMEM_SPEC, HBM_SPEC, HBM_SPEC],
        out_specs=(VMEM_SPEC, VMEM_SPEC),
        scratch_shapes=[pltpu.VMEM(keys.shape, BF16)] * 2 + [pltpu.SemaphoreType.DMA((2,))],
        compiler_params=params(60),
        cost_estimate=cost(2 * 2 * keys.size * HDIM, 4 * keys.size),
    )(me, keys, values)


def taken(me_ref, refs, backward):
    total = None
    for r, ref in enumerate(refs):
        bit = (me_ref[1] >> r) & 1
        wanted = jnp.where(bit == (0 if backward else 1), 1.0, 0.0)
        part = ref[...].astype(F32) * wanted
        total = part if total is None else total + part
    return total


def places(q_ref, heads):
    blocks = q_ref.shape[0] // SPAN
    for h in range(heads):
        for b in range(blocks):
            yield h, b, h * blocks + b, slice(b * SPAN, (b + 1) * SPAN), slice(h * HDIM, (h + 1) * HDIM)


def inverse_kernel(rounds, me_ref, k_ref, *refs):
    e_ref, x_ref, last_ref, a_ref, es, xs = refs[rounds:]
    heads = k_ref.shape[1] // HDIM
    eye = unit()
    grams = unfold_from(taken(me_ref, refs[:rounds], False), heads)
    for h, b, i, rows, cols in places(k_ref, heads):
        ridged = grams[h] + jnp.where(eye, RIDGE, 0.0)
        scale = 1.0 / jnp.sqrt(jnp.sum(ridged * ridged, keepdims=True))
        a_ref[i] = ridged
        es[i] = ridged * scale
        xs[i] = jnp.where(eye, scale, 0.0)
        k = k_ref[rows, cols]
        grams[h] = grams[h] + dot(k, k, (0, 0))
    nil = jnp.zeros((HDIM, HDIM), BF16)

    def step(j, carry):
        for i in range(es.shape[0]):
            e, x = es[i], xs[i]
            eh, el = split(e)
            xh, xl = split(x)
            e_ref[j, i] = eh
            x_ref[j, i] = xh
            left = cat([cat([eh, el], 1), cat([xh, xl], 1)], 0)
            right = cat([cat([eh, el], 1), cat([eh, nil], 1)], 0)
            both = dot(left, right)
            both = both[:, :HDIM] + both[:, HDIM:]
            es[i] = 2.0 * e - both[:HDIM]
            xs[i] = 2.0 * x - both[HDIM:]
        return carry

    lax.fori_loop(0, NEWTON, step, 0)
    for i in range(xs.shape[0]):
        last_ref[i] = xs[i]


def inverses(me, keys, grams, count):
    stash = shape((NEWTON, count, HDIM, HDIM), BF16)
    state = shape((count, HDIM, HDIM))
    return pl.pallas_call(
        functools.partial(inverse_kernel, len(grams)),
        out_shape=(stash, stash, state, state),
        in_specs=[SMEM_SPEC] + [VMEM_SPEC] * (1 + len(grams)),
        out_specs=(VMEM_SPEC,) * 4,
        scratch_shapes=[pltpu.VMEM((count, HDIM, HDIM), F32)] * 2,
        compiler_params=params(),
        cost_estimate=cost(2_000_000_000, 8_000_000),
    )(me, keys, *grams)


def outputs_kernel(rounds, me_ref, q_ref, k_ref, v_ref, last_ref, *refs):
    out_ref, pre_ref, s_ref, w_ref = refs[rounds:]
    prefix = taken(me_ref, refs[:rounds], False)
    heads = q_ref.shape[1] // HDIM
    keep = causal()
    nil = jnp.zeros((HDIM, HDIM), BF16)
    pairs = [prefix[h * HDIM : (h + 1) * HDIM, :] for h in range(heads)]
    for h, b, i, rows, cols in places(q_ref, heads):
        q, k, v = q_ref[rows, cols], k_ref[rows, cols], v_ref[rows, cols]
        xh, xl = split(last_ref[i])
        sh, sl = split(dot(cat([q, q], 1), cat([xh, xl], 0)))
        both = cat([sh, sl], 1)
        s_ref[i] = both
        scores = dot(both, cat([k, k], 1), (1, 1))
        scores = jnp.where(keep, scores, 0.0).astype(BF16)
        w_ref[i] = scores
        nh, nl = split(pairs[h])
        pre_ref[i] = cat([nh, nl], 1)
        state = dot(both, cat([cat([nh, nl], 1), cat([nh, nil], 1)], 0))
        out = dot(scores, v) + state[:, :HDIM] + state[:, HDIM:]
        out_ref[rows, cols] = out.astype(BF16)
        pairs[h] = pairs[h] + dot(k, v, (0, 0))


def outputs(me, queries, keys, values, last, pairs):
    count = last.shape[0]
    return pl.pallas_call(
        functools.partial(outputs_kernel, len(pairs)),
        out_shape=(
            shape(queries.shape, BF16),
            shape((count, HDIM, 2 * HDIM), BF16),
            shape((count, SPAN, 2 * HDIM), BF16),
            shape((count, SPAN, SPAN), BF16),
        ),
        in_specs=[SMEM_SPEC] + [VMEM_SPEC] * (4 + len(pairs)),
        out_specs=(VMEM_SPEC,) * 4,
        compiler_params=params(),
        cost_estimate=cost(2_000_000_000, 8_000_000),
    )(me, queries, keys, values, last, *pairs)


def tangent_kernel(
    q_ref, k_ref, v_ref, do_ref, e_ref, x_ref, last_ref, a_ref, pre_ref, s_ref, w_ref,
    dq_ref, dk_ref, dv_ref, da_ref, dn_ref, sum_ref, send_ref, des, dxs, first,
):
    heads = q_ref.shape[1] // HDIM
    keep = causal()
    nil = jnp.zeros((HDIM, HDIM), BF16)
    for h, b, i, rows, cols in places(q_ref, heads):
        q, k, v, do = q_ref[rows, cols], k_ref[rows, cols], v_ref[rows, cols], do_ref[rows, cols]
        weights = jnp.where(keep, dot(do, v, (1, 1)), 0.0).astype(BF16)
        ds = dot(weights, k) + dot(cat([do, do], 1), pre_ref[i], (1, 1))
        ds = ds.astype(BF16)
        xh, xl = split(last_ref[i])
        inverse = cat([xh, xl], 0)
        both = s_ref[i]
        sh = both[:, :HDIM]
        scores = w_ref[i]
        dv_ref[rows, cols] = dot(scores, do, (0, 0))
        dk_ref[rows, cols] = dot(weights, sh, (0, 0))
        state = dot(both, do, (0, 0))
        dn_ref[i] = state[:HDIM] + state[HDIM:]
        dq_ref[rows, cols] = dot(cat([ds, ds], 1), inverse).astype(BF16)
        bar = dot(q, ds, (0, 0))
        bar = bar + bar.T
        ridged = a_ref[i]
        scale = 1.0 / jnp.sqrt(jnp.sum(ridged * ridged, keepdims=True))
        first[i] = bar
        des[i] = bar * scale
        dxs[i] = jnp.zeros((HDIM, HDIM), F32)

    def step(j, carry):
        for i in range(des.shape[0]):
            e, x = e_ref[j, i], x_ref[j, i]
            de, dx = des[i], dxs[i]
            left = cat([cat([dx.astype(BF16), x], 1), cat([nil, e], 1)], 0)
            both = dot(left, cat([e, de.astype(BF16)], 0))
            turned = both[HDIM:]
            dxs[i] = 2.0 * dx - both[:HDIM]
            des[i] = 2.0 * de - (turned + turned.T)
        return carry

    lax.fori_loop(0, NEWTON, step, 0)
    sum_a = [jnp.zeros((HDIM, HDIM), F32) for _ in range(heads)]
    sum_n = [jnp.zeros((HDIM, HDIM), F32) for _ in range(heads)]
    for h, b, i, rows, cols in places(q_ref, heads):
        ridged, dx = a_ref[i], dxs[i]
        square = jnp.sum(ridged * ridged, keepdims=True)
        along = jnp.sum(first[i] * last_ref[i] + dx * ridged, keepdims=True)
        da = dx - (along / square) * ridged
        da_ref[i] = da
        sum_a[h] = sum_a[h] + da
        sum_n[h] = sum_n[h] + dn_ref[i]
    for h in range(heads):
        sum_ref[h * HDIM : (h + 1) * HDIM, :] = sum_n[h]
    fold_into(sum_ref, sum_a, heads * HDIM)
    send_ref[...] = sum_ref[...].astype(BF16)


def tangent(queries, keys, values, grads, stash):
    heads = queries.shape[1] // HDIM
    count = stash[-1].shape[0]
    state = shape((count, HDIM, HDIM))
    wide = shape(queries.shape)
    rows = heads * HDIM + folded(heads) * (HDIM + 8)
    return pl.pallas_call(
        tangent_kernel,
        out_shape=(
            shape(queries.shape, BF16), wide, wide, state, state,
            shape((rows, HDIM)), shape((rows, HDIM), BF16),
        ),
        in_specs=[VMEM_SPEC] * 11,
        out_specs=(VMEM_SPEC,) * 7,
        scratch_shapes=[pltpu.VMEM((count, HDIM, HDIM), F32)] * 3,
        compiler_params=params(),
        cost_estimate=cost(4_000_000_000, 8_000_000),
    )(queries, keys, values, grads, *stash)


def finish_kernel(rounds, me_ref, k_ref, v_ref, dk_ref, dv_ref, da_ref, dn_ref, *refs):
    gk_ref, gv_ref = refs[rounds:]
    sum_ref = taken(me_ref, refs[:rounds], True)
    heads = k_ref.shape[1] // HDIM
    sa = unfold_from(sum_ref, heads, heads * HDIM)
    sn = [sum_ref[h * HDIM : (h + 1) * HDIM, :] for h in range(heads)]
    for h, b, i, rows, cols in reversed(list(places(k_ref, heads))):
        k, v = k_ref[rows, cols], v_ref[rows, cols]
        nh, nl = split(sn[h])
        grad_k = dk_ref[rows, cols] + dot(k, sa[h].astype(BF16))
        grad_k = grad_k + dot(cat([v, v], 1), cat([nh, nl], 1), (1, 1))
        grad_v = dv_ref[rows, cols] + dot(cat([k, k], 1), cat([nh, nl], 0))
        gk_ref[rows, cols] = grad_k.astype(BF16)
        gv_ref[rows, cols] = grad_v.astype(BF16)
        sa[h] = sa[h] + da_ref[i]
        sn[h] = sn[h] + dn_ref[i]


def finish(me, keys, values, dk, dv, da, dn, sums):
    return pl.pallas_call(
        functools.partial(finish_kernel, len(sums)),
        out_shape=(shape(keys.shape, BF16),) * 2,
        in_specs=[SMEM_SPEC] + [VMEM_SPEC] * (6 + len(sums)),
        out_specs=(VMEM_SPEC,) * 2,
        compiler_params=params(),
        cost_estimate=cost(1_000_000_000, 6_000_000),
    )(me, keys, values, dk, dv, da, dn, *sums)


def grads_kernel(first, me_ref, w_ref, *refs):
    out_ref = refs[-1]
    me = me_ref[0]
    total = refs[0][...] if first else None
    for s, part in enumerate(refs[1:-1] if first else refs[:-1]):
        width = part.shape[1]
        cols = pl.ds(pl.multiple_of((me ^ (first + s)) * width, width), width)
        term = dot(part[...], w_ref[:, cols], (1, 1))
        total = term if total is None else total + term
    out_ref[...] = total.astype(out_ref.dtype)


def head_grads(me, w_out, parts, first, begun=None):
    rows = parts[0].shape[0]
    begun = [] if begun is None else [begun]
    return pl.pallas_call(
        functools.partial(grads_kernel, first),
        out_shape=shape((rows, w_out.shape[0]), BF16 if begun else F32),
        in_specs=[SMEM_SPEC] + [VMEM_SPEC] * (1 + len(parts) + len(begun)),
        out_specs=VMEM_SPEC,
        compiler_params=params(),
        cost_estimate=cost(rows * w_out.size, 4_000_000),
    )(me, w_out, *begun, *parts)


def columns_kernel(me_ref, w_ref, *refs):
    for s, out_ref in enumerate(refs):
        width = out_ref.shape[1]
        cols = pl.ds(pl.multiple_of((me_ref[0] ^ s) * width, width), width)
        out_ref[...] = w_ref[:, cols]


def column_pieces(me, w_out, count):
    piece = shape((w_out.shape[0], w_out.shape[1] // count), BF16)
    return pl.pallas_call(
        columns_kernel,
        out_shape=(piece,) * count,
        in_specs=[SMEM_SPEC, VMEM_SPEC],
        out_specs=(VMEM_SPEC,) * count,
        compiler_params=params(),
        cost_estimate=cost(0, 4 * w_out.size),
    )(me, w_out)


def weights_kernel(me_ref, h_ref, *refs):
    parts, outs, all_ref = refs[:-5], refs[-5:-1], refs[-1]
    me, mine = me_ref[0], me_ref[1]
    count, _, width = all_ref.shape
    fold = parts[0].shape[1] // width
    for s, part in enumerate(parts):
        term = dot(h_ref[...], part[...], (0, 0)).astype(BF16)
        for f in range(fold):
            target = (me ^ s) * fold + f
            all_ref[target ^ mine] = term[:, f * width : (f + 1) * width]
    for t in range(count):
        ref = outs[2 * (t % 2) + (t >= count // 2)]
        ref[t % (count // 2) // 2] = all_ref[t]


def weight_terms(me, heads_out, parts, count):
    feats = sum(part.shape[1] for part in parts)
    piece = (heads_out.shape[1], feats // count)
    return pl.pallas_call(
        weights_kernel,
        out_shape=(shape((count // 4,) + piece, BF16),) * 4,
        in_specs=[SMEM_SPEC] + [VMEM_SPEC] * (1 + len(parts)),
        out_specs=(VMEM_SPEC,) * 4,
        scratch_shapes=[pltpu.VMEM((count,) + piece, BF16)],
        compiler_params=params(),
        cost_estimate=cost(2 * heads_out.size * feats, 6_000_000),
    )(me, heads_out, *parts)


def layer_kernel(*refs):
    count = (len(refs) - 1) // 2
    total = None
    for s in range(count):
        term = dot(refs[s][...], refs[count + s][...])
        total = term if total is None else total + term
    refs[-1][...] = total.astype(BF16)


def layer(parts, blocks):
    rows, cols = parts[0].shape[0], blocks[0].shape[1]
    return pl.pallas_call(
        layer_kernel,
        out_shape=shape((rows, cols), BF16),
        in_specs=[VMEM_SPEC] * (len(parts) + len(blocks)),
        out_specs=VMEM_SPEC,
        compiler_params=params(),
        cost_estimate=cost(2 * rows * cols * sum(p.shape[1] for p in parts), 6_000_000),
    )(*parts, *blocks)


def swap(value, axis, distance):
    count = lax.axis_size(axis)
    return lax.ppermute(value, axis, [(i, i ^ distance) for i in range(count)])


def after(value, *others):
    return lax.optimization_barrier((value,) + others)[0]


def doublings(axis):
    return [1 << i for i in range((lax.axis_size(axis) - 1).bit_length())]


def shards(queries, keys, values, w_out, cotangent):
    heads = queries.shape[1] // HDIM
    count = heads * (queries.shape[0] // SPAN)
    head_count, ctx_count = lax.axis_size("head"), lax.axis_size("ctx")
    me = jnp.stack([lax.axis_index("head"), lax.axis_index("ctx")]).astype(jnp.int32)
    evens = range(2, head_count, 2)

    gram, pair = totals(me, keys, values, heads)
    cot = after(cotangent, gram, pair)
    far = {s: swap(cot, "head", s) for s in evens}
    near = swap(cot, "head", 1)

    grams, pairs = [], []
    begun = None
    for distance in doublings("ctx"):
        if distance == ctx_count // 2:
            gram = after(gram, begun)
        grams.append(swap(gram, "ctx", distance))
        pairs.append(swap(pair, "ctx", distance))
        if begun is None:
            begun = head_grads(me, w_out, [cotangent, after(near, grams[0])], 0)
        gram, pair = gram + grams[-1], pair + pairs[-1]
    *stash, last, ridged = inverses(me, keys, grams, count)
    pairs[-1] = after(pairs[-1], last)
    parts = []
    for s in evens:
        parts += [far[s], swap(after(far[s], pairs[-1]), "head", 1)]
    columns = column_pieces(me, after(w_out, begun), head_count)
    columns = [after(c, pairs[-1], *far.values()) for c in columns]
    columns = [swap(c, "head", s) if s else c for s, c in enumerate(columns)]
    heads_out, states, solved, scores = outputs(me, queries, keys, values, last, pairs)

    grads = head_grads(me, w_out, parts, 2, after(begun, heads_out))
    parts = [cotangent, near] + parts
    even_low, even_high, odd_low, odd_high = weight_terms(
        me, after(heads_out, grads), parts, ctx_count
    )
    high = swap(odd_high, "ctx", 1)
    low = swap(odd_low, "ctx", 1)

    outs_out = after(heads_out, odd_low)
    outs_far = [swap(outs_out, "head", s) for s in evens]
    outs_near = swap(outs_out, "head", 1)

    grad_queries, dk, dv, da, dn, sums, send = tangent(
        queries, keys, values, after(grads, odd_low), [*stash, last, ridged, states, solved, scores]
    )

    high, low = after(high, grad_queries), after(low, grad_queries)
    high = even_high.astype(F32) + high.astype(F32)
    half = ctx_count // 4
    moved = [swap(high[u].astype(BF16), "ctx", 2 * (half + u)) for u in range(half)]

    later = []
    for distance in doublings("ctx"):
        later.append(swap(send, "ctx", distance))
        sums = sums + later[-1].astype(F32)
        send = sums.astype(BF16)

    low = even_low.astype(F32) + low.astype(F32)
    moved += [swap(low[u].astype(BF16), "ctx", 2 * u) for u in range(1, half)]
    grad_weight = low[0]
    for part in moved:
        grad_weight = grad_weight + part.astype(F32)

    outs = [heads_out, outs_near]
    for part in outs_far:
        outs += [part, swap(after(part, grad_queries), "head", 1)]
    layer_out = layer(outs, columns)
    grad_keys, grad_values = finish(me, keys, values, dk, dv, da, dn, later)
    return (layer_out, grad_queries, grad_keys, grad_values, grad_weight)


def solution(mesh):
    in_specs = (
        P("ctx", "head"),
        P("ctx", "head"),
        P("ctx", "head"),
        P("head", None),
        P("ctx", "head"),
    )
    out_specs = (
        P("ctx", "head"),
        P("ctx", "head"),
        P("ctx", "head"),
        P("ctx", "head"),
        P("head", "ctx"),
    )
    return jax.shard_map(shards, mesh=mesh, in_specs=in_specs, out_specs=out_specs, check_vma=False)
```

```python
import functools

import jax
import jax.numpy as jnp
from jax import lax
from jax.experimental import pallas as pl
from jax.experimental.pallas import tpu as pltpu
from jax.sharding import PartitionSpec as P


HDIM = 128
SPAN = 256
NEWTON = 8
RIDGE = 1.0
F32 = jnp.float32
BF16 = jnp.bfloat16
VMEM_SPEC = pl.BlockSpec(memory_space=pltpu.VMEM)


def dot(left, right, axes=(1, 0)):
    return lax.dot_general(
        left, right, (((axes[0],), (axes[1],)), ((), ())), preferred_element_type=F32
    )


def split(value):
    high = value.astype(BF16)
    return high, (value - high.astype(F32)).astype(BF16)


def cat(parts, axis):
    return jnp.concatenate(parts, axis=axis)


def params(limit=8):
    return pltpu.CompilerParams(vmem_limit_bytes=limit * 1024 * 1024)


def cost(flops, size):
    return pl.CostEstimate(flops=flops, bytes_accessed=size, transcendentals=0)


def shape(dims, dtype=F32):
    return jax.ShapeDtypeStruct(dims, dtype)


def unit():
    rows = lax.broadcasted_iota(jnp.int32, (HDIM, HDIM), 0)
    cols = lax.broadcasted_iota(jnp.int32, (HDIM, HDIM), 1)
    return rows == cols


def causal():
    rows = lax.broadcasted_iota(jnp.int32, (SPAN, SPAN), 0)
    cols = lax.broadcasted_iota(jnp.int32, (SPAN, SPAN), 1)
    return rows >= cols


def corner():
    rows = lax.broadcasted_iota(jnp.int32, (HDIM, HDIM), 0)
    cols = lax.broadcasted_iota(jnp.int32, (HDIM, HDIM), 1)
    return rows, cols


def fold(one, two):
    rows, cols = corner()
    both = jnp.where(rows <= cols, one, two)
    line = jnp.sum(jnp.where(rows == cols, two, 0.0), axis=0, keepdims=True)
    return both, jnp.broadcast_to(line, (8, HDIM))


def unfold(both, line):
    rows, cols = corner()
    turned = both.T
    one = jnp.where(rows <= cols, both, turned)
    two = jnp.where(rows > cols, both, turned)
    two = jnp.where(rows == cols, line[:1], two)
    return one, two


def folded(heads):
    return (heads + 1) // 2


def fold_into(ref, mats, base=0):
    for i in range(folded(len(mats))):
        one, two = mats[2 * i], mats[min(2 * i + 1, len(mats) - 1)]
        both, line = fold(one, two)
        top = base + i * (HDIM + 8)
        ref[top : top + HDIM, :] = both
        ref[top + HDIM : top + HDIM + 8, :] = line


def unfold_from(ref, heads, base=0):
    mats = []
    for i in range(folded(heads)):
        top = base + i * (HDIM + 8)
        mats += unfold(ref[top : top + HDIM, :], ref[top + HDIM : top + HDIM + 8, :])
    return mats[:heads]


def totals_kernel(k_ref, v_ref, g_ref, n_ref):
    grams = []
    for h in range(k_ref.shape[1] // HDIM):
        cols = slice(h * HDIM, (h + 1) * HDIM)
        k = k_ref[:, cols]
        both = dot(k, cat([k, v_ref[:, cols]], 1), (0, 0))
        grams.append(both[:, :HDIM])
        n_ref[cols, :] = both[:, HDIM:]
    fold_into(g_ref, grams)


def totals(keys, values, heads):
    return pl.pallas_call(
        totals_kernel,
        out_shape=(shape((folded(heads) * (HDIM + 8), HDIM)), shape((heads * HDIM, HDIM))),
        in_specs=[VMEM_SPEC] * 2,
        out_specs=(VMEM_SPEC, VMEM_SPEC),
        compiler_params=params(),
        cost_estimate=cost(2 * 2 * keys.size * HDIM, 4 * keys.size),
    )(keys, values)


def taken(refs, backward):
    total = None
    mine = lax.axis_index("ctx")
    for r, ref in enumerate(refs):
        bit = (mine >> r) & 1
        wanted = jnp.where(bit == (0 if backward else 1), 1.0, 0.0)
        part = ref[...].astype(F32) * wanted
        total = part if total is None else total + part
    return total


def places(q_ref, heads):
    blocks = q_ref.shape[0] // SPAN
    for h in range(heads):
        for b in range(blocks):
            yield h, b, h * blocks + b, slice(b * SPAN, (b + 1) * SPAN), slice(h * HDIM, (h + 1) * HDIM)


def inverse_kernel(rounds, k_ref, *refs):
    e_ref, x_ref, last_ref, a_ref, es, xs = refs[rounds:]
    heads = k_ref.shape[1] // HDIM
    eye = unit()
    grams = unfold_from(taken(refs[:rounds], False), heads)
    for h, b, i, rows, cols in places(k_ref, heads):
        ridged = grams[h] + jnp.where(eye, RIDGE, 0.0)
        scale = 1.0 / jnp.sqrt(jnp.sum(ridged * ridged, keepdims=True))
        a_ref[i] = ridged
        es[i] = ridged * scale
        xs[i] = jnp.where(eye, scale, 0.0)
        k = k_ref[rows, cols]
        grams[h] = grams[h] + dot(k, k, (0, 0))
    nil = jnp.zeros((HDIM, HDIM), BF16)

    def step(j, carry):
        for i in range(es.shape[0]):
            e, x = es[i], xs[i]
            eh, el = split(e)
            xh, xl = split(x)
            e_ref[j, i] = eh
            x_ref[j, i] = xh
            left = cat([cat([eh, el], 1), cat([xh, xl], 1)], 0)
            right = cat([cat([eh, el], 1), cat([eh, nil], 1)], 0)
            both = dot(left, right)
            both = both[:, :HDIM] + both[:, HDIM:]
            es[i] = 2.0 * e - both[:HDIM]
            xs[i] = 2.0 * x - both[HDIM:]
        return carry

    lax.fori_loop(0, NEWTON, step, 0)
    for i in range(xs.shape[0]):
        last_ref[i] = xs[i]


def inverses(keys, grams, count):
    stash = shape((NEWTON, count, HDIM, HDIM), BF16)
    state = shape((count, HDIM, HDIM))
    return pl.pallas_call(
        functools.partial(inverse_kernel, len(grams)),
        out_shape=(stash, stash, state, state),
        in_specs=[VMEM_SPEC] * (1 + len(grams)),
        out_specs=(VMEM_SPEC,) * 4,
        scratch_shapes=[pltpu.VMEM((count, HDIM, HDIM), F32)] * 2,
        compiler_params=params(),
        cost_estimate=cost(2_000_000_000, 8_000_000),
    )(keys, *grams)


def outputs_kernel(rounds, q_ref, k_ref, v_ref, last_ref, *refs):
    out_ref, pre_ref, s_ref, w_ref = refs[rounds:]
    prefix = taken(refs[:rounds], False)
    heads = q_ref.shape[1] // HDIM
    keep = causal()
    nil = jnp.zeros((HDIM, HDIM), BF16)
    pairs = [prefix[h * HDIM : (h + 1) * HDIM, :] for h in range(heads)]
    for h, b, i, rows, cols in places(q_ref, heads):
        q, k, v = q_ref[rows, cols], k_ref[rows, cols], v_ref[rows, cols]
        xh, xl = split(last_ref[i])
        sh, sl = split(dot(cat([q, q], 1), cat([xh, xl], 0)))
        both = cat([sh, sl], 1)
        s_ref[i] = both
        scores = dot(both, cat([k, k], 1), (1, 1))
        scores = jnp.where(keep, scores, 0.0).astype(BF16)
        w_ref[i] = scores
        nh, nl = split(pairs[h])
        pre_ref[i] = cat([nh, nl], 1)
        state = dot(both, cat([cat([nh, nl], 1), cat([nh, nil], 1)], 0))
        out = dot(scores, v) + state[:, :HDIM] + state[:, HDIM:]
        out_ref[rows, cols] = out.astype(BF16)
        pairs[h] = pairs[h] + dot(k, v, (0, 0))


def outputs(queries, keys, values, last, pairs):
    count = last.shape[0]
    return pl.pallas_call(
        functools.partial(outputs_kernel, len(pairs)),
        out_shape=(
            shape(queries.shape, BF16),
            shape((count, HDIM, 2 * HDIM), BF16),
            shape((count, SPAN, 2 * HDIM), BF16),
            shape((count, SPAN, SPAN), BF16),
        ),
        in_specs=[VMEM_SPEC] * (4 + len(pairs)),
        out_specs=(VMEM_SPEC,) * 4,
        compiler_params=params(),
        cost_estimate=cost(2_000_000_000, 8_000_000),
    )(queries, keys, values, last, *pairs)


def tangent_kernel(
    q_ref, k_ref, v_ref, do_ref, e_ref, x_ref, last_ref, a_ref, pre_ref, s_ref, w_ref,
    dq_ref, dk_ref, dv_ref, da_ref, dn_ref, sum_ref, send_ref, des, dxs, first,
):
    heads = q_ref.shape[1] // HDIM
    keep = causal()
    nil = jnp.zeros((HDIM, HDIM), BF16)
    for h, b, i, rows, cols in places(q_ref, heads):
        q, k, v, do = q_ref[rows, cols], k_ref[rows, cols], v_ref[rows, cols], do_ref[rows, cols]
        weights = jnp.where(keep, dot(do, v, (1, 1)), 0.0).astype(BF16)
        ds = dot(weights, k) + dot(cat([do, do], 1), pre_ref[i], (1, 1))
        ds = ds.astype(BF16)
        xh, xl = split(last_ref[i])
        inverse = cat([xh, xl], 0)
        both = s_ref[i]
        sh = both[:, :HDIM]
        scores = w_ref[i]
        dv_ref[rows, cols] = dot(scores, do, (0, 0))
        dk_ref[rows, cols] = dot(weights, sh, (0, 0))
        state = dot(both, do, (0, 0))
        dn_ref[i] = state[:HDIM] + state[HDIM:]
        dq_ref[rows, cols] = dot(cat([ds, ds], 1), inverse).astype(BF16)
        bar = dot(q, ds, (0, 0))
        bar = bar + bar.T
        ridged = a_ref[i]
        scale = 1.0 / jnp.sqrt(jnp.sum(ridged * ridged, keepdims=True))
        first[i] = bar
        des[i] = bar * scale
        dxs[i] = jnp.zeros((HDIM, HDIM), F32)

    def step(j, carry):
        for i in range(des.shape[0]):
            e, x = e_ref[j, i], x_ref[j, i]
            de, dx = des[i], dxs[i]
            left = cat([cat([dx.astype(BF16), x], 1), cat([nil, e], 1)], 0)
            both = dot(left, cat([e, de.astype(BF16)], 0))
            turned = both[HDIM:]
            dxs[i] = 2.0 * dx - both[:HDIM]
            des[i] = 2.0 * de - (turned + turned.T)
        return carry

    lax.fori_loop(0, NEWTON, step, 0)
    sum_a = [jnp.zeros((HDIM, HDIM), F32) for _ in range(heads)]
    sum_n = [jnp.zeros((HDIM, HDIM), F32) for _ in range(heads)]
    for h, b, i, rows, cols in places(q_ref, heads):
        ridged, dx = a_ref[i], dxs[i]
        square = jnp.sum(ridged * ridged, keepdims=True)
        along = jnp.sum(first[i] * last_ref[i] + dx * ridged, keepdims=True)
        da = dx - (along / square) * ridged
        da_ref[i] = da
        sum_a[h] = sum_a[h] + da
        sum_n[h] = sum_n[h] + dn_ref[i]
    for h in range(heads):
        sum_ref[h * HDIM : (h + 1) * HDIM, :] = sum_n[h]
    fold_into(sum_ref, sum_a, heads * HDIM)
    send_ref[...] = sum_ref[...].astype(BF16)


def tangent(queries, keys, values, grads, stash):
    heads = queries.shape[1] // HDIM
    count = stash[-1].shape[0]
    state = shape((count, HDIM, HDIM))
    wide = shape(queries.shape)
    rows = heads * HDIM + folded(heads) * (HDIM + 8)
    return pl.pallas_call(
        tangent_kernel,
        out_shape=(
            shape(queries.shape, BF16), wide, wide, state, state,
            shape((rows, HDIM)), shape((rows, HDIM), BF16),
        ),
        in_specs=[VMEM_SPEC] * 11,
        out_specs=(VMEM_SPEC,) * 7,
        scratch_shapes=[pltpu.VMEM((count, HDIM, HDIM), F32)] * 3,
        compiler_params=params(),
        cost_estimate=cost(4_000_000_000, 8_000_000),
    )(queries, keys, values, grads, *stash)


def finish_kernel(rounds, k_ref, v_ref, dk_ref, dv_ref, da_ref, dn_ref, *refs):
    gk_ref, gv_ref = refs[rounds:]
    sum_ref = taken(refs[:rounds], True)
    heads = k_ref.shape[1] // HDIM
    sa = unfold_from(sum_ref, heads, heads * HDIM)
    sn = [sum_ref[h * HDIM : (h + 1) * HDIM, :] for h in range(heads)]
    for h, b, i, rows, cols in reversed(list(places(k_ref, heads))):
        k, v = k_ref[rows, cols], v_ref[rows, cols]
        nh, nl = split(sn[h])
        grad_k = dk_ref[rows, cols] + dot(k, sa[h].astype(BF16))
        grad_k = grad_k + dot(cat([v, v], 1), cat([nh, nl], 1), (1, 1))
        grad_v = dv_ref[rows, cols] + dot(cat([k, k], 1), cat([nh, nl], 0))
        gk_ref[rows, cols] = grad_k.astype(BF16)
        gv_ref[rows, cols] = grad_v.astype(BF16)
        sa[h] = sa[h] + da_ref[i]
        sn[h] = sn[h] + dn_ref[i]


def finish(keys, values, dk, dv, da, dn, sums):
    return pl.pallas_call(
        functools.partial(finish_kernel, len(sums)),
        out_shape=(shape(keys.shape, BF16),) * 2,
        in_specs=[VMEM_SPEC] * (6 + len(sums)),
        out_specs=(VMEM_SPEC,) * 2,
        compiler_params=params(),
        cost_estimate=cost(1_000_000_000, 6_000_000),
    )(keys, values, dk, dv, da, dn, *sums)


def grads_kernel(first, w_ref, *refs):
    out_ref = refs[-1]
    me = lax.axis_index("head")
    total = refs[0][...] if first else None
    for s, part in enumerate(refs[1:-1] if first else refs[:-1]):
        width = part.shape[1]
        cols = pl.ds(pl.multiple_of((me ^ (first + s)) * width, width), width)
        term = dot(part[...], w_ref[:, cols], (1, 1))
        total = term if total is None else total + term
    out_ref[...] = total.astype(out_ref.dtype)


def head_grads(w_out, parts, first, begun=None):
    rows = parts[0].shape[0]
    begun = [] if begun is None else [begun]
    return pl.pallas_call(
        functools.partial(grads_kernel, first),
        out_shape=shape((rows, w_out.shape[0]), BF16 if begun else F32),
        in_specs=[VMEM_SPEC] * (1 + len(parts) + len(begun)),
        out_specs=VMEM_SPEC,
        compiler_params=params(),
        cost_estimate=cost(rows * w_out.size, 4_000_000),
    )(w_out, *begun, *parts)


def columns_kernel(w_ref, *refs):
    for s, out_ref in enumerate(refs):
        width = out_ref.shape[1]
        cols = pl.ds(pl.multiple_of((lax.axis_index("head") ^ s) * width, width), width)
        out_ref[...] = w_ref[:, cols]


def column_pieces(w_out, count):
    piece = shape((w_out.shape[0], w_out.shape[1] // count), BF16)
    return pl.pallas_call(
        columns_kernel,
        out_shape=(piece,) * count,
        in_specs=[VMEM_SPEC],
        out_specs=(VMEM_SPEC,) * count,
        compiler_params=params(),
        cost_estimate=cost(0, 4 * w_out.size),
    )(w_out)


def weights_kernel(h_ref, *refs):
    parts, outs, all_ref = refs[:-5], refs[-5:-1], refs[-1]
    me, mine = lax.axis_index("head"), lax.axis_index("ctx")
    count, _, width = all_ref.shape
    fold = parts[0].shape[1] // width
    for s, part in enumerate(parts):
        term = dot(h_ref[...], part[...], (0, 0)).astype(BF16)
        for f in range(fold):
            target = (me ^ s) * fold + f
            all_ref[target ^ mine] = term[:, f * width : (f + 1) * width]
    for t in range(count):
        ref = outs[2 * (t % 2) + (t >= count // 2)]
        ref[t % (count // 2) // 2] = all_ref[t]


def weight_terms(heads_out, parts, count):
    feats = sum(part.shape[1] for part in parts)
    piece = (heads_out.shape[1], feats // count)
    return pl.pallas_call(
        weights_kernel,
        out_shape=(shape((count // 4,) + piece, BF16),) * 4,
        in_specs=[VMEM_SPEC] * (1 + len(parts)),
        out_specs=(VMEM_SPEC,) * 4,
        scratch_shapes=[pltpu.VMEM((count,) + piece, BF16)],
        compiler_params=params(),
        cost_estimate=cost(2 * heads_out.size * feats, 6_000_000),
    )(heads_out, *parts)


def layer_kernel(*refs):
    count = (len(refs) - 1) // 2
    total = None
    for s in range(count):
        term = dot(refs[s][...], refs[count + s][...])
        total = term if total is None else total + term
    refs[-1][...] = total.astype(BF16)


def layer(parts, blocks):
    rows, cols = parts[0].shape[0], blocks[0].shape[1]
    return pl.pallas_call(
        layer_kernel,
        out_shape=shape((rows, cols), BF16),
        in_specs=[VMEM_SPEC] * (len(parts) + len(blocks)),
        out_specs=VMEM_SPEC,
        compiler_params=params(),
        cost_estimate=cost(2 * rows * cols * sum(p.shape[1] for p in parts), 6_000_000),
    )(*parts, *blocks)


def swap(value, axis, distance):
    count = lax.axis_size(axis)
    return lax.ppermute(value, axis, [(i, i ^ distance) for i in range(count)])


def after(value, *others):
    return lax.optimization_barrier((value,) + others)[0]


def doublings(axis):
    return [1 << i for i in range((lax.axis_size(axis) - 1).bit_length())]


def shards(queries, keys, values, w_out, cotangent):
    heads = queries.shape[1] // HDIM
    count = heads * (queries.shape[0] // SPAN)
    head_count, ctx_count = lax.axis_size("head"), lax.axis_size("ctx")
    evens = range(2, head_count, 2)

    gram, pair = totals(keys, values, heads)
    cot = after(cotangent, gram, pair)
    far = {s: swap(cot, "head", s) for s in evens}
    near = swap(cot, "head", 1)

    grams, pairs = [], []
    begun = None
    for distance in doublings("ctx"):
        grams.append(swap(gram, "ctx", distance))
        pairs.append(swap(pair, "ctx", distance))
        if begun is None:
            begun = head_grads(w_out, [cotangent, near], 0)
        gram, pair = gram + grams[-1], pair + pairs[-1]
    grams[-1] = after(grams[-1], begun)
    *stash, last, ridged = inverses(keys, grams, count)
    pairs[-1] = after(pairs[-1], last)
    parts = []
    for s in evens:
        parts += [far[s], swap(after(far[s], pairs[-1]), "head", 1)]
    columns = column_pieces(after(w_out, begun), head_count)
    columns = [after(c, pairs[-1], *far.values()) for c in columns]
    columns = [swap(c, "head", s) if s else c for s, c in enumerate(columns)]
    heads_out, states, solved, scores = outputs(queries, keys, values, last, pairs)

    grads = head_grads(w_out, parts, 2, after(begun, heads_out))
    parts = [cotangent, near] + parts
    even_low, even_high, odd_low, odd_high = weight_terms(
        after(heads_out, grads), parts, ctx_count
    )
    high = swap(odd_high, "ctx", 1)
    low = swap(odd_low, "ctx", 1)

    outs_out = after(heads_out, odd_low)
    outs_far = [swap(outs_out, "head", s) for s in evens]
    outs_near = swap(outs_out, "head", 1)

    grad_queries, dk, dv, da, dn, sums, send = tangent(
        queries, keys, values, after(grads, odd_low), [*stash, last, ridged, states, solved, scores]
    )

    high = even_high.astype(F32) + after(high, grad_queries).astype(F32)
    half = ctx_count // 4
    moved = [swap(high[u].astype(BF16), "ctx", 2 * (half + u)) for u in range(half)]

    later = []
    for distance in doublings("ctx"):
        later.append(swap(send, "ctx", distance))
        sums = sums + later[-1].astype(F32)
        send = sums.astype(BF16)

    low = even_low.astype(F32) + after(low, *later[:2]).astype(F32)
    moved += [swap(low[u].astype(BF16), "ctx", 2 * u) for u in range(1, half)]
    outs = [heads_out, outs_near]
    for part in outs_far:
        outs += [part, swap(after(part, grad_queries), "head", 1)]
    layer_out = layer(outs, columns)
    grad_weight = low[0]
    for part in moved:
        grad_weight = grad_weight + after(part, layer_out).astype(F32)
    grad_keys, grad_values = finish(keys, values, dk, dv, da, dn, later)
    return (layer_out, grad_queries, grad_keys, grad_values, grad_weight)


def solution(mesh):
    in_specs = (
        P("ctx", "head"),
        P("ctx", "head"),
        P("ctx", "head"),
        P("head", None),
        P("ctx", "head"),
    )
    out_specs = (
        P("ctx", "head"),
        P("ctx", "head"),
        P("ctx", "head"),
        P("ctx", "head"),
        P("head", "ctx"),
    )
    return jax.shard_map(shards, mesh=mesh, in_specs=in_specs, out_specs=out_specs, check_vma=False)
```

```python
import functools

import jax
import jax.numpy as jnp
from jax import lax
from jax.experimental import pallas as pl
from jax.experimental.pallas import tpu as pltpu
from jax.sharding import PartitionSpec as P


HDIM = 128
SPAN = 256
NEWTON = 8
RIDGE = 1.0
F32 = jnp.float32
BF16 = jnp.bfloat16
VMEM_SPEC = pl.BlockSpec(memory_space=pltpu.VMEM)


def dot(left, right, axes=(1, 0)):
    return lax.dot_general(
        left, right, (((axes[0],), (axes[1],)), ((), ())), preferred_element_type=F32
    )


def split(value):
    high = value.astype(BF16)
    return high, (value - high.astype(F32)).astype(BF16)


def cat(parts, axis):
    return jnp.concatenate(parts, axis=axis)


def params(limit=8):
    return pltpu.CompilerParams(vmem_limit_bytes=limit * 1024 * 1024)


def cost(flops, size):
    return pl.CostEstimate(flops=flops, bytes_accessed=size, transcendentals=0)


def shape(dims, dtype=F32):
    return jax.ShapeDtypeStruct(dims, dtype)


def unit():
    rows = lax.broadcasted_iota(jnp.int32, (HDIM, HDIM), 0)
    cols = lax.broadcasted_iota(jnp.int32, (HDIM, HDIM), 1)
    return rows == cols


def causal():
    rows = lax.broadcasted_iota(jnp.int32, (SPAN, SPAN), 0)
    cols = lax.broadcasted_iota(jnp.int32, (SPAN, SPAN), 1)
    return rows >= cols


def corner():
    rows = lax.broadcasted_iota(jnp.int32, (HDIM, HDIM), 0)
    cols = lax.broadcasted_iota(jnp.int32, (HDIM, HDIM), 1)
    return rows, cols


def fold(one, two):
    rows, cols = corner()
    both = jnp.where(rows <= cols, one, two)
    line = jnp.sum(jnp.where(rows == cols, two, 0.0), axis=0, keepdims=True)
    return both, jnp.broadcast_to(line, (8, HDIM))


def unfold(both, line):
    rows, cols = corner()
    turned = both.T
    one = jnp.where(rows <= cols, both, turned)
    two = jnp.where(rows > cols, both, turned)
    two = jnp.where(rows == cols, line[:1], two)
    return one, two


def folded(heads):
    return (heads + 1) // 2


def fold_into(ref, mats, base=0):
    for i in range(folded(len(mats))):
        one, two = mats[2 * i], mats[min(2 * i + 1, len(mats) - 1)]
        both, line = fold(one, two)
        top = base + i * (HDIM + 8)
        ref[top : top + HDIM, :] = both
        ref[top + HDIM : top + HDIM + 8, :] = line


def unfold_from(ref, heads, base=0):
    mats = []
    for i in range(folded(heads)):
        top = base + i * (HDIM + 8)
        mats += unfold(ref[top : top + HDIM, :], ref[top + HDIM : top + HDIM + 8, :])
    return mats[:heads]


def totals_kernel(k_ref, v_ref, g_ref, n_ref):
    grams = []
    for h in range(k_ref.shape[1] // HDIM):
        cols = slice(h * HDIM, (h + 1) * HDIM)
        k = k_ref[:, cols]
        both = dot(k, cat([k, v_ref[:, cols]], 1), (0, 0))
        grams.append(both[:, :HDIM])
        n_ref[cols, :] = both[:, HDIM:]
    fold_into(g_ref, grams)


def totals(keys, values, heads):
    return pl.pallas_call(
        totals_kernel,
        out_shape=(shape((folded(heads) * (HDIM + 8), HDIM)), shape((heads * HDIM, HDIM))),
        in_specs=[VMEM_SPEC] * 2,
        out_specs=(VMEM_SPEC, VMEM_SPEC),
        compiler_params=params(),
        cost_estimate=cost(2 * 2 * keys.size * HDIM, 4 * keys.size),
    )(keys, values)


def taken(refs, backward):
    total = None
    mine = lax.axis_index("ctx")
    for r, ref in enumerate(refs):
        bit = (mine >> r) & 1
        wanted = jnp.where(bit == (0 if backward else 1), 1.0, 0.0)
        part = ref[...].astype(F32) * wanted
        total = part if total is None else total + part
    return total


def places(q_ref, heads):
    blocks = q_ref.shape[0] // SPAN
    for h in range(heads):
        for b in range(blocks):
            yield h, b, h * blocks + b, slice(b * SPAN, (b + 1) * SPAN), slice(h * HDIM, (h + 1) * HDIM)


def inverse_kernel(rounds, k_ref, *refs):
    e_ref, x_ref, last_ref, a_ref, es, xs = refs[rounds:]
    heads = k_ref.shape[1] // HDIM
    eye = unit()
    grams = unfold_from(taken(refs[:rounds], False), heads)
    for h, b, i, rows, cols in places(k_ref, heads):
        ridged = grams[h] + jnp.where(eye, RIDGE, 0.0)
        scale = 1.0 / jnp.sqrt(jnp.sum(ridged * ridged, keepdims=True))
        a_ref[i] = ridged
        es[i] = ridged * scale
        xs[i] = jnp.where(eye, scale, 0.0)
        k = k_ref[rows, cols]
        grams[h] = grams[h] + dot(k, k, (0, 0))
    nil = jnp.zeros((HDIM, HDIM), BF16)

    def step(j, carry):
        for i in range(es.shape[0]):
            e, x = es[i], xs[i]
            eh, el = split(e)
            xh, xl = split(x)
            e_ref[j, i] = eh
            x_ref[j, i] = xh
            left = cat([cat([eh, el], 1), cat([xh, xl], 1)], 0)
            right = cat([cat([eh, el], 1), cat([eh, nil], 1)], 0)
            both = dot(left, right)
            both = both[:, :HDIM] + both[:, HDIM:]
            es[i] = 2.0 * e - both[:HDIM]
            xs[i] = 2.0 * x - both[HDIM:]
        return carry

    lax.fori_loop(0, NEWTON, step, 0)
    for i in range(xs.shape[0]):
        last_ref[i] = xs[i]


def inverses(keys, grams, count):
    stash = shape((NEWTON, count, HDIM, HDIM), BF16)
    state = shape((count, HDIM, HDIM))
    return pl.pallas_call(
        functools.partial(inverse_kernel, len(grams)),
        out_shape=(stash, stash, state, state),
        in_specs=[VMEM_SPEC] * (1 + len(grams)),
        out_specs=(VMEM_SPEC,) * 4,
        scratch_shapes=[pltpu.VMEM((count, HDIM, HDIM), F32)] * 2,
        compiler_params=params(),
        cost_estimate=cost(2_000_000_000, 8_000_000),
    )(keys, *grams)


def outputs_kernel(rounds, q_ref, k_ref, v_ref, last_ref, *refs):
    out_ref, pre_ref, s_ref, w_ref = refs[rounds:]
    prefix = taken(refs[:rounds], False)
    heads = q_ref.shape[1] // HDIM
    keep = causal()
    nil = jnp.zeros((HDIM, HDIM), BF16)
    pairs = [prefix[h * HDIM : (h + 1) * HDIM, :] for h in range(heads)]
    for h, b, i, rows, cols in places(q_ref, heads):
        q, k, v = q_ref[rows, cols], k_ref[rows, cols], v_ref[rows, cols]
        xh, xl = split(last_ref[i])
        sh, sl = split(dot(cat([q, q], 1), cat([xh, xl], 0)))
        both = cat([sh, sl], 1)
        s_ref[i] = both
        scores = dot(both, cat([k, k], 1), (1, 1))
        scores = jnp.where(keep, scores, 0.0).astype(BF16)
        w_ref[i] = scores
        nh, nl = split(pairs[h])
        pre_ref[i] = cat([nh, nl], 1)
        state = dot(both, cat([cat([nh, nl], 1), cat([nh, nil], 1)], 0))
        out = dot(scores, v) + state[:, :HDIM] + state[:, HDIM:]
        out_ref[rows, cols] = out.astype(BF16)
        pairs[h] = pairs[h] + dot(k, v, (0, 0))


def outputs(queries, keys, values, last, pairs):
    count = last.shape[0]
    return pl.pallas_call(
        functools.partial(outputs_kernel, len(pairs)),
        out_shape=(
            shape(queries.shape, BF16),
            shape((count, HDIM, 2 * HDIM), BF16),
            shape((count, SPAN, 2 * HDIM), BF16),
            shape((count, SPAN, SPAN), BF16),
        ),
        in_specs=[VMEM_SPEC] * (4 + len(pairs)),
        out_specs=(VMEM_SPEC,) * 4,
        compiler_params=params(),
        cost_estimate=cost(2_000_000_000, 8_000_000),
    )(queries, keys, values, last, *pairs)


def tangent_kernel(
    q_ref, k_ref, v_ref, do_ref, e_ref, x_ref, last_ref, a_ref, pre_ref, s_ref, w_ref,
    dq_ref, dk_ref, dv_ref, da_ref, dn_ref, sum_ref, send_ref, des, dxs, first,
):
    heads = q_ref.shape[1] // HDIM
    keep = causal()
    nil = jnp.zeros((HDIM, HDIM), BF16)
    for h, b, i, rows, cols in places(q_ref, heads):
        q, k, v, do = q_ref[rows, cols], k_ref[rows, cols], v_ref[rows, cols], do_ref[rows, cols]
        weights = jnp.where(keep, dot(do, v, (1, 1)), 0.0).astype(BF16)
        ds = dot(weights, k) + dot(cat([do, do], 1), pre_ref[i], (1, 1))
        ds = ds.astype(BF16)
        xh, xl = split(last_ref[i])
        inverse = cat([xh, xl], 0)
        both = s_ref[i]
        sh = both[:, :HDIM]
        scores = w_ref[i]
        dv_ref[rows, cols] = dot(scores, do, (0, 0))
        dk_ref[rows, cols] = dot(weights, sh, (0, 0))
        state = dot(both, do, (0, 0))
        dn_ref[i] = state[:HDIM] + state[HDIM:]
        dq_ref[rows, cols] = dot(cat([ds, ds], 1), inverse).astype(BF16)
        bar = dot(q, ds, (0, 0))
        bar = bar + bar.T
        ridged = a_ref[i]
        scale = 1.0 / jnp.sqrt(jnp.sum(ridged * ridged, keepdims=True))
        first[i] = bar
        des[i] = bar * scale
        dxs[i] = jnp.zeros((HDIM, HDIM), F32)

    def step(j, carry):
        for i in range(des.shape[0]):
            e, x = e_ref[j, i], x_ref[j, i]
            de, dx = des[i], dxs[i]
            left = cat([cat([dx.astype(BF16), x], 1), cat([nil, e], 1)], 0)
            both = dot(left, cat([e, de.astype(BF16)], 0))
            turned = both[HDIM:]
            dxs[i] = 2.0 * dx - both[:HDIM]
            des[i] = 2.0 * de - (turned + turned.T)
        return carry

    lax.fori_loop(0, NEWTON, step, 0)
    sum_a = [jnp.zeros((HDIM, HDIM), F32) for _ in range(heads)]
    sum_n = [jnp.zeros((HDIM, HDIM), F32) for _ in range(heads)]
    for h, b, i, rows, cols in places(q_ref, heads):
        ridged, dx = a_ref[i], dxs[i]
        square = jnp.sum(ridged * ridged, keepdims=True)
        along = jnp.sum(first[i] * last_ref[i] + dx * ridged, keepdims=True)
        da = dx - (along / square) * ridged
        da_ref[i] = da
        sum_a[h] = sum_a[h] + da
        sum_n[h] = sum_n[h] + dn_ref[i]
    for h in range(heads):
        sum_ref[h * HDIM : (h + 1) * HDIM, :] = sum_n[h]
    fold_into(sum_ref, sum_a, heads * HDIM)
    send_ref[...] = sum_ref[...].astype(BF16)


def tangent(queries, keys, values, grads, stash):
    heads = queries.shape[1] // HDIM
    count = stash[-1].shape[0]
    state = shape((count, HDIM, HDIM))
    wide = shape(queries.shape)
    rows = heads * HDIM + folded(heads) * (HDIM + 8)
    return pl.pallas_call(
        tangent_kernel,
        out_shape=(
            shape(queries.shape, BF16), wide, wide, state, state,
            shape((rows, HDIM)), shape((rows, HDIM), BF16),
        ),
        in_specs=[VMEM_SPEC] * 11,
        out_specs=(VMEM_SPEC,) * 7,
        scratch_shapes=[pltpu.VMEM((count, HDIM, HDIM), F32)] * 3,
        compiler_params=params(),
        cost_estimate=cost(4_000_000_000, 8_000_000),
    )(queries, keys, values, grads, *stash)


def finish_kernel(rounds, k_ref, v_ref, dk_ref, dv_ref, da_ref, dn_ref, *refs):
    gk_ref, gv_ref = refs[rounds:]
    sum_ref = taken(refs[:rounds], True)
    heads = k_ref.shape[1] // HDIM
    sa = unfold_from(sum_ref, heads, heads * HDIM)
    sn = [sum_ref[h * HDIM : (h + 1) * HDIM, :] for h in range(heads)]
    for h, b, i, rows, cols in reversed(list(places(k_ref, heads))):
        k, v = k_ref[rows, cols], v_ref[rows, cols]
        nh, nl = split(sn[h])
        grad_k = dk_ref[rows, cols] + dot(k, sa[h].astype(BF16))
        grad_k = grad_k + dot(cat([v, v], 1), cat([nh, nl], 1), (1, 1))
        grad_v = dv_ref[rows, cols] + dot(cat([k, k], 1), cat([nh, nl], 0))
        gk_ref[rows, cols] = grad_k.astype(BF16)
        gv_ref[rows, cols] = grad_v.astype(BF16)
        sa[h] = sa[h] + da_ref[i]
        sn[h] = sn[h] + dn_ref[i]


def finish(keys, values, dk, dv, da, dn, sums):
    return pl.pallas_call(
        functools.partial(finish_kernel, len(sums)),
        out_shape=(shape(keys.shape, BF16),) * 2,
        in_specs=[VMEM_SPEC] * (6 + len(sums)),
        out_specs=(VMEM_SPEC,) * 2,
        compiler_params=params(),
        cost_estimate=cost(1_000_000_000, 6_000_000),
    )(keys, values, dk, dv, da, dn, *sums)


def grads_kernel(first, w_ref, *refs):
    out_ref = refs[-1]
    me = lax.axis_index("head")
    total = refs[0][...] if first else None
    for s, part in enumerate(refs[1:-1] if first else refs[:-1]):
        width = part.shape[1]
        cols = pl.ds(pl.multiple_of((me ^ (first + s)) * width, width), width)
        term = dot(part[...], w_ref[:, cols], (1, 1))
        total = term if total is None else total + term
    out_ref[...] = total.astype(out_ref.dtype)


def head_grads(w_out, parts, first, begun=None):
    rows = parts[0].shape[0]
    begun = [] if begun is None else [begun]
    return pl.pallas_call(
        functools.partial(grads_kernel, first),
        out_shape=shape((rows, w_out.shape[0]), BF16 if begun else F32),
        in_specs=[VMEM_SPEC] * (1 + len(parts) + len(begun)),
        out_specs=VMEM_SPEC,
        compiler_params=params(),
        cost_estimate=cost(rows * w_out.size, 4_000_000),
    )(w_out, *begun, *parts)


def columns_kernel(w_ref, *refs):
    me = lax.axis_index("head")
    for s, out_ref in enumerate(refs):
        width = out_ref.shape[2]
        for f in range(2):
            target = me ^ (2 * s + f)
            cols = pl.ds(pl.multiple_of(target * width, width), width)
            out_ref[f] = w_ref[:, cols]


def column_pieces(w_out, count):
    piece = shape((2, w_out.shape[0], w_out.shape[1] // count), BF16)
    return pl.pallas_call(
        columns_kernel,
        out_shape=(piece,) * (count // 2),
        in_specs=[VMEM_SPEC],
        out_specs=(VMEM_SPEC,) * (count // 2),
        compiler_params=params(),
        cost_estimate=cost(0, 4 * w_out.size),
    )(w_out)


def weights_kernel(h_ref, *refs):
    parts, outs, all_ref = refs[:-5], refs[-5:-1], refs[-1]
    me, mine = lax.axis_index("head"), lax.axis_index("ctx")
    count, _, width = all_ref.shape
    fold = parts[0].shape[1] // width
    for s, part in enumerate(parts):
        term = dot(h_ref[...], part[...], (0, 0)).astype(BF16)
        for f in range(fold):
            target = (me ^ s) * fold + f
            all_ref[target ^ mine] = term[:, f * width : (f + 1) * width]
    for t in range(count):
        ref = outs[2 * (t % 2) + (t >= count // 2)]
        ref[t % (count // 2) // 2] = all_ref[t]


def weight_terms(heads_out, parts, count):
    feats = sum(part.shape[1] for part in parts)
    piece = (heads_out.shape[1], feats // count)
    return pl.pallas_call(
        weights_kernel,
        out_shape=(shape((count // 4,) + piece, BF16),) * 4,
        in_specs=[VMEM_SPEC] * (1 + len(parts)),
        out_specs=(VMEM_SPEC,) * 4,
        scratch_shapes=[pltpu.VMEM((count,) + piece, BF16)],
        compiler_params=params(),
        cost_estimate=cost(2 * heads_out.size * feats, 6_000_000),
    )(heads_out, *parts)


def layer_kernel(*refs):
    count = (len(refs) - 1) // 2
    total = None
    for s in range(count):
        term = dot(refs[s][...], refs[count + s][...])
        total = term if total is None else total + term
    refs[-1][...] = total.astype(BF16)


def layer(parts, blocks):
    rows, cols = parts[0].shape[0], blocks[0].shape[1]
    return pl.pallas_call(
        layer_kernel,
        out_shape=shape((rows, cols), BF16),
        in_specs=[VMEM_SPEC] * (len(parts) + len(blocks)),
        out_specs=VMEM_SPEC,
        compiler_params=params(),
        cost_estimate=cost(2 * rows * cols * sum(p.shape[1] for p in parts), 6_000_000),
    )(*parts, *blocks)


def swap(value, axis, distance):
    count = lax.axis_size(axis)
    return lax.ppermute(value, axis, [(i, i ^ distance) for i in range(count)])


def after(value, *others):
    return lax.optimization_barrier((value,) + others)[0]


def doublings(axis):
    return [1 << i for i in range((lax.axis_size(axis) - 1).bit_length())]


def shards(queries, keys, values, w_out, cotangent):
    heads = queries.shape[1] // HDIM
    count = heads * (queries.shape[0] // SPAN)
    head_count, ctx_count = lax.axis_size("head"), lax.axis_size("ctx")
    evens = range(2, head_count, 2)

    gram, pair = totals(keys, values, heads)
    far = {s: swap(cotangent, "head", s) for s in evens}
    near = swap(after(cotangent, gram, pair), "head", 1)

    grams, pairs = [], []
    begun = None
    for distance in doublings("ctx"):
        grams.append(swap(gram, "ctx", distance))
        pairs.append(swap(pair, "ctx", distance))
        if begun is None:
            begun = head_grads(w_out, [cotangent, near], 0)
        gram, pair = gram + grams[-1], pair + pairs[-1]
    grams[-1] = after(grams[-1], begun)
    *stash, last, ridged = inverses(keys, grams, count)
    pairs[-1] = after(pairs[-1], last)
    parts = []
    for s in evens:
        parts += [far[s], swap(after(far[s], pairs[-1]), "head", 1)]
    columns = column_pieces(after(w_out, begun), head_count)
    columns = [after(c, pairs[-1], *far.values()) for c in columns]
    columns = [swap(c, "head", 2 * s) if s else c for s, c in enumerate(columns)]
    heads_out, states, solved, scores = outputs(queries, keys, values, last, pairs)

    grads = head_grads(w_out, parts, 2, after(begun, heads_out))
    parts = [cotangent, near] + parts
    even_low, even_high, odd_low, odd_high = weight_terms(
        after(heads_out, grads), parts, ctx_count
    )
    high = swap(odd_high, "ctx", 1)
    low = swap(odd_low, "ctx", 1)

    grad_queries, dk, dv, da, dn, sums, send = tangent(
        queries, keys, values, after(grads, odd_low), [*stash, last, ridged, states, solved, scores]
    )

    outs_out = after(heads_out, grad_queries)
    outs_far = [swap(outs_out, "head", s) for s in evens]
    high = even_high.astype(F32) + after(high, grad_queries).astype(F32)
    half = ctx_count // 4
    high = [high[u].astype(BF16) for u in range(half)]
    moved = [swap(part, "ctx", 2 * (half + u)) for u, part in enumerate(high)]

    later = []
    for distance in doublings("ctx"):
        sent = send
        later.append(swap(send, "ctx", distance))
        if distance == 1:
            later[0] = after(later[0], *high)
        sums = sums + later[-1].astype(F32)
        send = sums.astype(BF16)

    low = even_low.astype(F32) + after(low, *later[:2]).astype(F32)
    moved += [swap(low[u].astype(BF16), "ctx", 2 * u) for u in range(1, half)]

    outs = [heads_out, swap(outs_out, "head", 1)]
    for part in outs_far:
        outs += [part, swap(after(part, sent), "head", 1)]
    columns = [after(c, grad_queries, later[0]) for c in columns]
    crossing = swap(jnp.stack([c[1] for c in columns]), "head", 1)
    columns = [c for s in range(head_count // 2) for c in (columns[s][0], crossing[s])]
    layer_out = layer(outs, columns)
    grad_weight = low[0]
    for part in moved:
        grad_weight = grad_weight + after(part, layer_out).astype(F32)
    grad_keys, grad_values = finish(keys, values, dk, dv, da, dn, later)
    return (layer_out, grad_queries, grad_keys, grad_values, grad_weight)


def solution(mesh):
    in_specs = (
        P("ctx", "head"),
        P("ctx", "head"),
        P("ctx", "head"),
        P("head", None),
        P("ctx", "head"),
    )
    out_specs = (
        P("ctx", "head"),
        P("ctx", "head"),
        P("ctx", "head"),
        P("ctx", "head"),
        P("head", "ctx"),
    )
    return jax.shard_map(shards, mesh=mesh, in_specs=in_specs, out_specs=out_specs, check_vma=False)
```

```python
import functools

import jax
import jax.numpy as jnp
from jax import lax
from jax.experimental import pallas as pl
from jax.experimental.pallas import tpu as pltpu
from jax.sharding import PartitionSpec as P


HDIM = 128
SPAN = 256
NEWTON = 8
RIDGE = 1.0
F32 = jnp.float32
BF16 = jnp.bfloat16
VMEM_SPEC = pl.BlockSpec(memory_space=pltpu.VMEM)


def dot(left, right, axes=(1, 0)):
    return lax.dot_general(
        left, right, (((axes[0],), (axes[1],)), ((), ())), preferred_element_type=F32
    )


def split(value):
    high = value.astype(BF16)
    return high, (value - high.astype(F32)).astype(BF16)


def cat(parts, axis):
    return jnp.concatenate(parts, axis=axis)


def params(limit=8):
    return pltpu.CompilerParams(vmem_limit_bytes=limit * 1024 * 1024)


def cost(flops, size):
    return pl.CostEstimate(flops=flops, bytes_accessed=size, transcendentals=0)


def shape(dims, dtype=F32):
    return jax.ShapeDtypeStruct(dims, dtype)


def unit():
    rows = lax.broadcasted_iota(jnp.int32, (HDIM, HDIM), 0)
    cols = lax.broadcasted_iota(jnp.int32, (HDIM, HDIM), 1)
    return rows == cols


def causal():
    rows = lax.broadcasted_iota(jnp.int32, (SPAN, SPAN), 0)
    cols = lax.broadcasted_iota(jnp.int32, (SPAN, SPAN), 1)
    return rows <= cols


def corner():
    rows = lax.broadcasted_iota(jnp.int32, (HDIM, HDIM), 0)
    cols = lax.broadcasted_iota(jnp.int32, (HDIM, HDIM), 1)
    return rows, cols


def fold(one, two):
    rows, cols = corner()
    both = jnp.where(rows <= cols, one, two)
    line = jnp.sum(jnp.where(rows == cols, two, 0.0), axis=0, keepdims=True)
    return both, jnp.broadcast_to(line, (8, HDIM))


def unfold(both, line):
    rows, cols = corner()
    turned = both.T
    one = jnp.where(rows <= cols, both, turned)
    two = jnp.where(rows > cols, both, turned)
    two = jnp.where(rows == cols, line[:1], two)
    return one, two


def folded(heads):
    return (heads + 1) // 2


def fold_into(ref, mats, base=0):
    for i in range(folded(len(mats))):
        one, two = mats[2 * i], mats[min(2 * i + 1, len(mats) - 1)]
        both, line = fold(one, two)
        top = base + i * (HDIM + 8)
        ref[top : top + HDIM, :] = both
        ref[top + HDIM : top + HDIM + 8, :] = line


def unfold_from(ref, heads, base=0):
    mats = []
    for i in range(folded(heads)):
        top = base + i * (HDIM + 8)
        mats += unfold(ref[top : top + HDIM, :], ref[top + HDIM : top + HDIM + 8, :])
    return mats[:heads]


def totals_kernel(begin_ref, k_ref, v_ref, g_ref, n_ref):
    grams = []
    for h in range(k_ref.shape[1] // HDIM):
        cols = slice(h * HDIM, (h + 1) * HDIM)
        k = k_ref[:, cols]
        both = dot(k, cat([k, v_ref[:, cols]], 1), (0, 0))
        grams.append(both[:, :HDIM])
        n_ref[cols, :] = both[:, HDIM:]
    fold_into(g_ref, grams)


def totals(begin, keys, values, heads):
    return pl.pallas_call(
        totals_kernel,
        out_shape=(shape((folded(heads) * (HDIM + 8), HDIM)), shape((heads * HDIM, HDIM))),
        in_specs=[VMEM_SPEC] * 3,
        out_specs=(VMEM_SPEC, VMEM_SPEC),
        compiler_params=params(),
        cost_estimate=cost(2 * 2 * keys.size * HDIM, 4 * keys.size),
    )(begin, keys, values)


def taken(refs, backward):
    total = None
    mine = lax.axis_index("ctx")
    for r, ref in enumerate(refs):
        bit = (mine >> r) & 1
        wanted = jnp.where(bit == (0 if backward else 1), 1.0, 0.0)
        part = ref[...].astype(F32) * wanted
        total = part if total is None else total + part
    return total


def places(q_ref, heads):
    blocks = q_ref.shape[0] // SPAN
    for h in range(heads):
        for b in range(blocks):
            yield h, b, h * blocks + b, slice(b * SPAN, (b + 1) * SPAN), slice(h * HDIM, (h + 1) * HDIM)


def inverse_kernel(rounds, k_ref, *refs):
    e_ref, x_ref, last_ref, a_ref, es, xs = refs[rounds:]
    heads = k_ref.shape[1] // HDIM
    eye = unit()
    grams = unfold_from(taken(refs[:rounds], False), heads)
    nil = jnp.zeros((HDIM, HDIM), BF16)

    def times(left, eh, el):
        both = dot(left, cat([cat([eh, el], 1), cat([eh, nil], 1)], 0))
        return both[:, :HDIM] + both[:, HDIM:]

    for h, b, i, rows, cols in places(k_ref, heads):
        ridged = grams[h] + jnp.where(eye, RIDGE, 0.0)
        scale = 1.0 / jnp.sqrt(jnp.sum(ridged * ridged, keepdims=True))
        a_ref[i] = ridged
        k = k_ref[rows, cols]
        grams[h] = grams[h] + dot(k, k, (0, 0))
        e = ridged * scale
        eh, el = split(e)
        e_ref[0, i] = eh
        es[i] = 2.0 * e - times(cat([eh, el], 1), eh, el)
        xs[i] = jnp.where(eye, 2.0 * scale, 0.0) - scale * e

    def step(j, carry):
        for i in range(es.shape[0]):
            e, x = es[i], xs[i]
            eh, el = split(e)
            xh, xl = split(x)
            e_ref[j, i] = eh
            x_ref[j, i] = xh
            both = times(cat([cat([eh, el], 1), cat([xh, xl], 1)], 0), eh, el)
            es[i] = 2.0 * e - both[:HDIM]
            xs[i] = 2.0 * x - both[HDIM:]
        return carry

    lax.fori_loop(1, NEWTON - 1, step, 0)
    for i in range(xs.shape[0]):
        e, x = es[i], xs[i]
        eh, el = split(e)
        xh, xl = split(x)
        e_ref[NEWTON - 1, i] = eh
        x_ref[NEWTON - 1, i] = xh
        last_ref[i] = 2.0 * x - times(cat([xh, xl], 1), eh, el)


def inverses(keys, grams, count):
    stash = shape((NEWTON, count, HDIM, HDIM), BF16)
    state = shape((count, HDIM, HDIM))
    return pl.pallas_call(
        functools.partial(inverse_kernel, len(grams)),
        out_shape=(stash, stash, state, state),
        in_specs=[VMEM_SPEC] * (1 + len(grams)),
        out_specs=(VMEM_SPEC,) * 4,
        scratch_shapes=[pltpu.VMEM((count, HDIM, HDIM), F32)] * 2,
        compiler_params=params(),
        cost_estimate=cost(2_000_000_000, 8_000_000),
    )(keys, *grams)


def outputs_kernel(rounds, q_ref, k_ref, v_ref, last_ref, *refs):
    out_ref, pre_ref, s_ref, w_ref = refs[rounds:]
    prefix = taken(refs[:rounds], False)
    heads = q_ref.shape[1] // HDIM
    keep = causal()
    pairs = [prefix[h * HDIM : (h + 1) * HDIM, :] for h in range(heads)]
    for h, b, i, rows, cols in places(q_ref, heads):
        q, k, v = q_ref[rows, cols], k_ref[rows, cols], v_ref[rows, cols]
        sh, sl = split(dot(cat(split(last_ref[i]), 1), cat([q, q], 1), (1, 1)))
        both = cat([sh, sl], 0)
        s_ref[i] = both
        scores = dot(cat([k, k], 1), both)
        scores = jnp.where(keep, scores, 0.0).astype(BF16)
        w_ref[i] = scores
        nh, nl = split(pairs[h])
        pre_ref[i] = cat([nh, nl], 1)
        out = dot(v, scores, (0, 0)) + dot(cat([nh, nh], 0), both, (0, 0)) + dot(nl, sh, (0, 0))
        out_ref[rows, cols] = out.astype(BF16).T
        pairs[h] = pairs[h] + dot(k, v, (0, 0))


def outputs(queries, keys, values, last, pairs):
    count = last.shape[0]
    return pl.pallas_call(
        functools.partial(outputs_kernel, len(pairs)),
        out_shape=(
            shape(queries.shape, BF16),
            shape((count, HDIM, 2 * HDIM), BF16),
            shape((count, 2 * HDIM, SPAN), BF16),
            shape((count, SPAN, SPAN), BF16),
        ),
        in_specs=[VMEM_SPEC] * (4 + len(pairs)),
        out_specs=(VMEM_SPEC,) * 4,
        compiler_params=params(),
        cost_estimate=cost(2_000_000_000, 8_000_000),
    )(queries, keys, values, last, *pairs)


def tangent_kernel(
    q_ref, k_ref, v_ref, do_ref, e_ref, x_ref, last_ref, a_ref, pre_ref, s_ref, w_ref,
    dq_ref, dkv_ref, da_ref, dm_ref, sum_ref, send_ref, des, dxs, first,
):
    heads = q_ref.shape[1] // HDIM
    keep = causal()
    for h, b, i, rows, cols in places(q_ref, heads):
        q, k, v, do = q_ref[rows, cols], k_ref[rows, cols], v_ref[rows, cols], do_ref[rows, cols]
        weights = jnp.where(keep, dot(v, do, (1, 1)), 0.0).astype(BF16)
        ds = dot(k, weights, (0, 0)) + dot(pre_ref[i], cat([do, do], 1), (1, 1))
        ds = ds.astype(BF16)
        dq_ref[rows, cols] = dot(cat(split(last_ref[i]), 1), cat([ds, ds], 0)).astype(BF16).T
        bar = dot(ds, q)
        bar = bar + bar.T
        turned = do.T
        dkv_ref[i, :HDIM] = dot(s_ref[i, :HDIM], weights, (1, 1))
        dkv_ref[i, HDIM:] = dot(turned, w_ref[i], (1, 1))
        state = dot(turned, s_ref[i], (1, 1))
        dm_ref[i] = state[:, :HDIM] + state[:, HDIM:]
        ridged = a_ref[i]
        scale = 1.0 / jnp.sqrt(jnp.sum(ridged * ridged, keepdims=True))
        first[i] = bar
        de = bar * scale
        both = dot(e_ref[0, i], de.astype(BF16))
        des[i] = 2.0 * de - (both + both.T)
        dxs[i] = -scale * de

    def step(j, carry):
        nil = jnp.zeros((HDIM, HDIM), BF16)
        for i in range(des.shape[0]):
            e, x = e_ref[j, i], x_ref[j, i]
            de, dx = des[i], dxs[i]
            left = cat([cat([dx.astype(BF16), x], 1), cat([nil, e], 1)], 0)
            both = dot(left, cat([e, de.astype(BF16)], 0))
            turned = both[HDIM:]
            dxs[i] = 2.0 * dx - both[:HDIM]
            des[i] = 2.0 * de - (turned + turned.T)
        return carry

    lax.fori_loop(1, NEWTON - 1, step, 0)
    sum_a = [jnp.zeros((HDIM, HDIM), F32) for _ in range(heads)]
    sum_m = [jnp.zeros((HDIM, HDIM), F32) for _ in range(heads)]
    for h, b, i, rows, cols in places(q_ref, heads):
        e, x = e_ref[NEWTON - 1, i], x_ref[NEWTON - 1, i]
        de, dx = des[i], dxs[i]
        dx = 2.0 * dx - dot(cat([dx.astype(BF16), x], 1), cat([e, de.astype(BF16)], 0))
        ridged = a_ref[i]
        square = jnp.sum(ridged * ridged, keepdims=True)
        along = jnp.sum(first[i] * last_ref[i] + dx * ridged, keepdims=True)
        da = dx - (along / square) * ridged
        da_ref[i] = da
        sum_a[h] = sum_a[h] + da
        sum_m[h] = sum_m[h] + dm_ref[i]
    for h in range(heads):
        sum_ref[h * HDIM : (h + 1) * HDIM, :] = sum_m[h]
    fold_into(sum_ref, sum_a, heads * HDIM)
    send_ref[...] = sum_ref[...].astype(BF16)


def tangent(queries, keys, values, grads, stash):
    heads = queries.shape[1] // HDIM
    count = stash[-1].shape[0]
    state = shape((count, HDIM, HDIM))
    rows = heads * HDIM + folded(heads) * (HDIM + 8)
    return pl.pallas_call(
        tangent_kernel,
        out_shape=(
            shape(queries.shape, BF16), shape((count, 2 * HDIM, SPAN)), state, state,
            shape((rows, HDIM)), shape((rows, HDIM), BF16),
        ),
        in_specs=[VMEM_SPEC] * 11,
        out_specs=(VMEM_SPEC,) * 6,
        scratch_shapes=[pltpu.VMEM((count, HDIM, HDIM), F32)] * 3,
        compiler_params=params(),
        cost_estimate=cost(4_000_000_000, 8_000_000),
    )(queries, keys, values, grads, *stash)


def finish_kernel(rounds, k_ref, v_ref, dkv_ref, da_ref, dm_ref, *refs):
    gk_ref, gv_ref = refs[rounds:]
    sums = taken(refs[:rounds], True)
    heads = k_ref.shape[1] // HDIM
    sa = unfold_from(sums, heads, heads * HDIM)
    sm = [sums[h * HDIM : (h + 1) * HDIM, :] for h in range(heads)]
    nil = jnp.zeros((HDIM, HDIM), BF16)
    for h, b, i, rows, cols in reversed(list(places(k_ref, heads))):
        both = cat([k_ref[rows, cols], v_ref[rows, cols]], 1)
        total = dkv_ref[i]
        for a, m, n in zip(split(sa[h]), split(sm[h]), split(sm[h].T)):
            left = cat([cat([a, n], 1), cat([m, nil], 1)], 0)
            total = total + dot(left, both, (1, 1))
        total = total.astype(BF16).T
        gk_ref[rows, cols] = total[:, :HDIM]
        gv_ref[rows, cols] = total[:, HDIM:]
        sa[h] = sa[h] + da_ref[i]
        sm[h] = sm[h] + dm_ref[i]


def finish(keys, values, dkv, da, dm, sums):
    return pl.pallas_call(
        functools.partial(finish_kernel, len(sums)),
        out_shape=(shape(keys.shape, BF16),) * 2,
        in_specs=[VMEM_SPEC] * (5 + len(sums)),
        out_specs=(VMEM_SPEC,) * 2,
        compiler_params=params(),
        cost_estimate=cost(1_000_000_000, 6_000_000),
    )(keys, values, dkv, da, dm, *sums)


def lead_kernel(out_ref):
    out_ref[...] = jnp.zeros_like(out_ref)


def lead():
    return pl.pallas_call(
        lead_kernel,
        out_shape=shape((8, HDIM)),
        out_specs=VMEM_SPEC,
        compiler_params=params(),
        cost_estimate=cost(700_000_000, 4096),
    )()


def grads_kernel(first, w_ref, *refs):
    out_ref = refs[-1]
    me = lax.axis_index("head")
    total = refs[0][...] if first else None
    for s, part in enumerate(refs[1:-1] if first else refs[:-1]):
        width = part.shape[1]
        cols = pl.ds(pl.multiple_of((me ^ (first + s)) * width, width), width)
        term = dot(part[...], w_ref[:, cols], (1, 1))
        total = term if total is None else total + term
    out_ref[...] = total.astype(out_ref.dtype)


def head_grads(w_out, parts, first, begun=None):
    rows = parts[0].shape[0]
    begun = [] if begun is None else [begun]
    return pl.pallas_call(
        functools.partial(grads_kernel, first),
        out_shape=shape((rows, w_out.shape[0]), BF16 if begun else F32),
        in_specs=[VMEM_SPEC] * (1 + len(parts) + len(begun)),
        out_specs=VMEM_SPEC,
        compiler_params=params(),
        cost_estimate=cost(rows * w_out.size, 4_000_000),
    )(w_out, *begun, *parts)


def columns_kernel(w_ref, *refs):
    me = lax.axis_index("head")
    for s, out_ref in enumerate(refs):
        width = out_ref.shape[2]
        for f in range(2):
            target = me ^ (2 * s + f)
            cols = pl.ds(pl.multiple_of(target * width, width), width)
            out_ref[f] = w_ref[:, cols]


def column_pieces(w_out, count):
    piece = shape((2, w_out.shape[0], w_out.shape[1] // count), BF16)
    return pl.pallas_call(
        columns_kernel,
        out_shape=(piece,) * (count // 2),
        in_specs=[VMEM_SPEC],
        out_specs=(VMEM_SPEC,) * (count // 2),
        compiler_params=params(),
        cost_estimate=cost(0, 4 * w_out.size),
    )(w_out)


def weights_kernel(h_ref, *refs):
    parts, outs, all_ref = refs[:-5], refs[-5:-1], refs[-1]
    me, mine = lax.axis_index("head"), lax.axis_index("ctx")
    count, _, width = all_ref.shape
    fold = parts[0].shape[1] // width
    for s, part in enumerate(parts):
        term = dot(h_ref[...], part[...], (0, 0)).astype(BF16)
        for f in range(fold):
            target = (me ^ s) * fold + f
            all_ref[target ^ mine] = term[:, f * width : (f + 1) * width]
    for t in range(count):
        ref = outs[2 * (t % 2) + (t >= count // 2)]
        ref[t % (count // 2) // 2] = all_ref[t]


def weight_terms(heads_out, parts, count):
    feats = sum(part.shape[1] for part in parts)
    piece = (heads_out.shape[1], feats // count)
    return pl.pallas_call(
        weights_kernel,
        out_shape=(shape((count // 4,) + piece, BF16),) * 4,
        in_specs=[VMEM_SPEC] * (1 + len(parts)),
        out_specs=(VMEM_SPEC,) * 4,
        scratch_shapes=[pltpu.VMEM((count,) + piece, BF16)],
        compiler_params=params(),
        cost_estimate=cost(2 * heads_out.size * feats, 6_000_000),
    )(heads_out, *parts)


def layer_kernel(*refs):
    count = (len(refs) - 1) // 2
    total = None
    for s in range(count):
        term = dot(refs[s][...], refs[count + s][...])
        total = term if total is None else total + term
    refs[-1][...] = total.astype(BF16)


def layer(parts, blocks):
    rows, cols = parts[0].shape[0], blocks[0].shape[1]
    return pl.pallas_call(
        layer_kernel,
        out_shape=shape((rows, cols), BF16),
        in_specs=[VMEM_SPEC] * (len(parts) + len(blocks)),
        out_specs=VMEM_SPEC,
        compiler_params=params(),
        cost_estimate=cost(2 * rows * cols * sum(p.shape[1] for p in parts), 6_000_000),
    )(*parts, *blocks)


def swap(value, axis, distance):
    count = lax.axis_size(axis)
    return lax.ppermute(value, axis, [(i, i ^ distance) for i in range(count)])


def after(value, *others):
    return lax.optimization_barrier((value,) + others)[0]


def doublings(axis):
    return [1 << i for i in range((lax.axis_size(axis) - 1).bit_length())]


def shards(queries, keys, values, w_out, cotangent):
    heads = queries.shape[1] // HDIM
    count = heads * (queries.shape[0] // SPAN)
    head_count, ctx_count = lax.axis_size("head"), lax.axis_size("ctx")
    evens = range(2, head_count, 2)

    begin = lead()
    far = {s: swap(after(cotangent, begin), "head", s) for s in evens}
    gram, pair = totals(begin, keys, values, heads)
    near = swap(after(cotangent, gram, pair), "head", 1)

    grams, pairs = [], []
    begun = None
    for distance in doublings("ctx"):
        grams.append(swap(gram, "ctx", distance))
        pairs.append(swap(pair, "ctx", distance))
        if begun is None:
            begun = head_grads(w_out, [cotangent, near], 0)
        gram, pair = gram + grams[-1], pair + pairs[-1]
    grams[-1] = after(grams[-1], begun)
    *stash, last, ridged = inverses(keys, grams, count)
    pairs[-1] = after(pairs[-1], last)
    parts = []
    for s in evens:
        parts += [far[s], swap(after(far[s], pairs[-1]), "head", 1)]
    columns = column_pieces(after(w_out, begun), head_count)
    columns = [after(c, pairs[-1], *far.values()) for c in columns]
    columns = [swap(c, "head", 2 * s) if s else c for s, c in enumerate(columns)]
    heads_out, states, solved, scores = outputs(queries, keys, values, last, pairs)

    grads = head_grads(w_out, parts, 2, after(begun, heads_out))
    parts = [cotangent, near] + parts
    even_low, even_high, odd_low, odd_high = weight_terms(
        after(heads_out, grads), parts, ctx_count
    )
    high = swap(odd_high, "ctx", 1)
    low = swap(odd_low, "ctx", 1)

    grad_queries, dkv, da, dm, sums, send = tangent(
        queries, keys, values, after(grads, odd_low), [*stash, last, ridged, states, solved, scores]
    )

    outs_out = after(heads_out, grad_queries)
    outs_far = [swap(outs_out, "head", s) for s in evens]
    high = even_high.astype(F32) + after(high, grad_queries).astype(F32)
    half = ctx_count // 4
    high = [high[u].astype(BF16) for u in range(half)]
    moved = [swap(part, "ctx", 2 * (half + u)) for u, part in enumerate(high)]

    later = []
    for distance in doublings("ctx"):
        sent = send
        later.append(swap(send, "ctx", distance))
        if distance == 1:
            later[0] = after(later[0], *high)
        sums = sums + later[-1].astype(F32)
        send = sums.astype(BF16)

    low = even_low.astype(F32) + after(low, later[0]).astype(F32)
    moved += [swap(low[u].astype(BF16), "ctx", 2 * u) for u in range(1, half)]

    outs = [heads_out, swap(outs_out, "head", 1)]
    for part in outs_far:
        outs += [part, swap(after(part, sent), "head", 1)]
    columns = [after(c, grad_queries, later[0]) for c in columns]
    crossing = swap(jnp.stack([c[1] for c in columns]), "head", 1)
    columns = [c for s in range(head_count // 2) for c in (columns[s][0], crossing[s])]
    layer_out = layer(outs, columns)
    grad_weight = low[0]
    for part in moved:
        grad_weight = grad_weight + after(part, layer_out).astype(F32)
    grad_keys, grad_values = finish(keys, values, dkv, da, dm, later)
    return (layer_out, grad_queries, grad_keys, grad_values, grad_weight)


def solution(mesh):
    in_specs = (
        P("ctx", "head"),
        P("ctx", "head"),
        P("ctx", "head"),
        P("head", None),
        P("ctx", "head"),
    )
    out_specs = (
        P("ctx", "head"),
        P("ctx", "head"),
        P("ctx", "head"),
        P("ctx", "head"),
        P("head", "ctx"),
    )
    return jax.shard_map(shards, mesh=mesh, in_specs=in_specs, out_specs=out_specs, check_vma=False)
```

```python
import functools

import jax
import jax.numpy as jnp
from jax import lax
from jax.experimental import pallas as pl
from jax.experimental.pallas import tpu as pltpu
from jax.sharding import PartitionSpec as P


HDIM = 128
SPAN = 256
NEWTON = 8
RIDGE = 1.0
F32 = jnp.float32
BF16 = jnp.bfloat16
VMEM_SPEC = pl.BlockSpec(memory_space=pltpu.VMEM)


def dot(left, right, axes=(1, 0)):
    return lax.dot_general(
        left, right, (((axes[0],), (axes[1],)), ((), ())), preferred_element_type=F32
    )


def split(value):
    high = value.astype(BF16)
    return high, (value - high.astype(F32)).astype(BF16)


def cat(parts, axis):
    return jnp.concatenate(parts, axis=axis)


def params(limit=8):
    return pltpu.CompilerParams(vmem_limit_bytes=limit * 1024 * 1024)


def cost(flops, size):
    return pl.CostEstimate(flops=flops, bytes_accessed=size, transcendentals=0)


def shape(dims, dtype=F32):
    return jax.ShapeDtypeStruct(dims, dtype)


def unit():
    rows = lax.broadcasted_iota(jnp.int32, (HDIM, HDIM), 0)
    cols = lax.broadcasted_iota(jnp.int32, (HDIM, HDIM), 1)
    return rows == cols


def causal():
    rows = lax.broadcasted_iota(jnp.int32, (SPAN, SPAN), 0)
    cols = lax.broadcasted_iota(jnp.int32, (SPAN, SPAN), 1)
    return rows >= cols


def corner():
    rows = lax.broadcasted_iota(jnp.int32, (HDIM, HDIM), 0)
    cols = lax.broadcasted_iota(jnp.int32, (HDIM, HDIM), 1)
    return rows, cols


def fold(one, two):
    rows, cols = corner()
    both = jnp.where(rows <= cols, one, two)
    line = jnp.sum(jnp.where(rows == cols, two, 0.0), axis=0, keepdims=True)
    return both, jnp.broadcast_to(line, (8, HDIM))


def unfold(both, line):
    rows, cols = corner()
    turned = both.T
    one = jnp.where(rows <= cols, both, turned)
    two = jnp.where(rows > cols, both, turned)
    two = jnp.where(rows == cols, line[:1], two)
    return one, two


def folded(heads):
    return (heads + 1) // 2


def fold_into(ref, mats, base=0):
    for i in range(folded(len(mats))):
        one, two = mats[2 * i], mats[min(2 * i + 1, len(mats) - 1)]
        both, line = fold(one, two)
        top = base + i * (HDIM + 8)
        ref[top : top + HDIM, :] = both
        ref[top + HDIM : top + HDIM + 8, :] = line


def unfold_from(ref, heads, base=0):
    mats = []
    for i in range(folded(heads)):
        top = base + i * (HDIM + 8)
        mats += unfold(ref[top : top + HDIM, :], ref[top + HDIM : top + HDIM + 8, :])
    return mats[:heads]


def totals_kernel(begin_ref, k_ref, v_ref, g_ref, n_ref):
    grams = []
    for h in range(k_ref.shape[1] // HDIM):
        cols = slice(h * HDIM, (h + 1) * HDIM)
        k = k_ref[:, cols]
        both = dot(k, cat([k, v_ref[:, cols]], 1), (0, 0))
        grams.append(both[:, :HDIM])
        n_ref[cols, :] = both[:, HDIM:]
    fold_into(g_ref, grams)


def totals(begin, keys, values, heads):
    return pl.pallas_call(
        totals_kernel,
        out_shape=(shape((folded(heads) * (HDIM + 8), HDIM)), shape((heads * HDIM, HDIM))),
        in_specs=[VMEM_SPEC] * 3,
        out_specs=(VMEM_SPEC, VMEM_SPEC),
        compiler_params=params(),
        cost_estimate=cost(2 * 2 * keys.size * HDIM, 4 * keys.size),
    )(begin, keys, values)


def taken(refs, backward):
    total = None
    mine = lax.axis_index("ctx")
    for r, ref in enumerate(refs):
        bit = (mine >> r) & 1
        wanted = jnp.where(bit == (0 if backward else 1), 1.0, 0.0)
        part = ref[...].astype(F32) * wanted
        total = part if total is None else total + part
    return total


def places(q_ref, heads):
    blocks = q_ref.shape[0] // SPAN
    for h in range(heads):
        for b in range(blocks):
            yield h, b, h * blocks + b, slice(b * SPAN, (b + 1) * SPAN), slice(h * HDIM, (h + 1) * HDIM)


def inverse_kernel(rounds, k_ref, *refs):
    e_ref, x_ref, last_ref, a_ref, es, xs = refs[rounds:]
    heads = k_ref.shape[1] // HDIM
    eye = unit()
    grams = unfold_from(taken(refs[:rounds], False), heads)
    for h, b, i, rows, cols in places(k_ref, heads):
        ridged = grams[h] + jnp.where(eye, RIDGE, 0.0)
        scale = 1.0 / jnp.sqrt(jnp.sum(ridged * ridged, keepdims=True))
        a_ref[i] = ridged
        es[i] = ridged * scale
        xs[i] = jnp.where(eye, scale, 0.0)
        k = k_ref[rows, cols]
        grams[h] = grams[h] + dot(k, k, (0, 0))
    nil = jnp.zeros((HDIM, HDIM), BF16)

    def step(j, carry):
        for i in range(es.shape[0]):
            e, x = es[i], xs[i]
            eh, el = split(e)
            xh, xl = split(x)
            e_ref[j, i] = eh
            x_ref[j, i] = xh
            left = cat([cat([eh, el], 1), cat([xh, xl], 1)], 0)
            right = cat([cat([eh, el], 1), cat([eh, nil], 1)], 0)
            both = dot(left, right)
            both = both[:, :HDIM] + both[:, HDIM:]
            es[i] = 2.0 * e - both[:HDIM]
            xs[i] = 2.0 * x - both[HDIM:]
        return carry

    lax.fori_loop(0, NEWTON, step, 0)
    for i in range(xs.shape[0]):
        last_ref[i] = xs[i]


def inverses(keys, grams, count):
    stash = shape((NEWTON, count, HDIM, HDIM), BF16)
    state = shape((count, HDIM, HDIM))
    return pl.pallas_call(
        functools.partial(inverse_kernel, len(grams)),
        out_shape=(stash, stash, state, state),
        in_specs=[VMEM_SPEC] * (1 + len(grams)),
        out_specs=(VMEM_SPEC,) * 4,
        scratch_shapes=[pltpu.VMEM((count, HDIM, HDIM), F32)] * 2,
        compiler_params=params(),
        cost_estimate=cost(2_000_000_000, 8_000_000),
    )(keys, *grams)


def outputs_kernel(rounds, q_ref, k_ref, v_ref, last_ref, *refs):
    out_ref, pre_ref, s_ref, w_ref = refs[rounds:]
    prefix = taken(refs[:rounds], False)
    heads = q_ref.shape[1] // HDIM
    keep = causal()
    nil = jnp.zeros((HDIM, HDIM), BF16)
    pairs = [prefix[h * HDIM : (h + 1) * HDIM, :] for h in range(heads)]
    for h, b, i, rows, cols in places(q_ref, heads):
        q, k, v = q_ref[rows, cols], k_ref[rows, cols], v_ref[rows, cols]
        xh, xl = split(last_ref[i])
        sh, sl = split(dot(cat([q, q], 1), cat([xh, xl], 0)))
        both = cat([sh, sl], 1)
        s_ref[i] = both
        scores = dot(both, cat([k, k], 1), (1, 1))
        scores = jnp.where(keep, scores, 0.0).astype(BF16)
        w_ref[i] = scores
        nh, nl = split(pairs[h])
        pre_ref[i] = cat([nh, nl], 1)
        state = dot(both, cat([cat([nh, nl], 1), cat([nh, nil], 1)], 0))
        out = dot(scores, v) + state[:, :HDIM] + state[:, HDIM:]
        out_ref[rows, cols] = out.astype(BF16)
        pairs[h] = pairs[h] + dot(k, v, (0, 0))


def outputs(queries, keys, values, last, pairs):
    count = last.shape[0]
    return pl.pallas_call(
        functools.partial(outputs_kernel, len(pairs)),
        out_shape=(
            shape(queries.shape, BF16),
            shape((count, HDIM, 2 * HDIM), BF16),
            shape((count, SPAN, 2 * HDIM), BF16),
            shape((count, SPAN, SPAN), BF16),
        ),
        in_specs=[VMEM_SPEC] * (4 + len(pairs)),
        out_specs=(VMEM_SPEC,) * 4,
        compiler_params=params(),
        cost_estimate=cost(2_000_000_000, 8_000_000),
    )(queries, keys, values, last, *pairs)


def tangent_kernel(
    q_ref, k_ref, v_ref, do_ref, e_ref, x_ref, last_ref, a_ref, pre_ref, s_ref, w_ref,
    dq_ref, dk_ref, dv_ref, da_ref, dn_ref, sum_ref, send_ref, des, dxs, first,
):
    heads = q_ref.shape[1] // HDIM
    keep = causal()
    nil = jnp.zeros((HDIM, HDIM), BF16)
    for h, b, i, rows, cols in places(q_ref, heads):
        q, k, v, do = q_ref[rows, cols], k_ref[rows, cols], v_ref[rows, cols], do_ref[rows, cols]
        weights = jnp.where(keep, dot(do, v, (1, 1)), 0.0).astype(BF16)
        ds = dot(weights, k) + dot(cat([do, do], 1), pre_ref[i], (1, 1))
        ds = ds.astype(BF16)
        xh, xl = split(last_ref[i])
        inverse = cat([xh, xl], 0)
        both = s_ref[i]
        sh = both[:, :HDIM]
        scores = w_ref[i]
        dv_ref[rows, cols] = dot(scores, do, (0, 0))
        dk_ref[rows, cols] = dot(weights, sh, (0, 0))
        state = dot(both, do, (0, 0))
        dn_ref[i] = state[:HDIM] + state[HDIM:]
        dq_ref[rows, cols] = dot(cat([ds, ds], 1), inverse).astype(BF16)
        bar = dot(q, ds, (0, 0))
        bar = bar + bar.T
        ridged = a_ref[i]
        scale = 1.0 / jnp.sqrt(jnp.sum(ridged * ridged, keepdims=True))
        first[i] = bar
        des[i] = bar * scale
        dxs[i] = jnp.zeros((HDIM, HDIM), F32)

    def step(j, carry):
        for i in range(des.shape[0]):
            e, x = e_ref[j, i], x_ref[j, i]
            de, dx = des[i], dxs[i]
            left = cat([cat([dx.astype(BF16), x], 1), cat([nil, e], 1)], 0)
            both = dot(left, cat([e, de.astype(BF16)], 0))
            turned = both[HDIM:]
            dxs[i] = 2.0 * dx - both[:HDIM]
            des[i] = 2.0 * de - (turned + turned.T)
        return carry

    lax.fori_loop(0, NEWTON, step, 0)
    sum_a = [jnp.zeros((HDIM, HDIM), F32) for _ in range(heads)]
    sum_n = [jnp.zeros((HDIM, HDIM), F32) for _ in range(heads)]
    for h, b, i, rows, cols in places(q_ref, heads):
        ridged, dx = a_ref[i], dxs[i]
        square = jnp.sum(ridged * ridged, keepdims=True)
        along = jnp.sum(first[i] * last_ref[i] + dx * ridged, keepdims=True)
        da = dx - (along / square) * ridged
        da_ref[i] = da
        sum_a[h] = sum_a[h] + da
        sum_n[h] = sum_n[h] + dn_ref[i]
    for h in range(heads):
        sum_ref[h * HDIM : (h + 1) * HDIM, :] = sum_n[h]
    fold_into(sum_ref, sum_a, heads * HDIM)
    send_ref[...] = sum_ref[...].astype(BF16)


def tangent(queries, keys, values, grads, stash):
    heads = queries.shape[1] // HDIM
    count = stash[-1].shape[0]
    state = shape((count, HDIM, HDIM))
    wide = shape(queries.shape)
    rows = heads * HDIM + folded(heads) * (HDIM + 8)
    return pl.pallas_call(
        tangent_kernel,
        out_shape=(
            shape(queries.shape, BF16), wide, wide, state, state,
            shape((rows, HDIM)), shape((rows, HDIM), BF16),
        ),
        in_specs=[VMEM_SPEC] * 11,
        out_specs=(VMEM_SPEC,) * 7,
        scratch_shapes=[pltpu.VMEM((count, HDIM, HDIM), F32)] * 3,
        compiler_params=params(),
        cost_estimate=cost(4_000_000_000, 8_000_000),
    )(queries, keys, values, grads, *stash)


def finish_kernel(rounds, k_ref, v_ref, dk_ref, dv_ref, da_ref, dn_ref, *refs):
    gk_ref, gv_ref = refs[rounds:]
    sum_ref = taken(refs[:rounds], True)
    heads = k_ref.shape[1] // HDIM
    sa = unfold_from(sum_ref, heads, heads * HDIM)
    sn = [sum_ref[h * HDIM : (h + 1) * HDIM, :] for h in range(heads)]
    for h, b, i, rows, cols in reversed(list(places(k_ref, heads))):
        k, v = k_ref[rows, cols], v_ref[rows, cols]
        nh, nl = split(sn[h])
        grad_k = dk_ref[rows, cols] + dot(k, sa[h].astype(BF16))
        grad_k = grad_k + dot(cat([v, v], 1), cat([nh, nl], 1), (1, 1))
        grad_v = dv_ref[rows, cols] + dot(cat([k, k], 1), cat([nh, nl], 0))
        gk_ref[rows, cols] = grad_k.astype(BF16)
        gv_ref[rows, cols] = grad_v.astype(BF16)
        sa[h] = sa[h] + da_ref[i]
        sn[h] = sn[h] + dn_ref[i]


def finish(keys, values, dk, dv, da, dn, sums):
    return pl.pallas_call(
        functools.partial(finish_kernel, len(sums)),
        out_shape=(shape(keys.shape, BF16),) * 2,
        in_specs=[VMEM_SPEC] * (6 + len(sums)),
        out_specs=(VMEM_SPEC,) * 2,
        compiler_params=params(),
        cost_estimate=cost(1_000_000_000, 6_000_000),
    )(keys, values, dk, dv, da, dn, *sums)


def lead_kernel(out_ref):
    out_ref[...] = jnp.zeros_like(out_ref)


def lead():
    return pl.pallas_call(
        lead_kernel,
        out_shape=shape((8, HDIM)),
        out_specs=VMEM_SPEC,
        compiler_params=params(),
        cost_estimate=cost(700_000_000, 4096),
    )()


def grads_kernel(first, w_ref, *refs):
    out_ref = refs[-1]
    me = lax.axis_index("head")
    total = refs[0][...] if first else None
    for s, part in enumerate(refs[1:-1] if first else refs[:-1]):
        width = part.shape[1]
        cols = pl.ds(pl.multiple_of((me ^ (first + s)) * width, width), width)
        term = dot(part[...], w_ref[:, cols], (1, 1))
        total = term if total is None else total + term
    out_ref[...] = total.astype(out_ref.dtype)


def head_grads(w_out, parts, first, begun=None):
    rows = parts[0].shape[0]
    begun = [] if begun is None else [begun]
    return pl.pallas_call(
        functools.partial(grads_kernel, first),
        out_shape=shape((rows, w_out.shape[0]), BF16 if begun else F32),
        in_specs=[VMEM_SPEC] * (1 + len(parts) + len(begun)),
        out_specs=VMEM_SPEC,
        compiler_params=params(),
        cost_estimate=cost(rows * w_out.size, 4_000_000),
    )(w_out, *begun, *parts)


def columns_kernel(w_ref, *refs):
    me = lax.axis_index("head")
    for s, out_ref in enumerate(refs):
        width = out_ref.shape[2]
        for f in range(2):
            target = me ^ (2 * s + f)
            cols = pl.ds(pl.multiple_of(target * width, width), width)
            out_ref[f] = w_ref[:, cols]


def column_pieces(w_out, count):
    piece = shape((2, w_out.shape[0], w_out.shape[1] // count), BF16)
    return pl.pallas_call(
        columns_kernel,
        out_shape=(piece,) * (count // 2),
        in_specs=[VMEM_SPEC],
        out_specs=(VMEM_SPEC,) * (count // 2),
        compiler_params=params(),
        cost_estimate=cost(0, 4 * w_out.size),
    )(w_out)


def weights_kernel(h_ref, *refs):
    parts, outs, all_ref = refs[:-5], refs[-5:-1], refs[-1]
    me, mine = lax.axis_index("head"), lax.axis_index("ctx")
    count, _, width = all_ref.shape
    fold = parts[0].shape[1] // width
    for s, part in enumerate(parts):
        term = dot(h_ref[...], part[...], (0, 0)).astype(BF16)
        for f in range(fold):
            target = (me ^ s) * fold + f
            all_ref[target ^ mine] = term[:, f * width : (f + 1) * width]
    for t in range(count):
        ref = outs[2 * (t % 2) + (t >= count // 2)]
        ref[t % (count // 2) // 2] = all_ref[t]


def weight_terms(heads_out, parts, count):
    feats = sum(part.shape[1] for part in parts)
    piece = (heads_out.shape[1], feats // count)
    return pl.pallas_call(
        weights_kernel,
        out_shape=(shape((count // 4,) + piece, BF16),) * 4,
        in_specs=[VMEM_SPEC] * (1 + len(parts)),
        out_specs=(VMEM_SPEC,) * 4,
        scratch_shapes=[pltpu.VMEM((count,) + piece, BF16)],
        compiler_params=params(),
        cost_estimate=cost(2 * heads_out.size * feats, 6_000_000),
    )(heads_out, *parts)


def layer_kernel(*refs):
    count = (len(refs) - 1) // 2
    total = None
    for s in range(count):
        term = dot(refs[s][...], refs[count + s][...])
        total = term if total is None else total + term
    refs[-1][...] = total.astype(BF16)


def layer(parts, blocks):
    rows, cols = parts[0].shape[0], blocks[0].shape[1]
    return pl.pallas_call(
        layer_kernel,
        out_shape=shape((rows, cols), BF16),
        in_specs=[VMEM_SPEC] * (len(parts) + len(blocks)),
        out_specs=VMEM_SPEC,
        compiler_params=params(),
        cost_estimate=cost(2 * rows * cols * sum(p.shape[1] for p in parts), 6_000_000),
    )(*parts, *blocks)


def swap(value, axis, distance):
    count = lax.axis_size(axis)
    return lax.ppermute(value, axis, [(i, i ^ distance) for i in range(count)])


def after(value, *others):
    return lax.optimization_barrier((value,) + others)[0]


def doublings(axis):
    return [1 << i for i in range((lax.axis_size(axis) - 1).bit_length())]


def shards(queries, keys, values, w_out, cotangent):
    heads = queries.shape[1] // HDIM
    count = heads * (queries.shape[0] // SPAN)
    head_count, ctx_count = lax.axis_size("head"), lax.axis_size("ctx")
    evens = range(2, head_count, 2)

    begin = lead()
    far = {s: swap(after(cotangent, begin), "head", s) for s in evens}
    gram, pair = totals(begin, keys, values, heads)
    near = swap(after(cotangent, gram, pair), "head", 1)

    grams, pairs = [], []
    begun = None
    for distance in doublings("ctx"):
        grams.append(swap(gram, "ctx", distance))
        pairs.append(swap(pair.astype(BF16), "ctx", distance))
        if begun is None:
            begun = head_grads(w_out, [cotangent, near], 0)
        gram, pair = gram + grams[-1], pair + pairs[-1].astype(F32)
    grams[-1] = after(grams[-1], begun)
    *stash, last, ridged = inverses(keys, grams, count)
    pairs[-1] = after(pairs[-1], last)
    parts = []
    for s in evens:
        parts += [far[s], swap(after(far[s], pairs[-1]), "head", 1)]
    columns = column_pieces(after(w_out, begun), head_count)
    columns = [after(c, pairs[-1], *far.values()) for c in columns]
    columns = [swap(c, "head", 2 * s) if s else c for s, c in enumerate(columns)]
    heads_out, states, solved, scores = outputs(queries, keys, values, last, pairs)

    grads = head_grads(w_out, parts, 2, after(begun, heads_out))
    parts = [cotangent, near] + parts
    even_low, even_high, odd_low, odd_high = weight_terms(
        after(heads_out, grads), parts, ctx_count
    )
    high = swap(odd_high, "ctx", 1)
    low = swap(odd_low, "ctx", 1)

    grad_queries, dk, dv, da, dn, sums, send = tangent(
        queries, keys, values, after(grads, odd_low), [*stash, last, ridged, states, solved, scores]
    )

    outs_out = after(heads_out, grad_queries)
    outs_far = [swap(outs_out, "head", s) for s in evens]
    high = even_high.astype(F32) + after(high, grad_queries).astype(F32)
    half = ctx_count // 4
    high = [high[u].astype(BF16) for u in range(half)]
    moved = [swap(part, "ctx", 2 * (half + u)) for u, part in enumerate(high)]

    later = []
    for distance in doublings("ctx"):
        sent = send
        later.append(swap(send, "ctx", distance))
        if distance == 1:
            later[0] = after(later[0], *high)
        sums = sums + later[-1].astype(F32)
        send = sums.astype(BF16)

    low = even_low.astype(F32) + after(low, later[0]).astype(F32)
    moved += [swap(low[u].astype(BF16), "ctx", 2 * u) for u in range(1, half)]

    outs = [heads_out, swap(outs_out, "head", 1)]
    for part in outs_far:
        outs += [part, swap(after(part, sent), "head", 1)]
    columns = [after(c, grad_queries, later[0]) for c in columns]
    crossing = swap(jnp.stack([c[1] for c in columns]), "head", 1)
    columns = [c for s in range(head_count // 2) for c in (columns[s][0], crossing[s])]
    layer_out = layer(outs, columns)
    grad_weight = low[0]
    for part in moved:
        grad_weight = grad_weight + after(part, layer_out).astype(F32)
    grad_keys, grad_values = finish(keys, values, dk, dv, da, dn, later)
    return (layer_out, grad_queries, grad_keys, grad_values, grad_weight)


def solution(mesh):
    in_specs = (
        P("ctx", "head"),
        P("ctx", "head"),
        P("ctx", "head"),
        P("head", None),
        P("ctx", "head"),
    )
    out_specs = (
        P("ctx", "head"),
        P("ctx", "head"),
        P("ctx", "head"),
        P("ctx", "head"),
        P("head", "ctx"),
    )
    return jax.shard_map(shards, mesh=mesh, in_specs=in_specs, out_specs=out_specs, check_vma=False)
```

```python
import functools

import jax
import jax.numpy as jnp
from jax import lax
from jax.experimental import pallas as pl
from jax.experimental.pallas import tpu as pltpu
from jax.sharding import PartitionSpec as P


HDIM = 128
SPAN = 256
NEWTON = 8
RIDGE = 1.0
F32 = jnp.float32
BF16 = jnp.bfloat16
VMEM_SPEC = pl.BlockSpec(memory_space=pltpu.VMEM)
ANY_SPEC = pl.BlockSpec(memory_space=pl.ANY)


def dot(left, right, axes=(1, 0)):
    return lax.dot_general(
        left, right, (((axes[0],), (axes[1],)), ((), ())), preferred_element_type=F32
    )


def split(value):
    high = value.astype(BF16)
    return high, (value - high.astype(F32)).astype(BF16)


def cat(parts, axis):
    return jnp.concatenate(parts, axis=axis)


def params(limit=8):
    return pltpu.CompilerParams(vmem_limit_bytes=limit * 1024 * 1024)


def cost(flops, size):
    return pl.CostEstimate(flops=flops, bytes_accessed=size, transcendentals=0)


def shape(dims, dtype=F32):
    return jax.ShapeDtypeStruct(dims, dtype)


def unit():
    rows = lax.broadcasted_iota(jnp.int32, (HDIM, HDIM), 0)
    cols = lax.broadcasted_iota(jnp.int32, (HDIM, HDIM), 1)
    return rows == cols


def causal():
    rows = lax.broadcasted_iota(jnp.int32, (SPAN, SPAN), 0)
    cols = lax.broadcasted_iota(jnp.int32, (SPAN, SPAN), 1)
    return rows >= cols


def corner():
    rows = lax.broadcasted_iota(jnp.int32, (HDIM, HDIM), 0)
    cols = lax.broadcasted_iota(jnp.int32, (HDIM, HDIM), 1)
    return rows, cols


def fold(one, two):
    rows, cols = corner()
    both = jnp.where(rows <= cols, one, two)
    line = jnp.sum(jnp.where(rows == cols, two, 0.0), axis=0, keepdims=True)
    return both, jnp.broadcast_to(line, (8, HDIM))


def unfold(both, line):
    rows, cols = corner()
    turned = both.T
    one = jnp.where(rows <= cols, both, turned)
    two = jnp.where(rows > cols, both, turned)
    two = jnp.where(rows == cols, line[:1], two)
    return one, two


def folded(heads):
    return (heads + 1) // 2


def fold_into(ref, mats, base=0):
    for i in range(folded(len(mats))):
        one, two = mats[2 * i], mats[min(2 * i + 1, len(mats) - 1)]
        both, line = fold(one, two)
        top = base + i * (HDIM + 8)
        ref[top : top + HDIM, :] = both
        ref[top + HDIM : top + HDIM + 8, :] = line


def unfold_from(ref, heads, base=0):
    mats = []
    for i in range(folded(heads)):
        top = base + i * (HDIM + 8)
        mats += unfold(ref[top : top + HDIM, :], ref[top + HDIM : top + HDIM + 8, :])
    return mats[:heads]


def totals_kernel(begin_ref, k_ref, v_ref, g_ref, n_ref):
    grams = []
    for h in range(k_ref.shape[1] // HDIM):
        cols = slice(h * HDIM, (h + 1) * HDIM)
        k = k_ref[:, cols]
        both = dot(k, cat([k, v_ref[:, cols]], 1), (0, 0))
        grams.append(both[:, :HDIM])
        n_ref[cols, :] = both[:, HDIM:]
    fold_into(g_ref, grams)


def totals(begin, keys, values, heads):
    return pl.pallas_call(
        totals_kernel,
        out_shape=(shape((folded(heads) * (HDIM + 8), HDIM)), shape((heads * HDIM, HDIM))),
        in_specs=[VMEM_SPEC] * 3,
        out_specs=(VMEM_SPEC, VMEM_SPEC),
        compiler_params=params(),
        cost_estimate=cost(2 * 2 * keys.size * HDIM, 4 * keys.size),
    )(begin, keys, values)


def taken(refs, backward):
    total = None
    mine = lax.axis_index("ctx")
    for r, ref in enumerate(refs):
        bit = (mine >> r) & 1
        wanted = jnp.where(bit == (0 if backward else 1), 1.0, 0.0)
        part = ref[...].astype(F32) * wanted
        total = part if total is None else total + part
    return total


def places(q_ref, heads):
    blocks = q_ref.shape[0] // SPAN
    for h in range(heads):
        for b in range(blocks):
            yield h, b, h * blocks + b, slice(b * SPAN, (b + 1) * SPAN), slice(h * HDIM, (h + 1) * HDIM)


def inverse_kernel(rounds, k_ref, *refs):
    e_ref, x_ref, last_ref, a_ref, es, xs = refs[rounds:]
    heads = k_ref.shape[1] // HDIM
    eye = unit()
    grams = unfold_from(taken(refs[:rounds], False), heads)
    for h, b, i, rows, cols in places(k_ref, heads):
        ridged = grams[h] + jnp.where(eye, RIDGE, 0.0)
        scale = 1.0 / jnp.sqrt(jnp.sum(ridged * ridged, keepdims=True))
        a_ref[i] = ridged
        es[i] = ridged * scale
        xs[i] = jnp.where(eye, scale, 0.0)
        k = k_ref[rows, cols]
        grams[h] = grams[h] + dot(k, k, (0, 0))
    nil = jnp.zeros((HDIM, HDIM), BF16)

    def step(j, carry):
        for i in range(es.shape[0]):
            e, x = es[i], xs[i]
            eh, el = split(e)
            xh, xl = split(x)
            e_ref[j, i] = eh
            x_ref[j, i] = xh
            left = cat([cat([eh, el], 1), cat([xh, xl], 1)], 0)
            right = cat([cat([eh, el], 1), cat([eh, nil], 1)], 0)
            both = dot(left, right)
            both = both[:, :HDIM] + both[:, HDIM:]
            es[i] = 2.0 * e - both[:HDIM]
            xs[i] = 2.0 * x - both[HDIM:]
        return carry

    lax.fori_loop(0, NEWTON, step, 0)
    for i in range(xs.shape[0]):
        last_ref[i] = xs[i]


def inverses(keys, grams, count):
    stash = shape((NEWTON, count, HDIM, HDIM), BF16)
    state = shape((count, HDIM, HDIM))
    return pl.pallas_call(
        functools.partial(inverse_kernel, len(grams)),
        out_shape=(stash, stash, state, state),
        in_specs=[VMEM_SPEC] * (1 + len(grams)),
        out_specs=(VMEM_SPEC,) * 4,
        scratch_shapes=[pltpu.VMEM((count, HDIM, HDIM), F32)] * 2,
        compiler_params=params(),
        cost_estimate=cost(2_000_000_000, 8_000_000),
    )(keys, *grams)


def outputs_kernel(rounds, q_ref, k_ref, v_ref, last_ref, *refs):
    out_ref, pre_ref, s_ref, w_ref = refs[rounds:]
    prefix = taken(refs[:rounds], False)
    heads = q_ref.shape[1] // HDIM
    keep = causal()
    nil = jnp.zeros((HDIM, HDIM), BF16)
    pairs = [prefix[h * HDIM : (h + 1) * HDIM, :] for h in range(heads)]
    for h, b, i, rows, cols in places(q_ref, heads):
        q, k, v = q_ref[rows, cols], k_ref[rows, cols], v_ref[rows, cols]
        xh, xl = split(last_ref[i])
        sh, sl = split(dot(cat([q, q], 1), cat([xh, xl], 0)))
        both = cat([sh, sl], 1)
        s_ref[i] = both
        scores = dot(both, cat([k, k], 1), (1, 1))
        scores = jnp.where(keep, scores, 0.0).astype(BF16)
        w_ref[i] = scores
        nh, nl = split(pairs[h])
        pre_ref[i] = cat([nh, nl], 1)
        state = dot(both, cat([cat([nh, nl], 1), cat([nh, nil], 1)], 0))
        out = dot(scores, v) + state[:, :HDIM] + state[:, HDIM:]
        out_ref[rows, cols] = out.astype(BF16)
        pairs[h] = pairs[h] + dot(k, v, (0, 0))


def outputs(queries, keys, values, last, pairs):
    count = last.shape[0]
    return pl.pallas_call(
        functools.partial(outputs_kernel, len(pairs)),
        out_shape=(
            shape(queries.shape, BF16),
            shape((count, HDIM, 2 * HDIM), BF16),
            shape((count, SPAN, 2 * HDIM), BF16),
            shape((count, SPAN, SPAN), BF16),
        ),
        in_specs=[VMEM_SPEC] * (4 + len(pairs)),
        out_specs=(VMEM_SPEC,) * 4,
        compiler_params=params(),
        cost_estimate=cost(2_000_000_000, 8_000_000),
    )(queries, keys, values, last, *pairs)


def tangent_kernel(
    q_ref, k_ref, v_ref, do_ref, e_ref, x_ref, last_ref, a_ref, pre_ref, s_ref,
    p_ref, ds_ref, da_ref, dn_ref, sum_ref, send_ref, des, dxs, first,
):
    heads = q_ref.shape[1] // HDIM
    keep = causal()
    nil = jnp.zeros((HDIM, HDIM), BF16)
    for h, b, i, rows, cols in places(q_ref, heads):
        q, k, v, do = q_ref[rows, cols], k_ref[rows, cols], v_ref[rows, cols], do_ref[rows, cols]
        weights = jnp.where(keep, dot(do, v, (1, 1)), 0.0).astype(BF16)
        p_ref[i] = weights
        ds = dot(weights, k) + dot(cat([do, do], 1), pre_ref[i], (1, 1))
        ds = ds.astype(BF16)
        ds_ref[rows, cols] = ds
        state = dot(s_ref[i], do, (0, 0))
        dn_ref[i] = state[:HDIM] + state[HDIM:]
        bar = dot(q, ds, (0, 0))
        bar = bar + bar.T
        ridged = a_ref[i]
        scale = 1.0 / jnp.sqrt(jnp.sum(ridged * ridged, keepdims=True))
        first[i] = bar
        des[i] = bar * scale
        dxs[i] = jnp.zeros((HDIM, HDIM), F32)

    def step(j, carry):
        for i in range(des.shape[0]):
            e, x = e_ref[j, i], x_ref[j, i]
            de, dx = des[i], dxs[i]
            left = cat([cat([dx.astype(BF16), x], 1), cat([nil, e], 1)], 0)
            both = dot(left, cat([e, de.astype(BF16)], 0))
            turned = both[HDIM:]
            dxs[i] = 2.0 * dx - both[:HDIM]
            des[i] = 2.0 * de - (turned + turned.T)
        return carry

    lax.fori_loop(0, NEWTON, step, 0)
    sum_a = [jnp.zeros((HDIM, HDIM), F32) for _ in range(heads)]
    sum_n = [jnp.zeros((HDIM, HDIM), F32) for _ in range(heads)]
    for h, b, i, rows, cols in places(q_ref, heads):
        ridged, dx = a_ref[i], dxs[i]
        square = jnp.sum(ridged * ridged, keepdims=True)
        along = jnp.sum(first[i] * last_ref[i] + dx * ridged, keepdims=True)
        da = dx - (along / square) * ridged
        da_ref[i] = da
        sum_a[h] = sum_a[h] + da
        sum_n[h] = sum_n[h] + dn_ref[i]
    for h in range(heads):
        sum_ref[h * HDIM : (h + 1) * HDIM, :] = sum_n[h]
    fold_into(sum_ref, sum_a, heads * HDIM)
    send_ref[...] = sum_ref[...].astype(BF16)


def tangent(queries, keys, values, grads, stash):
    heads = queries.shape[1] // HDIM
    count = stash[-1].shape[0]
    state = shape((count, HDIM, HDIM))
    rows = heads * HDIM + folded(heads) * (HDIM + 8)
    return pl.pallas_call(
        tangent_kernel,
        out_shape=(
            shape((count, SPAN, SPAN), BF16), shape(queries.shape, BF16), state, state,
            shape((rows, HDIM)), shape((rows, HDIM), BF16),
        ),
        in_specs=[VMEM_SPEC] * 10,
        out_specs=(VMEM_SPEC,) * 6,
        scratch_shapes=[pltpu.VMEM((count, HDIM, HDIM), F32)] * 3,
        compiler_params=params(),
        cost_estimate=cost(4_000_000_000, 8_000_000),
    )(queries, keys, values, grads, *stash)


def rest_kernel(
    k_ref, v_ref, do_ref, last_ref, s_ref, w_ref, p_ref, ds_ref, da_ref, dn_ref,
    dq_ref, dk_ref, dv_ref,
):
    heads = k_ref.shape[1] // HDIM
    sa, sn = [None] * heads, [None] * heads
    for h, b, i, rows, cols in reversed(list(places(k_ref, heads))):
        k, v, do, ds = k_ref[rows, cols], v_ref[rows, cols], do_ref[rows, cols], ds_ref[rows, cols]
        dq_ref[rows, cols] = dot(cat([ds, ds], 1), cat(split(last_ref[i]), 0)).astype(BF16)
        dk = dot(p_ref[i], s_ref[i, :, :HDIM], (0, 0))
        dv = dot(w_ref[i], do, (0, 0))
        if sa[h] is None:
            sa[h], sn[h] = da_ref[i], dn_ref[i]
        else:
            nh, nl = split(sn[h])
            dk = dk + dot(k, sa[h].astype(BF16)) + dot(cat([v, v], 1), cat([nh, nl], 1), (1, 1))
            dv = dv + dot(cat([k, k], 1), cat([nh, nl], 0))
            sa[h], sn[h] = sa[h] + da_ref[i], sn[h] + dn_ref[i]
        dk_ref[rows, cols] = dk
        dv_ref[rows, cols] = dv


def rest(keys, values, grads, *stash):
    wide = shape(keys.shape)
    return pl.pallas_call(
        rest_kernel,
        out_shape=(shape(keys.shape, BF16), wide, wide),
        in_specs=[VMEM_SPEC] * 10,
        out_specs=(VMEM_SPEC,) * 3,
        compiler_params=params(),
        cost_estimate=cost(2_000_000_000, 6_000_000),
    )(keys, values, grads, *stash)


def finish_kernel(rounds, k_ref, v_ref, dk_ref, dv_ref, *refs):
    gk_hbm, gv_hbm, gk_ref, gv_ref, sems = refs[rounds:]
    sums = taken(refs[:rounds], True)
    heads = k_ref.shape[1] // HDIM
    nil = jnp.zeros((HDIM, HDIM), BF16)
    right = []
    for h, sa in enumerate(unfold_from(sums, heads, heads * HDIM)):
        sn = sums[h * HDIM : (h + 1) * HDIM, :]
        top = cat([sa.astype(BF16), sn.astype(BF16)], 1)
        right.append(cat([top, cat([sn.T.astype(BF16), nil], 1)], 0))
    copies = []
    for b in range(k_ref.shape[0] // SPAN):
        rows = slice(b * SPAN, (b + 1) * SPAN)
        for h in range(heads):
            cols = slice(h * HDIM, (h + 1) * HDIM)
            total = dot(cat([k_ref[rows, cols], v_ref[rows, cols]], 1), right[h])
            gk_ref[rows, cols] = (dk_ref[rows, cols] + total[:, :HDIM]).astype(BF16)
            gv_ref[rows, cols] = (dv_ref[rows, cols] + total[:, HDIM:]).astype(BF16)
        for i, (ref, hbm) in enumerate(((gk_ref, gk_hbm), (gv_ref, gv_hbm))):
            copies.append(pltpu.make_async_copy(ref.at[rows], hbm.at[rows], sems.at[b, i]))
            copies[-1].start()
    for copy in copies:
        copy.wait()


def finish(keys, values, dk, dv, sums):
    blocks = keys.shape[0] // SPAN
    return pl.pallas_call(
        functools.partial(finish_kernel, len(sums)),
        out_shape=(shape(keys.shape, BF16),) * 2,
        in_specs=[VMEM_SPEC] * (4 + len(sums)),
        out_specs=(ANY_SPEC,) * 2,
        scratch_shapes=[pltpu.VMEM(keys.shape, BF16)] * 2
        + [pltpu.SemaphoreType.DMA((blocks, 2))],
        compiler_params=params(),
        cost_estimate=cost(1_000_000_000, 6_000_000),
    )(keys, values, dk, dv, *sums)


def lead_kernel(out_ref):
    out_ref[...] = jnp.zeros_like(out_ref)


def lead():
    return pl.pallas_call(
        lead_kernel,
        out_shape=shape((8, HDIM)),
        out_specs=VMEM_SPEC,
        compiler_params=params(),
        cost_estimate=cost(700_000_000, 4096),
    )()


def grads_kernel(first, w_ref, *refs):
    out_ref = refs[-1]
    me = lax.axis_index("head")
    total = refs[0][...] if first else None
    for s, part in enumerate(refs[1:-1] if first else refs[:-1]):
        width = part.shape[1]
        cols = pl.ds(pl.multiple_of((me ^ (first + s)) * width, width), width)
        term = dot(part[...], w_ref[:, cols], (1, 1))
        total = term if total is None else total + term
    out_ref[...] = total.astype(out_ref.dtype)


def head_grads(w_out, parts, first, begun=None):
    rows = parts[0].shape[0]
    begun = [] if begun is None else [begun]
    return pl.pallas_call(
        functools.partial(grads_kernel, first),
        out_shape=shape((rows, w_out.shape[0]), BF16 if begun else F32),
        in_specs=[VMEM_SPEC] * (1 + len(parts) + len(begun)),
        out_specs=VMEM_SPEC,
        compiler_params=params(),
        cost_estimate=cost(rows * w_out.size, 4_000_000),
    )(w_out, *begun, *parts)


def columns_kernel(w_ref, *refs):
    me = lax.axis_index("head")
    for s, out_ref in enumerate(refs):
        width = out_ref.shape[2]
        for f in range(2):
            target = me ^ (2 * s + f)
            cols = pl.ds(pl.multiple_of(target * width, width), width)
            out_ref[f] = w_ref[:, cols]


def column_pieces(w_out, count):
    piece = shape((2, w_out.shape[0], w_out.shape[1] // count), BF16)
    return pl.pallas_call(
        columns_kernel,
        out_shape=(piece,) * (count // 2),
        in_specs=[VMEM_SPEC],
        out_specs=(VMEM_SPEC,) * (count // 2),
        compiler_params=params(),
        cost_estimate=cost(0, 4 * w_out.size),
    )(w_out)


def weights_kernel(h_ref, *refs):
    parts, outs, all_ref = refs[:-5], refs[-5:-1], refs[-1]
    me, mine = lax.axis_index("head"), lax.axis_index("ctx")
    count, _, width = all_ref.shape
    fold = parts[0].shape[1] // width
    for s, part in enumerate(parts):
        term = dot(h_ref[...], part[...], (0, 0)).astype(BF16)
        for f in range(fold):
            target = (me ^ s) * fold + f
            all_ref[target ^ mine] = term[:, f * width : (f + 1) * width]
    for t in range(count):
        ref = outs[2 * (t % 2) + (t >= count // 2)]
        ref[t % (count // 2) // 2] = all_ref[t]


def weight_terms(heads_out, parts, count):
    feats = sum(part.shape[1] for part in parts)
    piece = (heads_out.shape[1], feats // count)
    return pl.pallas_call(
        weights_kernel,
        out_shape=(shape((count // 4,) + piece, BF16),) * 4,
        in_specs=[VMEM_SPEC] * (1 + len(parts)),
        out_specs=(VMEM_SPEC,) * 4,
        scratch_shapes=[pltpu.VMEM((count,) + piece, BF16)],
        compiler_params=params(),
        cost_estimate=cost(2 * heads_out.size * feats, 6_000_000),
    )(heads_out, *parts)


def layer_kernel(*refs):
    count = (len(refs) - 1) // 2
    total = None
    for s in range(count):
        term = dot(refs[s][...], refs[count + s][...])
        total = term if total is None else total + term
    refs[-1][...] = total.astype(BF16)


def layer(parts, blocks):
    rows, cols = parts[0].shape[0], blocks[0].shape[1]
    return pl.pallas_call(
        layer_kernel,
        out_shape=shape((rows, cols), BF16),
        in_specs=[VMEM_SPEC] * (len(parts) + len(blocks)),
        out_specs=VMEM_SPEC,
        compiler_params=params(),
        cost_estimate=cost(2 * rows * cols * sum(p.shape[1] for p in parts), 6_000_000),
    )(*parts, *blocks)


def swap(value, axis, distance):
    count = lax.axis_size(axis)
    return lax.ppermute(value, axis, [(i, i ^ distance) for i in range(count)])


def after(value, *others):
    return lax.optimization_barrier((value,) + others)[0]


def doublings(axis):
    return [1 << i for i in range((lax.axis_size(axis) - 1).bit_length())]


def shards(queries, keys, values, w_out, cotangent):
    heads = queries.shape[1] // HDIM
    count = heads * (queries.shape[0] // SPAN)
    head_count, ctx_count = lax.axis_size("head"), lax.axis_size("ctx")
    evens = range(2, head_count, 2)

    begin = lead()
    far = {s: swap(after(cotangent, begin), "head", s) for s in evens}
    gram, pair = totals(begin, keys, values, heads)
    near = swap(after(cotangent, gram, pair), "head", 1)

    grams, pairs = [], []
    begun = None
    rounds = doublings("ctx")
    for r, distance in enumerate(rounds):
        grams.append(swap(gram, "ctx", distance))
        if begun is None:
            begun = head_grads(w_out, [cotangent, near], 0)
        if distance != rounds[-1]:
            gram = gram + grams[-1]
        if r:
            pairs[-1] = after(pairs[-1], gram)
            pair = pair + pairs[-1].astype(F32)
        pairs.append(swap(pair.astype(BF16), "ctx", distance))
    grams[-1] = after(grams[-1], begun)
    *stash, last, ridged = inverses(keys, grams, count)
    pairs[-1] = after(pairs[-1], last)
    parts = []
    for s in evens:
        parts += [far[s], swap(after(far[s], pairs[-1]), "head", 1)]
    columns = column_pieces(after(w_out, begun), head_count)
    columns = [after(c, pairs[-1], *far.values()) for c in columns]
    columns = [swap(c, "head", 2 * s) if s else c for s, c in enumerate(columns)]
    heads_out, states, solved, scores = outputs(queries, keys, values, last, pairs)

    grads = head_grads(w_out, parts, 2, after(begun, heads_out))
    parts = [cotangent, near] + parts
    even_low, even_high, odd_low, odd_high = weight_terms(
        after(heads_out, grads), parts, ctx_count
    )
    high = swap(odd_high, "ctx", 1)
    low = swap(odd_low, "ctx", 1)

    weights, ds, da, dn, sums, send = tangent(
        queries, keys, values, after(grads, odd_low), [*stash, last, ridged, states, solved]
    )

    outs_out = after(heads_out, send)
    outs_far = [swap(outs_out, "head", s) for s in evens]
    high = even_high.astype(F32) + after(high, send).astype(F32)
    half = ctx_count // 4
    high = [high[u].astype(BF16) for u in range(half)]
    moved = [swap(part, "ctx", 2 * (half + u)) for u, part in enumerate(high)]

    later = []
    for distance in doublings("ctx"):
        sent = send
        later.append(swap(send, "ctx", distance))
        if distance == 1:
            later[0] = after(later[0], *high)
        sums = sums + later[-1].astype(F32)
        send = sums.astype(BF16)

    low = even_low.astype(F32) + after(low, later[0]).astype(F32)
    moved += [swap(low[u].astype(BF16), "ctx", 2 * u) for u in range(1, half)]

    outs = [heads_out, swap(outs_out, "head", 1)]
    for part in outs_far:
        outs += [part, swap(after(part, sent), "head", 1)]
    columns = [after(c, later[0]) for c in columns]
    crossing = swap(jnp.stack([c[1] for c in columns]), "head", 1)
    columns = [c for s in range(head_count // 2) for c in (columns[s][0], crossing[s])]
    grad_queries, dk, dv = rest(
        keys, values, grads, last, solved, scores, weights, after(ds, sent), da, dn
    )
    layer_out = layer(outs, columns)
    grad_weight = low[0]
    for part in moved:
        grad_weight = grad_weight + after(part, layer_out).astype(F32)
    grad_keys, grad_values = finish(keys, values, dk, dv, later)
    return (layer_out, grad_queries, grad_keys, grad_values, grad_weight)


def solution(mesh):
    in_specs = (
        P("ctx", "head"),
        P("ctx", "head"),
        P("ctx", "head"),
        P("head", None),
        P("ctx", "head"),
    )
    out_specs = (
        P("ctx", "head"),
        P("ctx", "head"),
        P("ctx", "head"),
        P("ctx", "head"),
        P("head", "ctx"),
    )
    return jax.shard_map(shards, mesh=mesh, in_specs=in_specs, out_specs=out_specs, check_vma=False)
```

```python
import functools

import jax
import jax.numpy as jnp
from jax import lax
from jax.experimental import pallas as pl
from jax.experimental.pallas import tpu as pltpu
from jax.sharding import PartitionSpec as P


HDIM = 128
SPAN = 256
NEWTON = 8
RIDGE = 1.0
F32 = jnp.float32
BF16 = jnp.bfloat16
VMEM_SPEC = pl.BlockSpec(memory_space=pltpu.VMEM)
ANY_SPEC = pl.BlockSpec(memory_space=pl.ANY)


def dot(left, right, axes=(1, 0)):
    return lax.dot_general(
        left, right, (((axes[0],), (axes[1],)), ((), ())), preferred_element_type=F32
    )


def split(value):
    high = value.astype(BF16)
    return high, (value - high.astype(F32)).astype(BF16)


def cat(parts, axis):
    return jnp.concatenate(parts, axis=axis)


def params(limit=8):
    return pltpu.CompilerParams(vmem_limit_bytes=limit * 1024 * 1024)


def cost(flops, size):
    return pl.CostEstimate(flops=flops, bytes_accessed=size, transcendentals=0)


def shape(dims, dtype=F32):
    return jax.ShapeDtypeStruct(dims, dtype)


def unit():
    rows = lax.broadcasted_iota(jnp.int32, (HDIM, HDIM), 0)
    cols = lax.broadcasted_iota(jnp.int32, (HDIM, HDIM), 1)
    return rows == cols


def causal():
    rows = lax.broadcasted_iota(jnp.int32, (SPAN, SPAN), 0)
    cols = lax.broadcasted_iota(jnp.int32, (SPAN, SPAN), 1)
    return rows >= cols


def corner():
    rows = lax.broadcasted_iota(jnp.int32, (HDIM, HDIM), 0)
    cols = lax.broadcasted_iota(jnp.int32, (HDIM, HDIM), 1)
    return rows, cols


def fold(one, two):
    rows, cols = corner()
    both = jnp.where(rows <= cols, one, two)
    line = jnp.sum(jnp.where(rows == cols, two, 0.0), axis=0, keepdims=True)
    return both, jnp.broadcast_to(line, (8, HDIM))


def unfold(both, line):
    rows, cols = corner()
    turned = both.T
    one = jnp.where(rows <= cols, both, turned)
    two = jnp.where(rows > cols, both, turned)
    two = jnp.where(rows == cols, line[:1], two)
    return one, two


def folded(heads):
    return (heads + 1) // 2


def fold_into(ref, mats, base=0):
    for i in range(folded(len(mats))):
        one, two = mats[2 * i], mats[min(2 * i + 1, len(mats) - 1)]
        both, line = fold(one, two)
        top = base + i * (HDIM + 8)
        ref[top : top + HDIM, :] = both
        ref[top + HDIM : top + HDIM + 8, :] = line


def unfold_from(ref, heads, base=0):
    mats = []
    for i in range(folded(heads)):
        top = base + i * (HDIM + 8)
        mats += unfold(ref[top : top + HDIM, :], ref[top + HDIM : top + HDIM + 8, :])
    return mats[:heads]


def totals_kernel(begin_ref, k_ref, v_ref, g_ref, n_ref):
    grams = []
    for h in range(k_ref.shape[1] // HDIM):
        cols = slice(h * HDIM, (h + 1) * HDIM)
        k = k_ref[:, cols]
        both = dot(k, cat([k, v_ref[:, cols]], 1), (0, 0))
        grams.append(both[:, :HDIM])
        n_ref[cols, :] = both[:, HDIM:]
    fold_into(g_ref, grams)


def totals(begin, keys, values, heads):
    return pl.pallas_call(
        totals_kernel,
        out_shape=(shape((folded(heads) * (HDIM + 8), HDIM)), shape((heads * HDIM, HDIM))),
        in_specs=[VMEM_SPEC] * 3,
        out_specs=(VMEM_SPEC, VMEM_SPEC),
        compiler_params=params(),
        cost_estimate=cost(2 * 2 * keys.size * HDIM, 4 * keys.size),
    )(begin, keys, values)


def taken(refs, backward):
    total = None
    mine = lax.axis_index("ctx")
    for r, ref in enumerate(refs):
        bit = (mine >> r) & 1
        wanted = jnp.where(bit == (0 if backward else 1), 1.0, 0.0)
        part = ref[...].astype(F32) * wanted
        total = part if total is None else total + part
    return total


def places(q_ref, heads):
    blocks = q_ref.shape[0] // SPAN
    for h in range(heads):
        for b in range(blocks):
            yield h, b, h * blocks + b, slice(b * SPAN, (b + 1) * SPAN), slice(h * HDIM, (h + 1) * HDIM)


def inverse_kernel(rounds, k_ref, *refs):
    e_ref, x_ref, last_ref, a_ref, es, xs = refs[rounds:]
    heads = k_ref.shape[1] // HDIM
    eye = unit()
    grams = unfold_from(taken(refs[:rounds], False), heads)
    for h, b, i, rows, cols in places(k_ref, heads):
        ridged = grams[h] + jnp.where(eye, RIDGE, 0.0)
        scale = 1.0 / jnp.sqrt(jnp.sum(ridged * ridged, keepdims=True))
        a_ref[i] = ridged
        es[i] = ridged * scale
        xs[i] = jnp.where(eye, scale, 0.0)
        k = k_ref[rows, cols]
        grams[h] = grams[h] + dot(k, k, (0, 0))
    nil = jnp.zeros((HDIM, HDIM), BF16)

    def step(j, carry):
        for i in range(es.shape[0]):
            e, x = es[i], xs[i]
            eh, el = split(e)
            xh, xl = split(x)
            e_ref[j, i] = eh
            x_ref[j, i] = xh
            left = cat([cat([eh, el], 1), cat([xh, xl], 1)], 0)
            right = cat([cat([eh, el], 1), cat([eh, nil], 1)], 0)
            both = dot(left, right)
            both = both[:, :HDIM] + both[:, HDIM:]
            es[i] = 2.0 * e - both[:HDIM]
            xs[i] = 2.0 * x - both[HDIM:]
        return carry

    lax.fori_loop(0, NEWTON, step, 0)
    for i in range(xs.shape[0]):
        last_ref[i] = xs[i]


def inverses(keys, grams, count):
    stash = shape((NEWTON, count, HDIM, HDIM), BF16)
    state = shape((count, HDIM, HDIM))
    return pl.pallas_call(
        functools.partial(inverse_kernel, len(grams)),
        out_shape=(stash, stash, state, state),
        in_specs=[VMEM_SPEC] * (1 + len(grams)),
        out_specs=(VMEM_SPEC,) * 4,
        scratch_shapes=[pltpu.VMEM((count, HDIM, HDIM), F32)] * 2,
        compiler_params=params(),
        cost_estimate=cost(2_000_000_000, 8_000_000),
    )(keys, *grams)


def outputs_kernel(rounds, q_ref, k_ref, v_ref, last_ref, *refs):
    out_ref, pre_ref, s_ref, w_ref = refs[rounds:]
    prefix = taken(refs[:rounds], False)
    heads = q_ref.shape[1] // HDIM
    keep = causal()
    nil = jnp.zeros((HDIM, HDIM), BF16)
    pairs = [prefix[h * HDIM : (h + 1) * HDIM, :] for h in range(heads)]
    for h, b, i, rows, cols in places(q_ref, heads):
        q, k, v = q_ref[rows, cols], k_ref[rows, cols], v_ref[rows, cols]
        xh, xl = split(last_ref[i])
        sh, sl = split(dot(cat([q, q], 1), cat([xh, xl], 0)))
        both = cat([sh, sl], 1)
        s_ref[i] = both
        scores = dot(both, cat([k, k], 1), (1, 1))
        scores = jnp.where(keep, scores, 0.0).astype(BF16)
        w_ref[i] = scores
        nh, nl = split(pairs[h])
        pre_ref[i] = cat([nh, nl], 1)
        state = dot(both, cat([cat([nh, nl], 1), cat([nh, nil], 1)], 0))
        out = dot(scores, v) + state[:, :HDIM] + state[:, HDIM:]
        out_ref[rows, cols] = out.astype(BF16)
        pairs[h] = pairs[h] + dot(k, v, (0, 0))


def outputs(queries, keys, values, last, pairs):
    count = last.shape[0]
    return pl.pallas_call(
        functools.partial(outputs_kernel, len(pairs)),
        out_shape=(
            shape(queries.shape, BF16),
            shape((count, HDIM, 2 * HDIM), BF16),
            shape((count, SPAN, 2 * HDIM), BF16),
            shape((count, SPAN, SPAN), BF16),
        ),
        in_specs=[VMEM_SPEC] * (4 + len(pairs)),
        out_specs=(VMEM_SPEC,) * 4,
        compiler_params=params(),
        cost_estimate=cost(2_000_000_000, 8_000_000),
    )(queries, keys, values, last, *pairs)


def tangent_kernel(
    q_ref, k_ref, v_ref, do_ref, e_ref, x_ref, last_ref, a_ref, pre_ref, s_ref,
    p_ref, ds_ref, da_ref, dn_ref, sum_ref, send_ref, des, dxs, first,
):
    heads = q_ref.shape[1] // HDIM
    keep = causal()
    nil = jnp.zeros((HDIM, HDIM), BF16)
    for h, b, i, rows, cols in places(q_ref, heads):
        q, k, v, do = q_ref[rows, cols], k_ref[rows, cols], v_ref[rows, cols], do_ref[rows, cols]
        weights = jnp.where(keep, dot(do, v, (1, 1)), 0.0).astype(BF16)
        p_ref[i] = weights
        ds = dot(weights, k) + dot(cat([do, do], 1), pre_ref[i], (1, 1))
        ds = ds.astype(BF16)
        ds_ref[rows, cols] = ds
        state = dot(s_ref[i], do, (0, 0))
        dn_ref[i] = state[:HDIM] + state[HDIM:]
        bar = dot(q, ds, (0, 0))
        bar = bar + bar.T
        ridged = a_ref[i]
        scale = 1.0 / jnp.sqrt(jnp.sum(ridged * ridged, keepdims=True))
        first[i] = bar
        des[i] = bar * scale
        dxs[i] = jnp.zeros((HDIM, HDIM), F32)

    def step(j, carry):
        for i in range(des.shape[0]):
            e, x = e_ref[j, i], x_ref[j, i]
            de, dx = des[i], dxs[i]
            left = cat([cat([dx.astype(BF16), x], 1), cat([nil, e], 1)], 0)
            both = dot(left, cat([e, de.astype(BF16)], 0))
            turned = both[HDIM:]
            dxs[i] = 2.0 * dx - both[:HDIM]
            des[i] = 2.0 * de - (turned + turned.T)
        return carry

    lax.fori_loop(0, NEWTON, step, 0)
    sum_a = [jnp.zeros((HDIM, HDIM), F32) for _ in range(heads)]
    sum_n = [jnp.zeros((HDIM, HDIM), F32) for _ in range(heads)]
    for h, b, i, rows, cols in places(q_ref, heads):
        ridged, dx = a_ref[i], dxs[i]
        square = jnp.sum(ridged * ridged, keepdims=True)
        along = jnp.sum(first[i] * last_ref[i] + dx * ridged, keepdims=True)
        da = dx - (along / square) * ridged
        da_ref[i] = da
        sum_a[h] = sum_a[h] + da
        sum_n[h] = sum_n[h] + dn_ref[i]
    for h in range(heads):
        sum_ref[h * HDIM : (h + 1) * HDIM, :] = sum_n[h]
    fold_into(sum_ref, sum_a, heads * HDIM)
    send_ref[...] = sum_ref[...].astype(BF16)


def tangent(queries, keys, values, grads, stash):
    heads = queries.shape[1] // HDIM
    count = stash[-1].shape[0]
    state = shape((count, HDIM, HDIM))
    rows = heads * HDIM + folded(heads) * (HDIM + 8)
    return pl.pallas_call(
        tangent_kernel,
        out_shape=(
            shape((count, SPAN, SPAN), BF16), shape(queries.shape, BF16), state, state,
            shape((rows, HDIM)), shape((rows, HDIM), BF16),
        ),
        in_specs=[VMEM_SPEC] * 10,
        out_specs=(VMEM_SPEC,) * 6,
        scratch_shapes=[pltpu.VMEM((count, HDIM, HDIM), F32)] * 3,
        compiler_params=params(),
        cost_estimate=cost(4_000_000_000, 8_000_000),
    )(queries, keys, values, grads, *stash)


def rest_kernel(
    k_ref, v_ref, do_ref, last_ref, s_ref, w_ref, p_ref, ds_ref, da_ref, dn_ref,
    dq_ref, dk_ref, dv_ref,
):
    heads = k_ref.shape[1] // HDIM
    sa, sn = [None] * heads, [None] * heads
    for h, b, i, rows, cols in reversed(list(places(k_ref, heads))):
        k, v, do, ds = k_ref[rows, cols], v_ref[rows, cols], do_ref[rows, cols], ds_ref[rows, cols]
        dq_ref[rows, cols] = dot(cat([ds, ds], 1), cat(split(last_ref[i]), 0)).astype(BF16)
        dk = dot(p_ref[i], s_ref[i, :, :HDIM], (0, 0))
        dv = dot(w_ref[i], do, (0, 0))
        if sa[h] is None:
            sa[h], sn[h] = da_ref[i], dn_ref[i]
        else:
            nh, nl = split(sn[h])
            dk = dk + dot(k, sa[h].astype(BF16)) + dot(cat([v, v], 1), cat([nh, nl], 1), (1, 1))
            dv = dv + dot(cat([k, k], 1), cat([nh, nl], 0))
            sa[h], sn[h] = sa[h] + da_ref[i], sn[h] + dn_ref[i]
        dk_ref[rows, cols] = dk
        dv_ref[rows, cols] = dv


def rest(keys, values, grads, *stash):
    wide = shape(keys.shape)
    return pl.pallas_call(
        rest_kernel,
        out_shape=(shape(keys.shape, BF16), wide, wide),
        in_specs=[VMEM_SPEC] * 10,
        out_specs=(VMEM_SPEC,) * 3,
        compiler_params=params(),
        cost_estimate=cost(2_000_000_000, 6_000_000),
    )(keys, values, grads, *stash)


def finish_kernel(rounds, k_ref, v_ref, dk_ref, dv_ref, *refs):
    gk_hbm, gv_hbm, gk_ref, gv_ref, sems = refs[rounds:]
    sums = taken(refs[:rounds], True)
    heads = k_ref.shape[1] // HDIM
    nil = jnp.zeros((HDIM, HDIM), BF16)
    right = []
    for h, sa in enumerate(unfold_from(sums, heads, heads * HDIM)):
        sn = sums[h * HDIM : (h + 1) * HDIM, :]
        top = cat([sa.astype(BF16), sn.astype(BF16)], 1)
        right.append(cat([top, cat([sn.T.astype(BF16), nil], 1)], 0))
    copies = []
    for b in range(k_ref.shape[0] // SPAN):
        rows = slice(b * SPAN, (b + 1) * SPAN)
        for h in range(heads):
            cols = slice(h * HDIM, (h + 1) * HDIM)
            total = dot(cat([k_ref[rows, cols], v_ref[rows, cols]], 1), right[h])
            gk_ref[rows, cols] = (dk_ref[rows, cols] + total[:, :HDIM]).astype(BF16)
            gv_ref[rows, cols] = (dv_ref[rows, cols] + total[:, HDIM:]).astype(BF16)
        for i, (ref, hbm) in enumerate(((gk_ref, gk_hbm), (gv_ref, gv_hbm))):
            copies.append(pltpu.make_async_copy(ref.at[rows], hbm.at[rows], sems.at[b, i]))
            copies[-1].start()
    for copy in copies:
        copy.wait()


def finish(keys, values, dk, dv, sums):
    blocks = keys.shape[0] // SPAN
    return pl.pallas_call(
        functools.partial(finish_kernel, len(sums)),
        out_shape=(shape(keys.shape, BF16),) * 2,
        in_specs=[VMEM_SPEC] * (4 + len(sums)),
        out_specs=(ANY_SPEC,) * 2,
        scratch_shapes=[pltpu.VMEM(keys.shape, BF16)] * 2
        + [pltpu.SemaphoreType.DMA((blocks, 2))],
        compiler_params=params(),
        cost_estimate=cost(1_000_000_000, 6_000_000),
    )(keys, values, dk, dv, *sums)


def lead_kernel(out_ref):
    out_ref[...] = jnp.zeros_like(out_ref)


def lead():
    return pl.pallas_call(
        lead_kernel,
        out_shape=shape((8, HDIM)),
        out_specs=VMEM_SPEC,
        compiler_params=params(),
        cost_estimate=cost(700_000_000, 4096),
    )()


def grads_kernel(first, w_ref, *refs):
    out_ref = refs[-1]
    me = lax.axis_index("head")
    total = refs[0][...] if first else None
    for s, part in enumerate(refs[1:-1] if first else refs[:-1]):
        width = part.shape[1]
        cols = pl.ds(pl.multiple_of((me ^ (first + s)) * width, width), width)
        term = dot(part[...], w_ref[:, cols], (1, 1))
        total = term if total is None else total + term
    out_ref[...] = total.astype(out_ref.dtype)


def head_grads(w_out, parts, first, begun=None):
    rows = parts[0].shape[0]
    begun = [] if begun is None else [begun]
    return pl.pallas_call(
        functools.partial(grads_kernel, first),
        out_shape=shape((rows, w_out.shape[0]), BF16 if begun else F32),
        in_specs=[VMEM_SPEC] * (1 + len(parts) + len(begun)),
        out_specs=VMEM_SPEC,
        compiler_params=params(),
        cost_estimate=cost(rows * w_out.size, 4_000_000),
    )(w_out, *begun, *parts)


def columns_kernel(w_ref, *refs):
    me = lax.axis_index("head")
    for s, out_ref in enumerate(refs):
        width = out_ref.shape[2]
        for f in range(2):
            target = me ^ (2 * s + f)
            cols = pl.ds(pl.multiple_of(target * width, width), width)
            out_ref[f] = w_ref[:, cols]


def column_pieces(w_out, count):
    piece = shape((2, w_out.shape[0], w_out.shape[1] // count), BF16)
    return pl.pallas_call(
        columns_kernel,
        out_shape=(piece,) * (count // 2),
        in_specs=[VMEM_SPEC],
        out_specs=(VMEM_SPEC,) * (count // 2),
        compiler_params=params(),
        cost_estimate=cost(0, 4 * w_out.size),
    )(w_out)


def weights_kernel(h_ref, *refs):
    parts, outs, all_ref = refs[:-5], refs[-5:-1], refs[-1]
    me, mine = lax.axis_index("head"), lax.axis_index("ctx")
    count, _, width = all_ref.shape
    fold = parts[0].shape[1] // width
    for s, part in enumerate(parts):
        term = dot(h_ref[...], part[...], (0, 0)).astype(BF16)
        for f in range(fold):
            target = (me ^ s) * fold + f
            all_ref[target ^ mine] = term[:, f * width : (f + 1) * width]
    for t in range(count):
        ref = outs[2 * (t % 2) + (t >= count // 2)]
        ref[t % (count // 2) // 2] = all_ref[t]


def weight_terms(heads_out, parts, count):
    feats = sum(part.shape[1] for part in parts)
    piece = (heads_out.shape[1], feats // count)
    return pl.pallas_call(
        weights_kernel,
        out_shape=(shape((count // 4,) + piece, BF16),) * 4,
        in_specs=[VMEM_SPEC] * (1 + len(parts)),
        out_specs=(VMEM_SPEC,) * 4,
        scratch_shapes=[pltpu.VMEM((count,) + piece, BF16)],
        compiler_params=params(),
        cost_estimate=cost(2 * heads_out.size * feats, 6_000_000),
    )(heads_out, *parts)


def layer_kernel(*refs):
    count = (len(refs) - 1) // 2
    total = None
    for s in range(count):
        term = dot(refs[s][...], refs[count + s][...])
        total = term if total is None else total + term
    refs[-1][...] = total.astype(BF16)


def layer(parts, blocks):
    rows, cols = parts[0].shape[0], blocks[0].shape[1]
    return pl.pallas_call(
        layer_kernel,
        out_shape=shape((rows, cols), BF16),
        in_specs=[VMEM_SPEC] * (len(parts) + len(blocks)),
        out_specs=VMEM_SPEC,
        compiler_params=params(),
        cost_estimate=cost(2 * rows * cols * sum(p.shape[1] for p in parts), 6_000_000),
    )(*parts, *blocks)


def swap(value, axis, distance):
    count = lax.axis_size(axis)
    return lax.ppermute(value, axis, [(i, i ^ distance) for i in range(count)])


def after(value, *others):
    return lax.optimization_barrier((value,) + others)[0]


def doublings(axis):
    return [1 << i for i in range((lax.axis_size(axis) - 1).bit_length())]


def shards(queries, keys, values, w_out, cotangent):
    heads = queries.shape[1] // HDIM
    count = heads * (queries.shape[0] // SPAN)
    head_count, ctx_count = lax.axis_size("head"), lax.axis_size("ctx")
    evens = range(2, head_count, 2)

    far = {s: swap(cotangent, "head", s) for s in evens}
    begin = lead()
    gram, pair = totals(begin, keys, values, heads)
    near = swap(after(cotangent, gram, pair), "head", 1)

    grams, pairs = [], []
    begun = None
    rounds = doublings("ctx")
    for r, distance in enumerate(rounds):
        grams.append(swap(gram, "ctx", distance))
        if begun is None:
            begun = head_grads(w_out, [cotangent, near], 0)
        if distance != rounds[-1]:
            gram = gram + grams[-1]
        if r:
            pairs[-1] = after(pairs[-1], gram)
            pair = pair + pairs[-1].astype(F32)
        pairs.append(swap(pair.astype(BF16), "ctx", distance))
    grams[-1] = after(grams[-1], begun)
    *stash, last, ridged = inverses(keys, grams, count)
    pairs[-1] = after(pairs[-1], last)
    parts = []
    for s in evens:
        parts += [far[s], swap(after(far[s], pairs[-1]), "head", 1)]
    columns = column_pieces(after(w_out, begun), head_count)
    columns = [after(c, pairs[-1], *far.values()) for c in columns]
    columns = [swap(c, "head", 2 * s) if s else c for s, c in enumerate(columns)]
    heads_out, states, solved, scores = outputs(queries, keys, values, last, pairs)

    grads = head_grads(w_out, parts, 2, after(begun, heads_out))
    parts = [cotangent, near] + parts
    even_low, even_high, odd_low, odd_high = weight_terms(
        after(heads_out, grads), parts, ctx_count
    )
    high = swap(odd_high, "ctx", 1)

    weights, ds, da, dn, sums, send = tangent(
        queries, keys, values, after(grads, odd_low), [*stash, last, ridged, states, solved]
    )

    low = swap(after(odd_low, send), "ctx", 1)
    outs_out = after(heads_out, send)
    outs_far = [swap(outs_out, "head", s) for s in evens]
    high = even_high.astype(F32) + after(high, send).astype(F32)
    half = ctx_count // 4
    high = [high[u].astype(BF16) for u in range(half)]
    moved = [swap(part, "ctx", 2 * (half + u)) for u, part in enumerate(high)]

    later, sends = [], []
    for distance in doublings("ctx"):
        sends.append(send)
        later.append(swap(send, "ctx", distance))
        if distance == 1:
            later[0] = after(later[0], *high)
        sums = sums + later[-1].astype(F32)
        send = sums.astype(BF16)

    low = even_low.astype(F32) + after(low, sends[1]).astype(F32)
    moved += [swap(low[u].astype(BF16), "ctx", 2 * u) for u in range(1, half)]

    outs = [heads_out, swap(outs_out, "head", 1)]
    for part in outs_far:
        outs += [part, swap(after(part, sends[-1]), "head", 1)]
    columns = [after(c, sends[1]) for c in columns]
    crossing = jnp.stack([c[1] for c in columns])
    crossing = swap(crossing, "head", 1)
    columns = [c for s in range(head_count // 2) for c in (columns[s][0], crossing[s])]
    grad_queries, dk, dv = rest(
        keys, values, grads, last, solved, scores, weights, after(ds, sends[-1]), da, dn
    )
    layer_out = layer(outs, columns)
    grad_weight = low[0]
    for part in moved:
        grad_weight = grad_weight + after(part, layer_out).astype(F32)
    grad_keys, grad_values = finish(keys, values, dk, dv, later)
    return (layer_out, grad_queries, grad_keys, grad_values, grad_weight)


def solution(mesh):
    in_specs = (
        P("ctx", "head"),
        P("ctx", "head"),
        P("ctx", "head"),
        P("head", None),
        P("ctx", "head"),
    )
    out_specs = (
        P("ctx", "head"),
        P("ctx", "head"),
        P("ctx", "head"),
        P("ctx", "head"),
        P("head", "ctx"),
    )
    return jax.shard_map(shards, mesh=mesh, in_specs=in_specs, out_specs=out_specs, check_vma=False)
```

```python
import functools

import jax
import jax.numpy as jnp
from jax import lax
from jax.experimental import pallas as pl
from jax.experimental.pallas import tpu as pltpu
from jax.sharding import PartitionSpec as P


HDIM = 128
SPAN = 256
NEWTON = 8
RIDGE = 1.0
F32 = jnp.float32
BF16 = jnp.bfloat16
VMEM_SPEC = pl.BlockSpec(memory_space=pltpu.VMEM)
ANY_SPEC = pl.BlockSpec(memory_space=pl.ANY)


def dot(left, right, axes=(1, 0)):
    return lax.dot_general(
        left, right, (((axes[0],), (axes[1],)), ((), ())), preferred_element_type=F32
    )


def split(value):
    high = value.astype(BF16)
    return high, (value - high.astype(F32)).astype(BF16)


def cat(parts, axis):
    return jnp.concatenate(parts, axis=axis)


def params(limit=8):
    return pltpu.CompilerParams(vmem_limit_bytes=limit * 1024 * 1024)


def cost(flops, size):
    return pl.CostEstimate(flops=flops, bytes_accessed=size, transcendentals=0)


def shape(dims, dtype=F32):
    return jax.ShapeDtypeStruct(dims, dtype)


def unit():
    rows = lax.broadcasted_iota(jnp.int32, (HDIM, HDIM), 0)
    cols = lax.broadcasted_iota(jnp.int32, (HDIM, HDIM), 1)
    return rows == cols


def causal():
    rows = lax.broadcasted_iota(jnp.int32, (SPAN, SPAN), 0)
    cols = lax.broadcasted_iota(jnp.int32, (SPAN, SPAN), 1)
    return rows >= cols


def corner():
    rows = lax.broadcasted_iota(jnp.int32, (HDIM, HDIM), 0)
    cols = lax.broadcasted_iota(jnp.int32, (HDIM, HDIM), 1)
    return rows, cols


def fold(one, two):
    rows, cols = corner()
    both = jnp.where(rows <= cols, one, two)
    line = jnp.sum(jnp.where(rows == cols, two, 0.0), axis=0, keepdims=True)
    return both, jnp.broadcast_to(line, (8, HDIM))


def unfold(both, line):
    rows, cols = corner()
    turned = both.T
    one = jnp.where(rows <= cols, both, turned)
    two = jnp.where(rows > cols, both, turned)
    two = jnp.where(rows == cols, line[:1], two)
    return one, two


def folded(heads):
    return (heads + 1) // 2


def fold_into(ref, mats, base=0):
    for i in range(folded(len(mats))):
        one, two = mats[2 * i], mats[min(2 * i + 1, len(mats) - 1)]
        both, line = fold(one, two)
        top = base + i * (HDIM + 8)
        ref[top : top + HDIM, :] = both
        ref[top + HDIM : top + HDIM + 8, :] = line


def unfold_from(ref, heads, base=0):
    mats = []
    for i in range(folded(heads)):
        top = base + i * (HDIM + 8)
        mats += unfold(ref[top : top + HDIM, :], ref[top + HDIM : top + HDIM + 8, :])
    return mats[:heads]


def totals_kernel(begin_ref, k_ref, v_ref, g_ref, n_ref):
    grams = []
    for h in range(k_ref.shape[1] // HDIM):
        cols = slice(h * HDIM, (h + 1) * HDIM)
        k = k_ref[:, cols]
        both = dot(k, cat([k, v_ref[:, cols]], 1), (0, 0))
        grams.append(both[:, :HDIM])
        n_ref[cols, :] = both[:, HDIM:]
    fold_into(g_ref, grams)


def totals(begin, keys, values, heads):
    return pl.pallas_call(
        totals_kernel,
        out_shape=(shape((folded(heads) * (HDIM + 8), HDIM)), shape((heads * HDIM, HDIM))),
        in_specs=[VMEM_SPEC] * 3,
        out_specs=(VMEM_SPEC, VMEM_SPEC),
        compiler_params=params(),
        cost_estimate=cost(2 * 2 * keys.size * HDIM, 4 * keys.size),
    )(begin, keys, values)


def taken(refs, backward):
    total = None
    mine = lax.axis_index("ctx")
    for r, ref in enumerate(refs):
        bit = (mine >> r) & 1
        wanted = jnp.where(bit == (0 if backward else 1), 1.0, 0.0)
        part = ref[...].astype(F32) * wanted
        total = part if total is None else total + part
    return total


def places(q_ref, heads):
    blocks = q_ref.shape[0] // SPAN
    for h in range(heads):
        for b in range(blocks):
            yield h, b, h * blocks + b, slice(b * SPAN, (b + 1) * SPAN), slice(h * HDIM, (h + 1) * HDIM)


def inverse_kernel(rounds, k_ref, *refs):
    e_ref, x_ref, last_ref, a_ref, es, xs = refs[rounds:]
    heads = k_ref.shape[1] // HDIM
    eye = unit()
    grams = unfold_from(taken(refs[:rounds], False), heads)
    for h, b, i, rows, cols in places(k_ref, heads):
        ridged = grams[h] + jnp.where(eye, RIDGE, 0.0)
        scale = 1.0 / jnp.sqrt(jnp.sum(ridged * ridged, keepdims=True))
        a_ref[i] = ridged
        es[i] = ridged * scale
        xs[i] = jnp.where(eye, scale, 0.0)
        k = k_ref[rows, cols]
        grams[h] = grams[h] + dot(k, k, (0, 0))
    nil = jnp.zeros((HDIM, HDIM), BF16)

    def step(j, carry):
        for i in range(es.shape[0]):
            e, x = es[i], xs[i]
            eh, el = split(e)
            xh, xl = split(x)
            e_ref[j, i] = eh
            x_ref[j, i] = xh
            left = cat([cat([eh, el], 1), cat([xh, xl], 1)], 0)
            right = cat([cat([eh, el], 1), cat([eh, nil], 1)], 0)
            both = dot(left, right)
            both = both[:, :HDIM] + both[:, HDIM:]
            es[i] = 2.0 * e - both[:HDIM]
            xs[i] = 2.0 * x - both[HDIM:]
        return carry

    lax.fori_loop(0, NEWTON, step, 0)
    for i in range(xs.shape[0]):
        last_ref[i] = xs[i]


def inverses(keys, grams, count):
    stash = shape((NEWTON, count, HDIM, HDIM), BF16)
    state = shape((count, HDIM, HDIM))
    return pl.pallas_call(
        functools.partial(inverse_kernel, len(grams)),
        out_shape=(stash, stash, state, state),
        in_specs=[VMEM_SPEC] * (1 + len(grams)),
        out_specs=(VMEM_SPEC,) * 4,
        scratch_shapes=[pltpu.VMEM((count, HDIM, HDIM), F32)] * 2,
        compiler_params=params(),
        cost_estimate=cost(2_000_000_000, 8_000_000),
    )(keys, *grams)


def outputs_kernel(rounds, mark_ref, q_ref, k_ref, v_ref, last_ref, *refs):
    out_ref, pre_ref, s_ref, w_ref = refs[rounds:]
    prefix = taken(refs[:rounds], False)
    heads = q_ref.shape[1] // HDIM
    keep = causal()
    nil = jnp.zeros((HDIM, HDIM), BF16)
    pairs = [prefix[h * HDIM : (h + 1) * HDIM, :] for h in range(heads)]
    for h, b, i, rows, cols in places(q_ref, heads):
        q, k, v = q_ref[rows, cols], k_ref[rows, cols], v_ref[rows, cols]
        xh, xl = split(last_ref[i])
        sh, sl = split(dot(cat([q, q], 1), cat([xh, xl], 0)))
        both = cat([sh, sl], 1)
        s_ref[i] = both
        scores = dot(both, cat([k, k], 1), (1, 1))
        scores = jnp.where(keep, scores, 0.0).astype(BF16)
        w_ref[i] = scores
        nh, nl = split(pairs[h])
        pre_ref[i] = cat([nh, nl], 1)
        state = dot(both, cat([cat([nh, nl], 1), cat([nh, nil], 1)], 0))
        out = dot(scores, v) + state[:, :HDIM] + state[:, HDIM:]
        out_ref[rows, cols] = out.astype(BF16)
        pairs[h] = pairs[h] + dot(k, v, (0, 0))


def outputs(mark, queries, keys, values, last, pairs):
    count = last.shape[0]
    return pl.pallas_call(
        functools.partial(outputs_kernel, len(pairs)),
        out_shape=(
            shape(queries.shape, BF16),
            shape((count, HDIM, 2 * HDIM), BF16),
            shape((count, SPAN, 2 * HDIM), BF16),
            shape((count, SPAN, SPAN), BF16),
        ),
        in_specs=[VMEM_SPEC] * (5 + len(pairs)),
        out_specs=(VMEM_SPEC,) * 4,
        compiler_params=params(),
        cost_estimate=cost(2_000_000_000, 8_000_000),
    )(mark, queries, keys, values, last, *pairs)


def tangent_kernel(
    q_ref, k_ref, v_ref, do_ref, e_ref, x_ref, last_ref, a_ref, pre_ref, s_ref,
    p_ref, ds_ref, da_ref, dn_ref, sum_ref, send_ref, des, dxs, first,
):
    heads = q_ref.shape[1] // HDIM
    keep = causal()
    nil = jnp.zeros((HDIM, HDIM), BF16)
    for h, b, i, rows, cols in places(q_ref, heads):
        q, k, v, do = q_ref[rows, cols], k_ref[rows, cols], v_ref[rows, cols], do_ref[rows, cols]
        weights = jnp.where(keep, dot(do, v, (1, 1)), 0.0).astype(BF16)
        p_ref[i] = weights
        ds = dot(weights, k) + dot(cat([do, do], 1), pre_ref[i], (1, 1))
        ds = ds.astype(BF16)
        ds_ref[rows, cols] = ds
        state = dot(s_ref[i], do, (0, 0))
        dn_ref[i] = state[:HDIM] + state[HDIM:]
        bar = dot(q, ds, (0, 0))
        bar = bar + bar.T
        ridged = a_ref[i]
        scale = 1.0 / jnp.sqrt(jnp.sum(ridged * ridged, keepdims=True))
        first[i] = bar
        des[i] = bar * scale
        dxs[i] = jnp.zeros((HDIM, HDIM), F32)

    def step(j, carry):
        for i in range(des.shape[0]):
            e, x = e_ref[j, i], x_ref[j, i]
            de, dx = des[i], dxs[i]
            left = cat([cat([dx.astype(BF16), x], 1), cat([nil, e], 1)], 0)
            both = dot(left, cat([e, de.astype(BF16)], 0))
            turned = both[HDIM:]
            dxs[i] = 2.0 * dx - both[:HDIM]
            des[i] = 2.0 * de - (turned + turned.T)
        return carry

    lax.fori_loop(0, NEWTON, step, 0)
    sum_a = [jnp.zeros((HDIM, HDIM), F32) for _ in range(heads)]
    sum_n = [jnp.zeros((HDIM, HDIM), F32) for _ in range(heads)]
    for h, b, i, rows, cols in places(q_ref, heads):
        ridged, dx = a_ref[i], dxs[i]
        square = jnp.sum(ridged * ridged, keepdims=True)
        along = jnp.sum(first[i] * last_ref[i] + dx * ridged, keepdims=True)
        da = dx - (along / square) * ridged
        da_ref[i] = da
        sum_a[h] = sum_a[h] + da
        sum_n[h] = sum_n[h] + dn_ref[i]
    for h in range(heads):
        sum_ref[h * HDIM : (h + 1) * HDIM, :] = sum_n[h]
    fold_into(sum_ref, sum_a, heads * HDIM)
    send_ref[...] = sum_ref[...].astype(BF16)


def tangent(queries, keys, values, grads, stash):
    heads = queries.shape[1] // HDIM
    count = stash[-1].shape[0]
    state = shape((count, HDIM, HDIM))
    rows = heads * HDIM + folded(heads) * (HDIM + 8)
    return pl.pallas_call(
        tangent_kernel,
        out_shape=(
            shape((count, SPAN, SPAN), BF16), shape(queries.shape, BF16), state, state,
            shape((rows, HDIM)), shape((rows, HDIM), BF16),
        ),
        in_specs=[VMEM_SPEC] * 10,
        out_specs=(VMEM_SPEC,) * 6,
        scratch_shapes=[pltpu.VMEM((count, HDIM, HDIM), F32)] * 3,
        compiler_params=params(),
        cost_estimate=cost(4_000_000_000, 8_000_000),
    )(queries, keys, values, grads, *stash)


def rest_kernel(
    k_ref, v_ref, do_ref, last_ref, s_ref, w_ref, p_ref, ds_ref, da_ref, dn_ref,
    dq_hbm, dk_ref, dv_ref, dq_ref, sems,
):
    heads = k_ref.shape[1] // HDIM
    sa, sn = [None] * heads, [None] * heads
    copies = []
    for h, b, i, rows, cols in reversed(list(places(k_ref, heads))):
        k, v, do, ds = k_ref[rows, cols], v_ref[rows, cols], do_ref[rows, cols], ds_ref[rows, cols]
        dq_ref[rows, cols] = dot(cat([ds, ds], 1), cat(split(last_ref[i]), 0)).astype(BF16)
        dk = dot(p_ref[i], s_ref[i, :, :HDIM], (0, 0))
        dv = dot(w_ref[i], do, (0, 0))
        if sa[h] is None:
            sa[h], sn[h] = da_ref[i], dn_ref[i]
        else:
            nh, nl = split(sn[h])
            dk = dk + dot(k, sa[h].astype(BF16)) + dot(cat([v, v], 1), cat([nh, nl], 1), (1, 1))
            dv = dv + dot(cat([k, k], 1), cat([nh, nl], 0))
            sa[h], sn[h] = sa[h] + da_ref[i], sn[h] + dn_ref[i]
        dk_ref[rows, cols] = dk
        dv_ref[rows, cols] = dv
        copies.append(
            pltpu.make_async_copy(dq_ref.at[rows, cols], dq_hbm.at[rows, cols], sems.at[i])
        )
        copies[-1].start()
    for copy in copies:
        copy.wait()


def rest(keys, values, grads, *stash):
    wide = shape(keys.shape)
    return pl.pallas_call(
        rest_kernel,
        out_shape=(shape(keys.shape, BF16), wide, wide),
        in_specs=[VMEM_SPEC] * 10,
        out_specs=(ANY_SPEC, VMEM_SPEC, VMEM_SPEC),
        scratch_shapes=[
            pltpu.VMEM(keys.shape, BF16),
            pltpu.SemaphoreType.DMA((stash[0].shape[0],)),
        ],
        compiler_params=params(),
        cost_estimate=cost(2_000_000_000, 6_000_000),
    )(keys, values, grads, *stash)


def finish_kernel(rounds, k_ref, v_ref, dk_ref, dv_ref, *refs):
    low_ref, pieces = refs[rounds], refs[rounds + 1 : -8]
    gk_hbm, gv_hbm, gw_hbm, gk_ref, gv_ref, gw_ref, sems, gw_sem = refs[-8:]
    gw_ref[...] = low_ref[...]
    for piece in pieces:
        gw_ref[...] += piece[...].astype(F32)
    gw_copy = pltpu.make_async_copy(gw_ref, gw_hbm, gw_sem)
    gw_copy.start()
    sums = taken(refs[:rounds], True)
    heads = k_ref.shape[1] // HDIM
    nil = jnp.zeros((HDIM, HDIM), BF16)
    right = []
    for h, sa in enumerate(unfold_from(sums, heads, heads * HDIM)):
        sn = sums[h * HDIM : (h + 1) * HDIM, :]
        top = cat([sa.astype(BF16), sn.astype(BF16)], 1)
        right.append(cat([top, cat([sn.T.astype(BF16), nil], 1)], 0))
    copies = []
    for b in range(k_ref.shape[0] // SPAN):
        rows = slice(b * SPAN, (b + 1) * SPAN)
        for h in range(heads):
            cols = slice(h * HDIM, (h + 1) * HDIM)
            total = dot(cat([k_ref[rows, cols], v_ref[rows, cols]], 1), right[h])
            gk_ref[rows, cols] = (dk_ref[rows, cols] + total[:, :HDIM]).astype(BF16)
            gv_ref[rows, cols] = (dv_ref[rows, cols] + total[:, HDIM:]).astype(BF16)
        for i, (ref, hbm) in enumerate(((gk_ref, gk_hbm), (gv_ref, gv_hbm))):
            copies.append(pltpu.make_async_copy(ref.at[rows], hbm.at[rows], sems.at[b, i]))
            copies[-1].start()
    for copy in copies:
        copy.wait()
    gw_copy.wait()


def finish(keys, values, dk, dv, sums, low, pieces):
    blocks = keys.shape[0] // SPAN
    return pl.pallas_call(
        functools.partial(finish_kernel, len(sums)),
        out_shape=(shape(keys.shape, BF16),) * 2 + (shape(low.shape),),
        in_specs=[VMEM_SPEC] * (5 + len(sums) + len(pieces)),
        out_specs=(ANY_SPEC,) * 3,
        scratch_shapes=[pltpu.VMEM(keys.shape, BF16)] * 2
        + [pltpu.VMEM(low.shape, F32)]
        + [pltpu.SemaphoreType.DMA((blocks, 2)), pltpu.SemaphoreType.DMA(())],
        compiler_params=params(),
        cost_estimate=cost(1_000_000_000, 6_000_000),
    )(keys, values, dk, dv, *sums, low, *pieces)


def lead_kernel(*refs):
    refs[-1][...] = jnp.zeros_like(refs[-1])


def lead(flops, *behind):
    return pl.pallas_call(
        lead_kernel,
        out_shape=shape((8, HDIM)),
        in_specs=[VMEM_SPEC] * len(behind),
        out_specs=VMEM_SPEC,
        compiler_params=params(),
        cost_estimate=cost(flops, 4096),
    )(*behind)


def grads_kernel(first, w_ref, *refs):
    out_ref = refs[-1]
    me = lax.axis_index("head")
    total = refs[0][...] if first else None
    for s, part in enumerate(refs[1:-1] if first else refs[:-1]):
        width = part.shape[1]
        cols = pl.ds(pl.multiple_of((me ^ (first + s)) * width, width), width)
        term = dot(part[...], w_ref[:, cols], (1, 1))
        total = term if total is None else total + term
    out_ref[...] = total.astype(out_ref.dtype)


def head_grads(w_out, parts, first, begun=None):
    rows = parts[0].shape[0]
    begun = [] if begun is None else [begun]
    return pl.pallas_call(
        functools.partial(grads_kernel, first),
        out_shape=shape((rows, w_out.shape[0]), BF16 if begun else F32),
        in_specs=[VMEM_SPEC] * (1 + len(parts) + len(begun)),
        out_specs=VMEM_SPEC,
        compiler_params=params(),
        cost_estimate=cost(rows * w_out.size, 4_000_000),
    )(w_out, *begun, *parts)


def columns_kernel(w_ref, *refs):
    me = lax.axis_index("head")
    for s, out_ref in enumerate(refs):
        width = out_ref.shape[2]
        for f in range(2):
            target = me ^ (2 * s + f)
            cols = pl.ds(pl.multiple_of(target * width, width), width)
            out_ref[f] = w_ref[:, cols]


def column_pieces(w_out, count):
    piece = shape((2, w_out.shape[0], w_out.shape[1] // count), BF16)
    return pl.pallas_call(
        columns_kernel,
        out_shape=(piece,) * (count // 2),
        in_specs=[VMEM_SPEC],
        out_specs=(VMEM_SPEC,) * (count // 2),
        compiler_params=params(),
        cost_estimate=cost(0, 4 * w_out.size),
    )(w_out)


def weights_kernel(h_ref, *refs):
    parts, outs, all_ref = refs[:-5], refs[-5:-1], refs[-1]
    me, mine = lax.axis_index("head"), lax.axis_index("ctx")
    count, _, width = all_ref.shape
    fold = parts[0].shape[1] // width
    for s, part in enumerate(parts):
        term = dot(h_ref[...], part[...], (0, 0)).astype(BF16)
        for f in range(fold):
            target = (me ^ s) * fold + f
            all_ref[target ^ mine] = term[:, f * width : (f + 1) * width]
    for t in range(count):
        ref = outs[2 * (t % 2) + (t >= count // 2)]
        ref[t % (count // 2) // 2] = all_ref[t]


def weight_terms(heads_out, parts, count):
    feats = sum(part.shape[1] for part in parts)
    piece = (heads_out.shape[1], feats // count)
    return pl.pallas_call(
        weights_kernel,
        out_shape=(shape((count // 4,) + piece, BF16),) * 4,
        in_specs=[VMEM_SPEC] * (1 + len(parts)),
        out_specs=(VMEM_SPEC,) * 4,
        scratch_shapes=[pltpu.VMEM((count,) + piece, BF16)],
        compiler_params=params(),
        cost_estimate=cost(2 * heads_out.size * feats, 6_000_000),
    )(heads_out, *parts)


def layer_kernel(*refs):
    hbm, ref, sems = refs[-3:]
    count = (len(refs) - 3) // 2
    step = ref.shape[0] // sems.shape[0]
    copies = []
    for b in range(sems.shape[0]):
        rows = slice(b * step, (b + 1) * step)
        total = None
        for s in range(count):
            term = dot(refs[s][rows, :], refs[count + s][...])
            total = term if total is None else total + term
        ref[rows, :] = total.astype(BF16)
        copies.append(pltpu.make_async_copy(ref.at[rows], hbm.at[rows], sems.at[b]))
        copies[-1].start()
    for copy in copies:
        copy.wait()


def layer(parts, columns):
    rows, cols = parts[0].shape[0], columns[0].shape[1]
    return pl.pallas_call(
        layer_kernel,
        out_shape=shape((rows, cols), BF16),
        in_specs=[VMEM_SPEC] * (len(parts) + len(columns)),
        out_specs=ANY_SPEC,
        scratch_shapes=[pltpu.VMEM((rows, cols), BF16), pltpu.SemaphoreType.DMA((4,))],
        compiler_params=params(),
        cost_estimate=cost(2 * rows * cols * sum(p.shape[1] for p in parts), 6_000_000),
    )(*parts, *columns)


def swap(value, axis, distance):
    count = lax.axis_size(axis)
    return lax.ppermute(value, axis, [(i, i ^ distance) for i in range(count)])


def after(value, *others):
    return lax.optimization_barrier((value,) + others)[0]


def doublings(axis):
    return [1 << i for i in range((lax.axis_size(axis) - 1).bit_length())]


def shards(queries, keys, values, w_out, cotangent):
    heads = queries.shape[1] // HDIM
    count = heads * (queries.shape[0] // SPAN)
    head_count, ctx_count = lax.axis_size("head"), lax.axis_size("ctx")
    evens = range(2, head_count, 2)

    far = {s: swap(cotangent, "head", s) for s in evens}
    begin = lead(700_000_000)
    gram, pair = totals(begin, keys, values, heads)
    near = swap(after(cotangent, gram, pair), "head", 1)

    grams, pairs = [], []
    begun = None
    rounds = doublings("ctx")
    for r, distance in enumerate(rounds):
        grams.append(swap(gram, "ctx", distance))
        if begun is None:
            begun = head_grads(w_out, [cotangent, near], 0)
        if distance != rounds[-1]:
            gram = gram + grams[-1]
        if r:
            pairs[-1] = after(pairs[-1], gram)
            pair = pair + pairs[-1].astype(F32)
        pairs.append(swap(pair.astype(BF16), "ctx", distance))
    grams[-1] = after(grams[-1], begun)
    *stash, last, ridged = inverses(keys, grams, count)
    pairs[-1] = after(pairs[-1], last)
    parts = []
    for s in evens:
        parts += [far[s], swap(after(far[s], pairs[-1]), "head", 1)]
    columns = column_pieces(after(w_out, begun), head_count)
    columns = [after(c, pairs[-1]) for c in columns]
    columns = [swap(c, "head", 2 * s) if s else c for s, c in enumerate(columns)]
    mark = lead(1000, last)
    heads_out, states, solved, scores = outputs(mark, queries, keys, values, last, pairs)

    grads = head_grads(w_out, parts, 2, after(begun, heads_out))
    parts = [cotangent, near] + parts
    even_low, even_high, odd_low, odd_high = weight_terms(
        after(heads_out, grads), parts, ctx_count
    )
    high = swap(odd_high, "ctx", 1)

    weights, ds, da, dn, sums, send = tangent(
        queries, keys, values, after(grads, odd_low), [*stash, last, ridged, states, solved]
    )

    low = swap(after(odd_low, send), "ctx", 1)
    outs_out = after(heads_out, send)
    outs_far = [swap(outs_out, "head", s) for s in evens]
    high = even_high.astype(F32) + after(high, send).astype(F32)
    half = ctx_count // 4
    high = [high[u].astype(BF16) for u in range(half)]
    moved = [swap(part, "ctx", 2 * (half + u)) for u, part in enumerate(high)]

    later, sends = [], []
    for distance in doublings("ctx"):
        sends.append(send)
        later.append(swap(send, "ctx", distance))
        if distance == 1:
            later[0] = after(later[0], *high)
        sums = sums + later[-1].astype(F32)
        send = sums.astype(BF16)

    low = even_low.astype(F32) + after(low, sends[1]).astype(F32)
    moved += [swap(low[u].astype(BF16), "ctx", 2 * u) for u in range(1, half)]
    grad_queries, dk, dv = rest(
        keys, values, grads, last, solved, scores, weights, after(ds, low), da, dn
    )

    outs = [heads_out, swap(outs_out, "head", 1)]
    for part in outs_far:
        outs += [part, swap(after(part, sends[-1]), "head", 1)]
    columns = [after(c, sends[1]) for c in columns]
    crossing = jnp.stack([c[1] for c in columns])
    crossing = swap(crossing, "head", 1)
    columns = [c for s in range(head_count // 2) for c in (columns[s][0], crossing[s])]
    layer_out = layer(outs, columns)
    moved = [after(part, layer_out) for part in moved]
    grad_keys, grad_values, grad_weight = finish(keys, values, dk, dv, later, low[0], moved)
    return (layer_out, grad_queries, grad_keys, grad_values, grad_weight)


def solution(mesh):
    in_specs = (
        P("ctx", "head"),
        P("ctx", "head"),
        P("ctx", "head"),
        P("head", None),
        P("ctx", "head"),
    )
    out_specs = (
        P("ctx", "head"),
        P("ctx", "head"),
        P("ctx", "head"),
        P("ctx", "head"),
        P("head", "ctx"),
    )
    return jax.shard_map(shards, mesh=mesh, in_specs=in_specs, out_specs=out_specs, check_vma=False)
```

```python
import functools

import jax
import jax.numpy as jnp
from jax import lax
from jax.experimental import pallas as pl
from jax.experimental.pallas import tpu as pltpu
from jax.sharding import PartitionSpec as P


HDIM = 128
SPAN = 256
NEWTON = 8
RIDGE = 1.0
F32 = jnp.float32
BF16 = jnp.bfloat16
VMEM_SPEC = pl.BlockSpec(memory_space=pltpu.VMEM)
ANY_SPEC = pl.BlockSpec(memory_space=pl.ANY)


def dot(left, right, axes=(1, 0)):
    return lax.dot_general(
        left, right, (((axes[0],), (axes[1],)), ((), ())), preferred_element_type=F32
    )


def split(value):
    high = value.astype(BF16)
    return high, (value - high.astype(F32)).astype(BF16)


def cat(parts, axis):
    return jnp.concatenate(parts, axis=axis)


def params(limit=8):
    return pltpu.CompilerParams(vmem_limit_bytes=limit * 1024 * 1024)


def cost(flops, size):
    return pl.CostEstimate(flops=flops, bytes_accessed=size, transcendentals=0)


def shape(dims, dtype=F32):
    return jax.ShapeDtypeStruct(dims, dtype)


def unit():
    rows = lax.broadcasted_iota(jnp.int32, (HDIM, HDIM), 0)
    cols = lax.broadcasted_iota(jnp.int32, (HDIM, HDIM), 1)
    return rows == cols


def causal():
    rows = lax.broadcasted_iota(jnp.int32, (SPAN, SPAN), 0)
    cols = lax.broadcasted_iota(jnp.int32, (SPAN, SPAN), 1)
    return rows >= cols


def corner():
    rows = lax.broadcasted_iota(jnp.int32, (HDIM, HDIM), 0)
    cols = lax.broadcasted_iota(jnp.int32, (HDIM, HDIM), 1)
    return rows, cols


def fold(one, two):
    rows, cols = corner()
    both = jnp.where(rows <= cols, one, two)
    line = jnp.sum(jnp.where(rows == cols, two, 0.0), axis=0, keepdims=True)
    return both, jnp.broadcast_to(line, (8, HDIM))


def unfold(both, line):
    rows, cols = corner()
    turned = both.T
    one = jnp.where(rows <= cols, both, turned)
    two = jnp.where(rows > cols, both, turned)
    two = jnp.where(rows == cols, line[:1], two)
    return one, two


def folded(heads):
    return (heads + 1) // 2


def fold_into(ref, mats, base=0):
    for i in range(folded(len(mats))):
        one, two = mats[2 * i], mats[min(2 * i + 1, len(mats) - 1)]
        both, line = fold(one, two)
        top = base + i * (HDIM + 8)
        ref[top : top + HDIM, :] = both
        ref[top + HDIM : top + HDIM + 8, :] = line


def unfold_from(ref, heads, base=0):
    mats = []
    for i in range(folded(heads)):
        top = base + i * (HDIM + 8)
        mats += unfold(ref[top : top + HDIM, :], ref[top + HDIM : top + HDIM + 8, :])
    return mats[:heads]


def totals_kernel(begin_ref, k_ref, v_ref, g_ref, n_ref):
    grams = []
    for h in range(k_ref.shape[1] // HDIM):
        cols = slice(h * HDIM, (h + 1) * HDIM)
        k = k_ref[:, cols]
        both = dot(k, cat([k, v_ref[:, cols]], 1), (0, 0))
        grams.append(both[:, :HDIM])
        n_ref[cols, :] = both[:, HDIM:]
    fold_into(g_ref, grams)


def totals(begin, keys, values, heads):
    return pl.pallas_call(
        totals_kernel,
        out_shape=(shape((folded(heads) * (HDIM + 8), HDIM)), shape((heads * HDIM, HDIM))),
        in_specs=[VMEM_SPEC] * 3,
        out_specs=(VMEM_SPEC, VMEM_SPEC),
        compiler_params=params(),
        cost_estimate=cost(2 * 2 * keys.size * HDIM, 4 * keys.size),
    )(begin, keys, values)


def taken(refs, backward):
    total = None
    mine = lax.axis_index("ctx")
    for r, ref in enumerate(refs):
        bit = (mine >> r) & 1
        wanted = jnp.where(bit == (0 if backward else 1), 1.0, 0.0)
        part = ref[...].astype(F32) * wanted
        total = part if total is None else total + part
    return total


def places(q_ref, heads):
    blocks = q_ref.shape[0] // SPAN
    for h in range(heads):
        for b in range(blocks):
            yield h, b, h * blocks + b, slice(b * SPAN, (b + 1) * SPAN), slice(h * HDIM, (h + 1) * HDIM)


def inverse_kernel(rounds, k_ref, *refs):
    e_ref, x_ref, last_ref, a_ref, es, xs = refs[rounds:]
    heads = k_ref.shape[1] // HDIM
    eye = unit()
    grams = unfold_from(taken(refs[:rounds], False), heads)
    for h, b, i, rows, cols in places(k_ref, heads):
        ridged = grams[h] + jnp.where(eye, RIDGE, 0.0)
        scale = 1.0 / jnp.sqrt(jnp.sum(ridged * ridged, keepdims=True))
        a_ref[i] = ridged
        es[i] = ridged * scale
        xs[i] = jnp.where(eye, scale, 0.0)
        k = k_ref[rows, cols]
        grams[h] = grams[h] + dot(k, k, (0, 0))
    nil = jnp.zeros((HDIM, HDIM), BF16)

    def step(j, carry):
        for i in range(es.shape[0]):
            e, x = es[i], xs[i]
            eh, el = split(e)
            xh, xl = split(x)
            e_ref[j, i] = eh
            x_ref[j, i] = xh
            left = cat([cat([eh, el], 1), cat([xh, xl], 1)], 0)
            right = cat([cat([eh, el], 1), cat([eh, nil], 1)], 0)
            both = dot(left, right)
            both = both[:, :HDIM] + both[:, HDIM:]
            es[i] = 2.0 * e - both[:HDIM]
            xs[i] = 2.0 * x - both[HDIM:]
        return carry

    lax.fori_loop(0, NEWTON, step, 0)
    for i in range(xs.shape[0]):
        last_ref[i] = xs[i]


def inverses(keys, grams, count):
    stash = shape((NEWTON, count, HDIM, HDIM), BF16)
    state = shape((count, HDIM, HDIM))
    return pl.pallas_call(
        functools.partial(inverse_kernel, len(grams)),
        out_shape=(stash, stash, state, state),
        in_specs=[VMEM_SPEC] * (1 + len(grams)),
        out_specs=(VMEM_SPEC,) * 4,
        scratch_shapes=[pltpu.VMEM((count, HDIM, HDIM), F32)] * 2,
        compiler_params=params(),
        cost_estimate=cost(2_000_000_000, 8_000_000),
    )(keys, *grams)


def outputs_kernel(rounds, mark_ref, q_ref, k_ref, v_ref, last_ref, *refs):
    out_ref, pre_ref, s_ref, w_ref = refs[rounds:]
    prefix = taken(refs[:rounds], False)
    heads = q_ref.shape[1] // HDIM
    keep = causal()
    nil = jnp.zeros((HDIM, HDIM), BF16)
    pairs = [prefix[h * HDIM : (h + 1) * HDIM, :] for h in range(heads)]
    for h, b, i, rows, cols in places(q_ref, heads):
        q, k, v = q_ref[rows, cols], k_ref[rows, cols], v_ref[rows, cols]
        xh, xl = split(last_ref[i])
        sh, sl = split(dot(cat([q, q], 1), cat([xh, xl], 0)))
        both = cat([sh, sl], 1)
        s_ref[i] = both
        scores = dot(both, cat([k, k], 1), (1, 1))
        scores = jnp.where(keep, scores, 0.0).astype(BF16)
        w_ref[i] = scores
        nh, nl = split(pairs[h])
        pre_ref[i] = cat([nh, nl], 1)
        state = dot(both, cat([cat([nh, nl], 1), cat([nh, nil], 1)], 0))
        out = dot(scores, v) + state[:, :HDIM] + state[:, HDIM:]
        out_ref[rows, cols] = out.astype(BF16)
        pairs[h] = pairs[h] + dot(k, v, (0, 0))


def outputs(mark, queries, keys, values, last, pairs):
    count = last.shape[0]
    return pl.pallas_call(
        functools.partial(outputs_kernel, len(pairs)),
        out_shape=(
            shape(queries.shape, BF16),
            shape((count, HDIM, 2 * HDIM), BF16),
            shape((count, SPAN, 2 * HDIM), BF16),
            shape((count, SPAN, SPAN), BF16),
        ),
        in_specs=[VMEM_SPEC] * (5 + len(pairs)),
        out_specs=(VMEM_SPEC,) * 4,
        compiler_params=params(),
        cost_estimate=cost(2_000_000_000, 8_000_000),
    )(mark, queries, keys, values, last, *pairs)


def tangent_kernel(
    q_ref, k_ref, v_ref, do_ref, e_ref, x_ref, last_ref, a_ref, pre_ref, s_ref,
    p_ref, ds_ref, da_ref, dn_ref, sum_ref, send_ref, des, dxs, first,
):
    heads = q_ref.shape[1] // HDIM
    keep = causal()
    nil = jnp.zeros((HDIM, HDIM), BF16)
    for h, b, i, rows, cols in places(q_ref, heads):
        q, k, v, do = q_ref[rows, cols], k_ref[rows, cols], v_ref[rows, cols], do_ref[rows, cols]
        weights = jnp.where(keep, dot(do, v, (1, 1)), 0.0).astype(BF16)
        p_ref[i] = weights
        ds = dot(weights, k) + dot(cat([do, do], 1), pre_ref[i], (1, 1))
        ds = ds.astype(BF16)
        ds_ref[rows, cols] = ds
        state = dot(s_ref[i], do, (0, 0))
        dn_ref[i] = state[:HDIM] + state[HDIM:]
        bar = dot(q, ds, (0, 0))
        bar = bar + bar.T
        ridged = a_ref[i]
        scale = 1.0 / jnp.sqrt(jnp.sum(ridged * ridged, keepdims=True))
        first[i] = bar
        des[i] = bar * scale
        dxs[i] = jnp.zeros((HDIM, HDIM), F32)

    def step(j, carry):
        for i in range(des.shape[0]):
            e, x = e_ref[j, i], x_ref[j, i]
            de, dx = des[i], dxs[i]
            left = cat([cat([dx.astype(BF16), x], 1), cat([nil, e], 1)], 0)
            both = dot(left, cat([e, de.astype(BF16)], 0))
            turned = both[HDIM:]
            dxs[i] = 2.0 * dx - both[:HDIM]
            des[i] = 2.0 * de - (turned + turned.T)
        return carry

    lax.fori_loop(0, NEWTON, step, 0)
    sum_a = [jnp.zeros((HDIM, HDIM), F32) for _ in range(heads)]
    sum_n = [jnp.zeros((HDIM, HDIM), F32) for _ in range(heads)]
    for h, b, i, rows, cols in places(q_ref, heads):
        ridged, dx = a_ref[i], dxs[i]
        square = jnp.sum(ridged * ridged, keepdims=True)
        along = jnp.sum(first[i] * last_ref[i] + dx * ridged, keepdims=True)
        da = dx - (along / square) * ridged
        da_ref[i] = da
        sum_a[h] = sum_a[h] + da
        sum_n[h] = sum_n[h] + dn_ref[i]
    for h in range(heads):
        sum_ref[h * HDIM : (h + 1) * HDIM, :] = sum_n[h]
    fold_into(sum_ref, sum_a, heads * HDIM)
    send_ref[...] = sum_ref[...].astype(BF16)


def tangent(queries, keys, values, grads, stash):
    heads = queries.shape[1] // HDIM
    count = stash[-1].shape[0]
    state = shape((count, HDIM, HDIM))
    rows = heads * HDIM + folded(heads) * (HDIM + 8)
    return pl.pallas_call(
        tangent_kernel,
        out_shape=(
            shape((count, SPAN, SPAN), BF16), shape(queries.shape, BF16), state, state,
            shape((rows, HDIM)), shape((rows, HDIM), BF16),
        ),
        in_specs=[VMEM_SPEC] * 10,
        out_specs=(VMEM_SPEC,) * 6,
        scratch_shapes=[pltpu.VMEM((count, HDIM, HDIM), F32)] * 3,
        compiler_params=params(),
        cost_estimate=cost(4_000_000_000, 8_000_000),
    )(queries, keys, values, grads, *stash)


def rest_kernel(
    early_ref, k_ref, v_ref, do_ref, last_ref, s_ref, w_ref, p_ref, ds_ref, da_ref, dn_ref,
    dq_hbm, dk_ref, dv_ref, dq_ref, sems,
):
    heads = k_ref.shape[1] // HDIM
    sa, sn = [None] * heads, [None] * heads
    copies = []
    for h, b, i, rows, cols in reversed(list(places(k_ref, heads))):
        k, v, do, ds = k_ref[rows, cols], v_ref[rows, cols], do_ref[rows, cols], ds_ref[rows, cols]
        dq_ref[rows, cols] = dot(cat([ds, ds], 1), cat(split(last_ref[i]), 0)).astype(BF16)
        dk = dot(p_ref[i], s_ref[i, :, :HDIM], (0, 0))
        dv = dot(w_ref[i], do, (0, 0))
        if sa[h] is None:
            sa[h], sn[h] = da_ref[i], dn_ref[i]
        else:
            nh, nl = split(sn[h])
            dk = dk + dot(k, sa[h].astype(BF16)) + dot(cat([v, v], 1), cat([nh, nl], 1), (1, 1))
            dv = dv + dot(cat([k, k], 1), cat([nh, nl], 0))
            sa[h], sn[h] = sa[h] + da_ref[i], sn[h] + dn_ref[i]
        dk_ref[rows, cols] = dk
        dv_ref[rows, cols] = dv
        copies.append(
            pltpu.make_async_copy(dq_ref.at[rows, cols], dq_hbm.at[rows, cols], sems.at[i])
        )
        copies[-1].start()
    for copy in copies:
        copy.wait()


def rest(early, keys, values, grads, *stash):
    wide = shape(keys.shape)
    return pl.pallas_call(
        rest_kernel,
        out_shape=(shape(keys.shape, BF16), wide, wide),
        in_specs=[VMEM_SPEC] * 11,
        out_specs=(ANY_SPEC, VMEM_SPEC, VMEM_SPEC),
        scratch_shapes=[
            pltpu.VMEM(keys.shape, BF16),
            pltpu.SemaphoreType.DMA((stash[0].shape[0],)),
        ],
        compiler_params=params(),
        cost_estimate=cost(2_000_000_000, 6_000_000),
    )(early, keys, values, grads, *stash)


def finish_kernel(rounds, k_ref, v_ref, dk_ref, dv_ref, *refs):
    low_ref, pieces = refs[rounds], refs[rounds + 1 : -8]
    gk_hbm, gv_hbm, gw_hbm, gk_ref, gv_ref, gw_ref, sems, gw_sem = refs[-8:]
    gw_ref[...] = low_ref[...]
    for piece in pieces:
        gw_ref[...] += piece[...].astype(F32)
    gw_copy = pltpu.make_async_copy(gw_ref, gw_hbm, gw_sem)
    gw_copy.start()
    sums = taken(refs[:rounds], True)
    heads = k_ref.shape[1] // HDIM
    nil = jnp.zeros((HDIM, HDIM), BF16)
    right = []
    for h, sa in enumerate(unfold_from(sums, heads, heads * HDIM)):
        sn = sums[h * HDIM : (h + 1) * HDIM, :]
        top = cat([sa.astype(BF16), sn.astype(BF16)], 1)
        right.append(cat([top, cat([sn.T.astype(BF16), nil], 1)], 0))
    copies = []
    for b in range(k_ref.shape[0] // SPAN):
        rows = slice(b * SPAN, (b + 1) * SPAN)
        for h in range(heads):
            cols = slice(h * HDIM, (h + 1) * HDIM)
            total = dot(cat([k_ref[rows, cols], v_ref[rows, cols]], 1), right[h])
            gk_ref[rows, cols] = (dk_ref[rows, cols] + total[:, :HDIM]).astype(BF16)
            gv_ref[rows, cols] = (dv_ref[rows, cols] + total[:, HDIM:]).astype(BF16)
        for i, (ref, hbm) in enumerate(((gk_ref, gk_hbm), (gv_ref, gv_hbm))):
            copies.append(pltpu.make_async_copy(ref.at[rows], hbm.at[rows], sems.at[b, i]))
            copies[-1].start()
    for copy in copies:
        copy.wait()
    gw_copy.wait()


def finish(keys, values, dk, dv, sums, low, pieces):
    blocks = keys.shape[0] // SPAN
    return pl.pallas_call(
        functools.partial(finish_kernel, len(sums)),
        out_shape=(shape(keys.shape, BF16),) * 2 + (shape(low.shape),),
        in_specs=[VMEM_SPEC] * (5 + len(sums) + len(pieces)),
        out_specs=(ANY_SPEC,) * 3,
        scratch_shapes=[pltpu.VMEM(keys.shape, BF16)] * 2
        + [pltpu.VMEM(low.shape, F32)]
        + [pltpu.SemaphoreType.DMA((blocks, 2)), pltpu.SemaphoreType.DMA(())],
        compiler_params=params(),
        cost_estimate=cost(1_000_000_000, 6_000_000),
    )(keys, values, dk, dv, *sums, low, *pieces)


def lead_kernel(*refs):
    refs[-1][...] = jnp.zeros_like(refs[-1])


def lead(flops, *behind):
    return pl.pallas_call(
        lead_kernel,
        out_shape=shape((8, HDIM)),
        in_specs=[VMEM_SPEC] * len(behind),
        out_specs=VMEM_SPEC,
        compiler_params=params(),
        cost_estimate=cost(flops, 4096),
    )(*behind)


def grads_kernel(first, w_ref, *refs):
    out_ref = refs[-1]
    me = lax.axis_index("head")
    total = refs[0][...] if first else None
    for s, part in enumerate(refs[1:-1] if first else refs[:-1]):
        width = part.shape[1]
        cols = pl.ds(pl.multiple_of((me ^ (first + s)) * width, width), width)
        term = dot(part[...], w_ref[:, cols], (1, 1))
        total = term if total is None else total + term
    out_ref[...] = total.astype(out_ref.dtype)


def head_grads(w_out, parts, first, begun=None):
    rows = parts[0].shape[0]
    begun = [] if begun is None else [begun]
    return pl.pallas_call(
        functools.partial(grads_kernel, first),
        out_shape=shape((rows, w_out.shape[0]), BF16 if begun else F32),
        in_specs=[VMEM_SPEC] * (1 + len(parts) + len(begun)),
        out_specs=VMEM_SPEC,
        compiler_params=params(),
        cost_estimate=cost(rows * w_out.size, 4_000_000),
    )(w_out, *begun, *parts)


def columns_kernel(w_ref, *refs):
    me = lax.axis_index("head")
    for s, out_ref in enumerate(refs):
        width = out_ref.shape[2]
        for f in range(2):
            target = me ^ (2 * s + f)
            cols = pl.ds(pl.multiple_of(target * width, width), width)
            out_ref[f] = w_ref[:, cols]


def column_pieces(w_out, count):
    piece = shape((2, w_out.shape[0], w_out.shape[1] // count), BF16)
    return pl.pallas_call(
        columns_kernel,
        out_shape=(piece,) * (count // 2),
        in_specs=[VMEM_SPEC],
        out_specs=(VMEM_SPEC,) * (count // 2),
        compiler_params=params(),
        cost_estimate=cost(0, 4 * w_out.size),
    )(w_out)


def weights_kernel(h_ref, *refs):
    parts, outs, all_ref = refs[:-5], refs[-5:-1], refs[-1]
    me, mine = lax.axis_index("head"), lax.axis_index("ctx")
    count, _, width = all_ref.shape
    fold = parts[0].shape[1] // width
    for s, part in enumerate(parts):
        term = dot(h_ref[...], part[...], (0, 0)).astype(BF16)
        for f in range(fold):
            target = (me ^ s) * fold + f
            all_ref[target ^ mine] = term[:, f * width : (f + 1) * width]
    for t in range(count):
        ref = outs[2 * (t % 2) + (t >= count // 2)]
        ref[t % (count // 2) // 2] = all_ref[t]


def weight_terms(heads_out, parts, count):
    feats = sum(part.shape[1] for part in parts)
    piece = (heads_out.shape[1], feats // count)
    return pl.pallas_call(
        weights_kernel,
        out_shape=(shape((count // 4,) + piece, BF16),) * 4,
        in_specs=[VMEM_SPEC] * (1 + len(parts)),
        out_specs=(VMEM_SPEC,) * 4,
        scratch_shapes=[pltpu.VMEM((count,) + piece, BF16)],
        compiler_params=params(),
        cost_estimate=cost(2 * heads_out.size * feats, 6_000_000),
    )(heads_out, *parts)


def layer_kernel(mark_ref, *refs):
    hbm, ref, sems = refs[-3:]
    count = (len(refs) - 3) // 2
    step = ref.shape[0] // sems.shape[0]
    copies = []
    for b in range(sems.shape[0]):
        rows = slice(b * step, (b + 1) * step)
        total = None
        for s in range(count):
            term = dot(refs[s][rows, :], refs[count + s][...])
            total = term if total is None else total + term
        ref[rows, :] = total.astype(BF16)
        copies.append(pltpu.make_async_copy(ref.at[rows], hbm.at[rows], sems.at[b]))
        copies[-1].start()
    for copy in copies:
        copy.wait()


def layer(mark, parts, columns):
    rows, cols = parts[0].shape[0], columns[0].shape[1]
    return pl.pallas_call(
        layer_kernel,
        out_shape=shape((rows, cols), BF16),
        in_specs=[VMEM_SPEC] * (1 + len(parts) + len(columns)),
        out_specs=ANY_SPEC,
        scratch_shapes=[pltpu.VMEM((rows, cols), BF16), pltpu.SemaphoreType.DMA((4,))],
        compiler_params=params(),
        cost_estimate=cost(2 * rows * cols * sum(p.shape[1] for p in parts), 6_000_000),
    )(mark, *parts, *columns)


def swap(value, axis, distance):
    count = lax.axis_size(axis)
    return lax.ppermute(value, axis, [(i, i ^ distance) for i in range(count)])


def after(value, *others):
    return lax.optimization_barrier((value,) + others)[0]


def doublings(axis):
    return [1 << i for i in range((lax.axis_size(axis) - 1).bit_length())]


def shards(queries, keys, values, w_out, cotangent):
    heads = queries.shape[1] // HDIM
    count = heads * (queries.shape[0] // SPAN)
    head_count, ctx_count = lax.axis_size("head"), lax.axis_size("ctx")
    evens = range(2, head_count, 2)

    far = {s: swap(cotangent, "head", s) for s in evens}
    begin = lead(700_000_000)
    gram, pair = totals(begin, keys, values, heads)
    near = swap(after(cotangent, gram, pair), "head", 1)

    grams, pairs = [], []
    begun = None
    rounds = doublings("ctx")
    for r, distance in enumerate(rounds):
        grams.append(swap(gram, "ctx", distance))
        if begun is None:
            begun = head_grads(w_out, [cotangent, near], 0)
        if distance != rounds[-1]:
            gram = gram + grams[-1]
        if r:
            pairs[-1] = after(pairs[-1], gram)
            pair = pair + pairs[-1].astype(F32)
        pairs.append(swap(pair.astype(BF16), "ctx", distance))
    grams[-1] = after(grams[-1], begun)
    *stash, last, ridged = inverses(keys, grams, count)
    pairs[-1] = after(pairs[-1], last)
    parts = []
    for s in evens:
        parts += [far[s], swap(after(far[s], pairs[-1]), "head", 1)]
    columns = column_pieces(after(w_out, begun), head_count)
    columns = [after(c, pairs[-1]) for c in columns]
    columns = [swap(c, "head", 2 * s) if s else c for s, c in enumerate(columns)]
    mark = lead(1000, last)
    heads_out, states, solved, scores = outputs(mark, queries, keys, values, last, pairs)

    even_low, even_high, odd_low, odd_high = weight_terms(
        heads_out, [cotangent, near] + parts, ctx_count
    )
    high = swap(odd_high, "ctx", 1)
    grads = head_grads(w_out, parts, 2, after(begun, odd_low))

    weights, ds, da, dn, sums, send = tangent(
        queries, keys, values, grads, [*stash, last, ridged, states, solved]
    )

    low = swap(after(odd_low, send), "ctx", 1)
    outs_out = after(heads_out, send)
    outs_far = [swap(outs_out, "head", s) for s in evens]
    high = even_high.astype(F32) + after(high, send).astype(F32)
    half = ctx_count // 4
    high = [high[u].astype(BF16) for u in range(half)]
    moved = [swap(part, "ctx", 2 * (half + u)) for u, part in enumerate(high)]

    early = lead(1000, send)
    later, sends = [], []
    for distance in doublings("ctx"):
        sends.append(send)
        later.append(swap(send, "ctx", distance))
        if distance == 1:
            later[0] = after(later[0], *high)
        sums = sums + later[-1].astype(F32)
        send = sums.astype(BF16)

    grad_queries, dk, dv = rest(
        early, keys, values, grads, last, solved, scores, weights, after(ds, sends[1]), da, dn
    )

    mark = lead(1000, sends[-1])
    low = even_low.astype(F32) + after(low, sends[-1]).astype(F32)
    moved += [swap(low[u].astype(BF16), "ctx", 2 * u) for u in range(1, half)]
    outs = [heads_out, swap(outs_out, "head", 1)]
    for part in outs_far:
        outs += [part, swap(after(part, sends[1]), "head", 1)]
    columns = [after(c, sends[1]) for c in columns]
    crossing = jnp.stack([c[1] for c in columns])
    crossing = swap(crossing, "head", 1)
    columns = [c for s in range(head_count // 2) for c in (columns[s][0], crossing[s])]
    layer_out = layer(mark, outs, columns)
    moved = [after(part, layer_out) for part in moved]
    grad_keys, grad_values, grad_weight = finish(keys, values, dk, dv, later, low[0], moved)
    return (layer_out, grad_queries, grad_keys, grad_values, grad_weight)


def solution(mesh):
    in_specs = (
        P("ctx", "head"),
        P("ctx", "head"),
        P("ctx", "head"),
        P("head", None),
        P("ctx", "head"),
    )
    out_specs = (
        P("ctx", "head"),
        P("ctx", "head"),
        P("ctx", "head"),
        P("ctx", "head"),
        P("head", "ctx"),
    )
    return jax.shard_map(shards, mesh=mesh, in_specs=in_specs, out_specs=out_specs, check_vma=False)
```

```python
import functools

import jax
import jax.numpy as jnp
from jax import lax
from jax.experimental import pallas as pl
from jax.experimental.pallas import tpu as pltpu
from jax.sharding import PartitionSpec as P


HDIM = 128
SPAN = 256
NEWTON = 8
RIDGE = 1.0
F32 = jnp.float32
BF16 = jnp.bfloat16
VMEM_SPEC = pl.BlockSpec(memory_space=pltpu.VMEM)
ANY_SPEC = pl.BlockSpec(memory_space=pl.ANY)


def dot(left, right, axes=(1, 0)):
    return lax.dot_general(
        left, right, (((axes[0],), (axes[1],)), ((), ())), preferred_element_type=F32
    )


def split(value):
    high = value.astype(BF16)
    return high, (value - high.astype(F32)).astype(BF16)


def cat(parts, axis):
    return jnp.concatenate(parts, axis=axis)


def params(limit=8):
    return pltpu.CompilerParams(vmem_limit_bytes=limit * 1024 * 1024)


def cost(flops, size):
    return pl.CostEstimate(flops=flops, bytes_accessed=size, transcendentals=0)


def shape(dims, dtype=F32):
    return jax.ShapeDtypeStruct(dims, dtype)


def unit():
    rows = lax.broadcasted_iota(jnp.int32, (HDIM, HDIM), 0)
    cols = lax.broadcasted_iota(jnp.int32, (HDIM, HDIM), 1)
    return rows == cols


def causal():
    rows = lax.broadcasted_iota(jnp.int32, (SPAN, SPAN), 0)
    cols = lax.broadcasted_iota(jnp.int32, (SPAN, SPAN), 1)
    return rows >= cols


def corner():
    rows = lax.broadcasted_iota(jnp.int32, (HDIM, HDIM), 0)
    cols = lax.broadcasted_iota(jnp.int32, (HDIM, HDIM), 1)
    return rows, cols


def fold(one, two):
    rows, cols = corner()
    both = jnp.where(rows <= cols, one, two)
    line = jnp.sum(jnp.where(rows == cols, two, 0.0), axis=0, keepdims=True)
    return both, jnp.broadcast_to(line, (8, HDIM))


def unfold(both, line):
    rows, cols = corner()
    turned = both.T
    one = jnp.where(rows <= cols, both, turned)
    two = jnp.where(rows > cols, both, turned)
    two = jnp.where(rows == cols, line[:1], two)
    return one, two


def folded(heads):
    return (heads + 1) // 2


def fold_into(ref, mats, base=0):
    for i in range(folded(len(mats))):
        one, two = mats[2 * i], mats[min(2 * i + 1, len(mats) - 1)]
        both, line = fold(one, two)
        top = base + i * (HDIM + 8)
        ref[top : top + HDIM, :] = both
        ref[top + HDIM : top + HDIM + 8, :] = line


def unfold_from(ref, heads, base=0):
    mats = []
    for i in range(folded(heads)):
        top = base + i * (HDIM + 8)
        mats += unfold(ref[top : top + HDIM, :], ref[top + HDIM : top + HDIM + 8, :])
    return mats[:heads]


def totals_kernel(begin_ref, k_ref, v_ref, g_ref, n_ref):
    grams = []
    for h in range(k_ref.shape[1] // HDIM):
        cols = slice(h * HDIM, (h + 1) * HDIM)
        k = k_ref[:, cols]
        both = dot(k, cat([k, v_ref[:, cols]], 1), (0, 0))
        grams.append(both[:, :HDIM])
        n_ref[cols, :] = both[:, HDIM:]
    fold_into(g_ref, grams)


def totals(begin, keys, values, heads):
    return pl.pallas_call(
        totals_kernel,
        out_shape=(shape((folded(heads) * (HDIM + 8), HDIM)), shape((heads * HDIM, HDIM))),
        in_specs=[VMEM_SPEC] * 3,
        out_specs=(VMEM_SPEC, VMEM_SPEC),
        compiler_params=params(),
        cost_estimate=cost(2 * 2 * keys.size * HDIM, 4 * keys.size),
    )(begin, keys, values)


def taken(refs, backward):
    total = None
    mine = lax.axis_index("ctx")
    for r, ref in enumerate(refs):
        bit = (mine >> r) & 1
        wanted = jnp.where(bit == (0 if backward else 1), 1.0, 0.0)
        part = ref[...].astype(F32) * wanted
        total = part if total is None else total + part
    return total


def places(q_ref, heads):
    blocks = q_ref.shape[0] // SPAN
    for h in range(heads):
        for b in range(blocks):
            yield h, b, h * blocks + b, slice(b * SPAN, (b + 1) * SPAN), slice(h * HDIM, (h + 1) * HDIM)


def inverse_kernel(rounds, k_ref, *refs):
    e_ref, x_ref, last_ref, a_ref, es, xs = refs[rounds:]
    heads = k_ref.shape[1] // HDIM
    eye = unit()
    grams = unfold_from(taken(refs[:rounds], False), heads)
    for h, b, i, rows, cols in places(k_ref, heads):
        ridged = grams[h] + jnp.where(eye, RIDGE, 0.0)
        scale = 1.0 / jnp.sqrt(jnp.sum(ridged * ridged, keepdims=True))
        a_ref[i] = ridged
        es[i] = ridged * scale
        xs[i] = jnp.where(eye, scale, 0.0)
        k = k_ref[rows, cols]
        grams[h] = grams[h] + dot(k, k, (0, 0))
    nil = jnp.zeros((HDIM, HDIM), BF16)

    def step(j, carry):
        for i in range(es.shape[0]):
            e, x = es[i], xs[i]
            eh, el = split(e)
            xh, xl = split(x)
            e_ref[j, i] = eh
            x_ref[j, i] = xh
            left = cat([cat([eh, el], 1), cat([xh, xl], 1)], 0)
            right = cat([cat([eh, el], 1), cat([eh, nil], 1)], 0)
            both = dot(left, right)
            both = both[:, :HDIM] + both[:, HDIM:]
            es[i] = 2.0 * e - both[:HDIM]
            xs[i] = 2.0 * x - both[HDIM:]
        return carry

    lax.fori_loop(0, NEWTON, step, 0)
    for i in range(xs.shape[0]):
        last_ref[i] = xs[i]


def inverses(keys, grams, count):
    stash = shape((NEWTON, count, HDIM, HDIM), BF16)
    state = shape((count, HDIM, HDIM))
    return pl.pallas_call(
        functools.partial(inverse_kernel, len(grams)),
        out_shape=(stash, stash, state, state),
        in_specs=[VMEM_SPEC] * (1 + len(grams)),
        out_specs=(VMEM_SPEC,) * 4,
        scratch_shapes=[pltpu.VMEM((count, HDIM, HDIM), F32)] * 2,
        compiler_params=params(),
        cost_estimate=cost(2_000_000_000, 8_000_000),
    )(keys, *grams)


def outputs_kernel(rounds, mark_ref, q_ref, k_ref, v_ref, last_ref, *refs):
    out_ref, pre_ref, s_ref, w_ref = refs[rounds:]
    prefix = taken(refs[:rounds], False)
    heads = q_ref.shape[1] // HDIM
    keep = causal()
    nil = jnp.zeros((HDIM, HDIM), BF16)
    pairs = [prefix[h * HDIM : (h + 1) * HDIM, :] for h in range(heads)]
    for h, b, i, rows, cols in places(q_ref, heads):
        q, k, v = q_ref[rows, cols], k_ref[rows, cols], v_ref[rows, cols]
        xh, xl = split(last_ref[i])
        sh, sl = split(dot(cat([q, q], 1), cat([xh, xl], 0)))
        both = cat([sh, sl], 1)
        s_ref[i] = both
        scores = dot(both, cat([k, k], 1), (1, 1))
        scores = jnp.where(keep, scores, 0.0).astype(BF16)
        w_ref[i] = scores
        nh, nl = split(pairs[h])
        pre_ref[i] = cat([nh, nl], 1)
        state = dot(both, cat([cat([nh, nl], 1), cat([nh, nil], 1)], 0))
        out = dot(scores, v) + state[:, :HDIM] + state[:, HDIM:]
        out_ref[rows, cols] = out.astype(BF16)
        pairs[h] = pairs[h] + dot(k, v, (0, 0))


def outputs(mark, queries, keys, values, last, pairs):
    count = last.shape[0]
    return pl.pallas_call(
        functools.partial(outputs_kernel, len(pairs)),
        out_shape=(
            shape(queries.shape, BF16),
            shape((count, HDIM, 2 * HDIM), BF16),
            shape((count, SPAN, 2 * HDIM), BF16),
            shape((count, SPAN, SPAN), BF16),
        ),
        in_specs=[VMEM_SPEC] * (5 + len(pairs)),
        out_specs=(VMEM_SPEC,) * 4,
        compiler_params=params(),
        cost_estimate=cost(2_000_000_000, 8_000_000),
    )(mark, queries, keys, values, last, *pairs)


def tangent_kernel(
    q_ref, k_ref, v_ref, do_ref, e_ref, x_ref, last_ref, a_ref, pre_ref, s_ref,
    p_ref, ds_ref, da_ref, dn_ref, sum_ref, send_ref, des, dxs, first,
):
    heads = q_ref.shape[1] // HDIM
    keep = causal()
    nil = jnp.zeros((HDIM, HDIM), BF16)
    for h, b, i, rows, cols in places(q_ref, heads):
        q, k, v, do = q_ref[rows, cols], k_ref[rows, cols], v_ref[rows, cols], do_ref[rows, cols]
        weights = jnp.where(keep, dot(do, v, (1, 1)), 0.0).astype(BF16)
        p_ref[i] = weights
        ds = dot(weights, k) + dot(cat([do, do], 1), pre_ref[i], (1, 1))
        ds = ds.astype(BF16)
        ds_ref[rows, cols] = ds
        state = dot(s_ref[i], do, (0, 0))
        dn_ref[i] = state[:HDIM] + state[HDIM:]
        bar = dot(q, ds, (0, 0))
        bar = bar + bar.T
        ridged = a_ref[i]
        scale = 1.0 / jnp.sqrt(jnp.sum(ridged * ridged, keepdims=True))
        first[i] = bar
        des[i] = bar * scale
        dxs[i] = jnp.zeros((HDIM, HDIM), F32)

    def step(j, carry):
        for i in range(des.shape[0]):
            e, x = e_ref[j, i], x_ref[j, i]
            de, dx = des[i], dxs[i]
            left = cat([cat([dx.astype(BF16), x], 1), cat([nil, e], 1)], 0)
            both = dot(left, cat([e, de.astype(BF16)], 0))
            turned = both[HDIM:]
            dxs[i] = 2.0 * dx - both[:HDIM]
            des[i] = 2.0 * de - (turned + turned.T)
        return carry

    lax.fori_loop(0, NEWTON, step, 0)
    sum_a = [jnp.zeros((HDIM, HDIM), F32) for _ in range(heads)]
    sum_n = [jnp.zeros((HDIM, HDIM), F32) for _ in range(heads)]
    for h, b, i, rows, cols in places(q_ref, heads):
        ridged, dx = a_ref[i], dxs[i]
        square = jnp.sum(ridged * ridged, keepdims=True)
        along = jnp.sum(first[i] * last_ref[i] + dx * ridged, keepdims=True)
        da = dx - (along / square) * ridged
        da_ref[i] = da
        sum_a[h] = sum_a[h] + da
        sum_n[h] = sum_n[h] + dn_ref[i]
    for h in range(heads):
        sum_ref[h * HDIM : (h + 1) * HDIM, :] = sum_n[h]
    fold_into(sum_ref, sum_a, heads * HDIM)
    send_ref[...] = sum_ref[...].astype(BF16)


def tangent(queries, keys, values, grads, stash):
    heads = queries.shape[1] // HDIM
    count = stash[-1].shape[0]
    state = shape((count, HDIM, HDIM))
    rows = heads * HDIM + folded(heads) * (HDIM + 8)
    return pl.pallas_call(
        tangent_kernel,
        out_shape=(
            shape((count, SPAN, SPAN), BF16), shape(queries.shape, BF16), state, state,
            shape((rows, HDIM)), shape((rows, HDIM), BF16),
        ),
        in_specs=[VMEM_SPEC] * 10,
        out_specs=(VMEM_SPEC,) * 6,
        scratch_shapes=[pltpu.VMEM((count, HDIM, HDIM), F32)] * 3,
        compiler_params=params(),
        cost_estimate=cost(4_000_000_000, 8_000_000),
    )(queries, keys, values, grads, *stash)


def rest_kernel(
    early_ref, k_ref, v_ref, do_ref, last_ref, s_ref, w_ref, p_ref, ds_ref, da_ref, dn_ref,
    dq_hbm, dk_ref, dv_ref, dq_ref, sems,
):
    heads = k_ref.shape[1] // HDIM
    sa, sn = [None] * heads, [None] * heads
    copies = []
    for h, b, i, rows, cols in reversed(list(places(k_ref, heads))):
        k, v, do, ds = k_ref[rows, cols], v_ref[rows, cols], do_ref[rows, cols], ds_ref[rows, cols]
        dq_ref[rows, cols] = dot(cat([ds, ds], 1), cat(split(last_ref[i]), 0)).astype(BF16)
        dk = dot(p_ref[i], s_ref[i, :, :HDIM], (0, 0))
        dv = dot(w_ref[i], do, (0, 0))
        if sa[h] is None:
            sa[h], sn[h] = da_ref[i], dn_ref[i]
        else:
            nh, nl = split(sn[h])
            dk = dk + dot(k, sa[h].astype(BF16)) + dot(cat([v, v], 1), cat([nh, nl], 1), (1, 1))
            dv = dv + dot(cat([k, k], 1), cat([nh, nl], 0))
            sa[h], sn[h] = sa[h] + da_ref[i], sn[h] + dn_ref[i]
        dk_ref[rows, cols] = dk
        dv_ref[rows, cols] = dv
        copies.append(
            pltpu.make_async_copy(dq_ref.at[rows, cols], dq_hbm.at[rows, cols], sems.at[i])
        )
        copies[-1].start()
    for copy in copies:
        copy.wait()


def rest(early, keys, values, grads, *stash):
    wide = shape(keys.shape)
    return pl.pallas_call(
        rest_kernel,
        out_shape=(shape(keys.shape, BF16), wide, wide),
        in_specs=[VMEM_SPEC] * 11,
        out_specs=(ANY_SPEC, VMEM_SPEC, VMEM_SPEC),
        scratch_shapes=[
            pltpu.VMEM(keys.shape, BF16),
            pltpu.SemaphoreType.DMA((stash[0].shape[0],)),
        ],
        compiler_params=params(),
        cost_estimate=cost(2_000_000_000, 6_000_000),
    )(early, keys, values, grads, *stash)


def finish_kernel(rounds, k_ref, v_ref, dk_ref, dv_ref, *refs):
    low_ref, pieces = refs[rounds], refs[rounds + 1 : -8]
    gk_hbm, gv_hbm, gw_hbm, gk_ref, gv_ref, gw_ref, sems, gw_sem = refs[-8:]
    gw_ref[...] = low_ref[...]
    for piece in pieces:
        gw_ref[...] += piece[...].astype(F32)
    gw_copy = pltpu.make_async_copy(gw_ref, gw_hbm, gw_sem)
    gw_copy.start()
    sums = taken(refs[:rounds], True)
    heads = k_ref.shape[1] // HDIM
    nil = jnp.zeros((HDIM, HDIM), BF16)
    right = []
    for h, sa in enumerate(unfold_from(sums, heads, heads * HDIM)):
        sn = sums[h * HDIM : (h + 1) * HDIM, :]
        top = cat([sa.astype(BF16), sn.astype(BF16)], 1)
        right.append(cat([top, cat([sn.T.astype(BF16), nil], 1)], 0))
    copies = []
    for b in range(k_ref.shape[0] // SPAN):
        rows = slice(b * SPAN, (b + 1) * SPAN)
        for h in range(heads):
            cols = slice(h * HDIM, (h + 1) * HDIM)
            total = dot(cat([k_ref[rows, cols], v_ref[rows, cols]], 1), right[h])
            gk_ref[rows, cols] = (dk_ref[rows, cols] + total[:, :HDIM]).astype(BF16)
            gv_ref[rows, cols] = (dv_ref[rows, cols] + total[:, HDIM:]).astype(BF16)
        for i, (ref, hbm) in enumerate(((gk_ref, gk_hbm), (gv_ref, gv_hbm))):
            copies.append(pltpu.make_async_copy(ref.at[rows], hbm.at[rows], sems.at[b, i]))
            copies[-1].start()
    for copy in copies:
        copy.wait()
    gw_copy.wait()


def finish(keys, values, dk, dv, sums, low, pieces):
    blocks = keys.shape[0] // SPAN
    return pl.pallas_call(
        functools.partial(finish_kernel, len(sums)),
        out_shape=(shape(keys.shape, BF16),) * 2 + (shape(low.shape),),
        in_specs=[VMEM_SPEC] * (5 + len(sums) + len(pieces)),
        out_specs=(ANY_SPEC,) * 3,
        scratch_shapes=[pltpu.VMEM(keys.shape, BF16)] * 2
        + [pltpu.VMEM(low.shape, F32)]
        + [pltpu.SemaphoreType.DMA((blocks, 2)), pltpu.SemaphoreType.DMA(())],
        compiler_params=params(),
        cost_estimate=cost(1_000_000_000, 6_000_000),
    )(keys, values, dk, dv, *sums, low, *pieces)


def lead_kernel(*refs):
    refs[-1][...] = jnp.zeros_like(refs[-1])


def lead(flops, *behind):
    return pl.pallas_call(
        lead_kernel,
        out_shape=shape((8, HDIM)),
        in_specs=[VMEM_SPEC] * len(behind),
        out_specs=VMEM_SPEC,
        compiler_params=params(),
        cost_estimate=cost(flops, 4096),
    )(*behind)


def grads_kernel(first, w_ref, *refs):
    out_ref = refs[-1]
    me = lax.axis_index("head")
    total = refs[0][...] if first else None
    for s, part in enumerate(refs[1:-1] if first else refs[:-1]):
        width = part.shape[1]
        cols = pl.ds(pl.multiple_of((me ^ (first + s)) * width, width), width)
        term = dot(part[...], w_ref[:, cols], (1, 1))
        total = term if total is None else total + term
    out_ref[...] = total.astype(out_ref.dtype)


def head_grads(w_out, parts, first, begun=None):
    rows = parts[0].shape[0]
    begun = [] if begun is None else [begun]
    return pl.pallas_call(
        functools.partial(grads_kernel, first),
        out_shape=shape((rows, w_out.shape[0]), BF16 if begun else F32),
        in_specs=[VMEM_SPEC] * (1 + len(parts) + len(begun)),
        out_specs=VMEM_SPEC,
        compiler_params=params(),
        cost_estimate=cost(rows * w_out.size, 4_000_000),
    )(w_out, *begun, *parts)


def columns_kernel(w_ref, *refs):
    me = lax.axis_index("head")
    for s, out_ref in enumerate(refs):
        width = out_ref.shape[2]
        for f in range(2):
            target = me ^ (2 * s + f)
            cols = pl.ds(pl.multiple_of(target * width, width), width)
            out_ref[f] = w_ref[:, cols]


def column_pieces(w_out, count):
    piece = shape((2, w_out.shape[0], w_out.shape[1] // count), BF16)
    return pl.pallas_call(
        columns_kernel,
        out_shape=(piece,) * (count // 2),
        in_specs=[VMEM_SPEC],
        out_specs=(VMEM_SPEC,) * (count // 2),
        compiler_params=params(),
        cost_estimate=cost(0, 4 * w_out.size),
    )(w_out)


def weights_kernel(h_ref, *refs):
    parts, outs, all_ref = refs[:-5], refs[-5:-1], refs[-1]
    me, mine = lax.axis_index("head"), lax.axis_index("ctx")
    count, _, width = all_ref.shape
    fold = parts[0].shape[1] // width
    for s, part in enumerate(parts):
        term = dot(h_ref[...], part[...], (0, 0)).astype(BF16)
        for f in range(fold):
            target = (me ^ s) * fold + f
            all_ref[target ^ mine] = term[:, f * width : (f + 1) * width]
    for t in range(count):
        ref = outs[2 * (t % 2) + (t >= count // 2)]
        ref[t % (count // 2) // 2] = all_ref[t]


def weight_terms(heads_out, parts, count):
    feats = sum(part.shape[1] for part in parts)
    piece = (heads_out.shape[1], feats // count)
    return pl.pallas_call(
        weights_kernel,
        out_shape=(shape((count // 4,) + piece, BF16),) * 4,
        in_specs=[VMEM_SPEC] * (1 + len(parts)),
        out_specs=(VMEM_SPEC,) * 4,
        scratch_shapes=[pltpu.VMEM((count,) + piece, BF16)],
        compiler_params=params(),
        cost_estimate=cost(2 * heads_out.size * feats, 6_000_000),
    )(heads_out, *parts)


def layer_kernel(mark_ref, *refs):
    hbm, ref, sems = refs[-3:]
    count = (len(refs) - 3) // 2
    step = ref.shape[0] // sems.shape[0]
    copies = []
    for b in range(sems.shape[0]):
        rows = slice(b * step, (b + 1) * step)
        total = None
        for s in range(count):
            term = dot(refs[s][rows, :], refs[count + s][...])
            total = term if total is None else total + term
        ref[rows, :] = total.astype(BF16)
        copies.append(pltpu.make_async_copy(ref.at[rows], hbm.at[rows], sems.at[b]))
        copies[-1].start()
    for copy in copies:
        copy.wait()


def layer(mark, parts, columns):
    rows, cols = parts[0].shape[0], columns[0].shape[1]
    return pl.pallas_call(
        layer_kernel,
        out_shape=shape((rows, cols), BF16),
        in_specs=[VMEM_SPEC] * (1 + len(parts) + len(columns)),
        out_specs=ANY_SPEC,
        scratch_shapes=[pltpu.VMEM((rows, cols), BF16), pltpu.SemaphoreType.DMA((4,))],
        compiler_params=params(),
        cost_estimate=cost(2 * rows * cols * sum(p.shape[1] for p in parts), 6_000_000),
    )(mark, *parts, *columns)


def swap(value, axis, distance):
    count = lax.axis_size(axis)
    return lax.ppermute(value, axis, [(i, i ^ distance) for i in range(count)])


def after(value, *others):
    return lax.optimization_barrier((value,) + others)[0]


def doublings(axis):
    return [1 << i for i in range((lax.axis_size(axis) - 1).bit_length())]


def shards(queries, keys, values, w_out, cotangent):
    heads = queries.shape[1] // HDIM
    count = heads * (queries.shape[0] // SPAN)
    head_count, ctx_count = lax.axis_size("head"), lax.axis_size("ctx")
    evens = range(2, head_count, 2)

    far = {s: swap(cotangent, "head", s) for s in evens}
    begin = lead(700_000_000)
    gram, pair = totals(begin, keys, values, heads)
    near = swap(after(cotangent, gram, pair), "head", 1)

    grams, pairs = [], []
    begun = None
    rounds = doublings("ctx")
    for r, distance in enumerate(rounds):
        grams.append(swap(gram, "ctx", distance))
        if begun is None:
            begun = head_grads(w_out, [cotangent, near], 0)
        if distance != rounds[-1]:
            gram = gram + grams[-1]
        if r:
            pairs[-1] = after(pairs[-1], gram)
            pair = pair + pairs[-1].astype(F32)
        pairs.append(swap(pair.astype(BF16), "ctx", distance))
    grams[-1] = after(grams[-1], begun)
    *stash, last, ridged = inverses(keys, grams, count)
    pairs[-1] = after(pairs[-1], last)
    parts = []
    for s in evens:
        parts += [far[s], swap(after(far[s], pairs[-1]), "head", 1)]
    columns = column_pieces(after(w_out, begun), head_count)
    columns = [after(c, pairs[-1]) for c in columns]
    columns = [swap(c, "head", 2 * s) if s else c for s, c in enumerate(columns)]
    mark = lead(1000, last)
    heads_out, states, solved, scores = outputs(mark, queries, keys, values, last, pairs)

    even_low, even_high, odd_low, odd_high = weight_terms(
        heads_out, [cotangent, near] + parts, ctx_count
    )
    high = swap(odd_high, "ctx", 1)
    grads = head_grads(w_out, parts, 2, after(begun, odd_low))

    weights, ds, da, dn, sums, send = tangent(
        queries, keys, values, grads, [*stash, last, ridged, states, solved]
    )

    low = swap(after(odd_low, send), "ctx", 1)
    outs_out = after(heads_out, send)
    outs_far = [swap(outs_out, "head", s) for s in evens]
    high = even_high.astype(F32) + after(high, send).astype(F32)
    half = ctx_count // 4
    aside = [swap(high[u].astype(BF16), "ctx", 2 * u) for u in range(1, half)]

    early = lead(1000, send)
    later, sends = [], []
    for distance in doublings("ctx"):
        sends.append(send)
        later.append(swap(send, "ctx", distance))
        sums = sums + later[-1].astype(F32)
        send = sums.astype(BF16)

    far_sum = high[0]
    for part in aside:
        far_sum = far_sum + after(part, sends[1]).astype(F32)
    moved = [swap(far_sum.astype(BF16), "ctx", 2 * half)]
    grad_queries, dk, dv = rest(
        early, keys, values, grads, last, solved, scores, weights, after(ds, sends[1]), da, dn
    )

    mark = lead(1000, dk)
    low = even_low.astype(F32) + after(low, dk).astype(F32)
    moved += [swap(low[u].astype(BF16), "ctx", 2 * u) for u in range(1, half)]
    outs = [heads_out, swap(outs_out, "head", 1)]
    for part in outs_far:
        outs += [part, swap(after(part, sends[-1]), "head", 1)]
    columns = [after(c, sends[1]) for c in columns]
    crossing = jnp.stack([c[1] for c in columns])
    crossing = swap(crossing, "head", 1)
    columns = [c for s in range(head_count // 2) for c in (columns[s][0], crossing[s])]
    layer_out = layer(mark, outs, columns)
    moved = [after(part, layer_out) for part in moved]
    grad_keys, grad_values, grad_weight = finish(keys, values, dk, dv, later, low[0], moved)
    return (layer_out, grad_queries, grad_keys, grad_values, grad_weight)


def solution(mesh):
    in_specs = (
        P("ctx", "head"),
        P("ctx", "head"),
        P("ctx", "head"),
        P("head", None),
        P("ctx", "head"),
    )
    out_specs = (
        P("ctx", "head"),
        P("ctx", "head"),
        P("ctx", "head"),
        P("ctx", "head"),
        P("head", "ctx"),
    )
    return jax.shard_map(shards, mesh=mesh, in_specs=in_specs, out_specs=out_specs, check_vma=False)
```

```python
import functools

import jax
import jax.numpy as jnp
from jax import lax
from jax.experimental import pallas as pl
from jax.experimental.pallas import tpu as pltpu
from jax.sharding import PartitionSpec as P


HDIM = 128
SPAN = 256
NEWTON = 8
RIDGE = 1.0
F32 = jnp.float32
BF16 = jnp.bfloat16
VMEM_SPEC = pl.BlockSpec(memory_space=pltpu.VMEM)
ANY_SPEC = pl.BlockSpec(memory_space=pl.ANY)


def dot(left, right, axes=(1, 0)):
    return lax.dot_general(
        left, right, (((axes[0],), (axes[1],)), ((), ())), preferred_element_type=F32
    )


def split(value):
    high = value.astype(BF16)
    return high, (value - high.astype(F32)).astype(BF16)


def cat(parts, axis):
    return jnp.concatenate(parts, axis=axis)


def params(limit=8):
    return pltpu.CompilerParams(vmem_limit_bytes=limit * 1024 * 1024)


def cost(flops, size):
    return pl.CostEstimate(flops=flops, bytes_accessed=size, transcendentals=0)


def shape(dims, dtype=F32):
    return jax.ShapeDtypeStruct(dims, dtype)


def unit():
    rows = lax.broadcasted_iota(jnp.int32, (HDIM, HDIM), 0)
    cols = lax.broadcasted_iota(jnp.int32, (HDIM, HDIM), 1)
    return rows == cols


def causal():
    rows = lax.broadcasted_iota(jnp.int32, (SPAN, SPAN), 0)
    cols = lax.broadcasted_iota(jnp.int32, (SPAN, SPAN), 1)
    return rows >= cols


def corner():
    rows = lax.broadcasted_iota(jnp.int32, (HDIM, HDIM), 0)
    cols = lax.broadcasted_iota(jnp.int32, (HDIM, HDIM), 1)
    return rows, cols


def fold(one, two):
    rows, cols = corner()
    both = jnp.where(rows <= cols, one, two)
    line = jnp.sum(jnp.where(rows == cols, two, 0.0), axis=0, keepdims=True)
    return both, jnp.broadcast_to(line, (8, HDIM))


def unfold(both, line):
    rows, cols = corner()
    turned = both.T
    one = jnp.where(rows <= cols, both, turned)
    two = jnp.where(rows > cols, both, turned)
    two = jnp.where(rows == cols, line[:1], two)
    return one, two


def folded(heads):
    return (heads + 1) // 2


def fold_into(ref, mats, base=0):
    for i in range(folded(len(mats))):
        one, two = mats[2 * i], mats[min(2 * i + 1, len(mats) - 1)]
        both, line = fold(one, two)
        top = base + i * (HDIM + 8)
        ref[top : top + HDIM, :] = both
        ref[top + HDIM : top + HDIM + 8, :] = line


def unfold_from(ref, heads, base=0):
    mats = []
    for i in range(folded(heads)):
        top = base + i * (HDIM + 8)
        mats += unfold(ref[top : top + HDIM, :], ref[top + HDIM : top + HDIM + 8, :])
    return mats[:heads]


def totals_kernel(begin_ref, k_ref, v_ref, g_ref, n_ref):
    grams = []
    for h in range(k_ref.shape[1] // HDIM):
        cols = slice(h * HDIM, (h + 1) * HDIM)
        k = k_ref[:, cols]
        both = dot(k, cat([k, v_ref[:, cols]], 1), (0, 0))
        grams.append(both[:, :HDIM])
        n_ref[cols, :] = both[:, HDIM:]
    fold_into(g_ref, grams)


def totals(begin, keys, values, heads):
    return pl.pallas_call(
        totals_kernel,
        out_shape=(shape((folded(heads) * (HDIM + 8), HDIM)), shape((heads * HDIM, HDIM))),
        in_specs=[VMEM_SPEC] * 3,
        out_specs=(VMEM_SPEC, VMEM_SPEC),
        compiler_params=params(),
        cost_estimate=cost(2 * 2 * keys.size * HDIM, 4 * keys.size),
    )(begin, keys, values)


def taken(refs, backward):
    total = None
    mine = lax.axis_index("ctx")
    for r, ref in enumerate(refs):
        bit = (mine >> r) & 1
        wanted = jnp.where(bit == (0 if backward else 1), 1.0, 0.0)
        part = ref[...].astype(F32) * wanted
        total = part if total is None else total + part
    return total


def places(q_ref, heads):
    blocks = q_ref.shape[0] // SPAN
    for h in range(heads):
        for b in range(blocks):
            yield h, b, h * blocks + b, slice(b * SPAN, (b + 1) * SPAN), slice(h * HDIM, (h + 1) * HDIM)


def inverse_kernel(rounds, k_ref, *refs):
    e_ref, x_ref, last_ref, a_ref, es, xs = refs[rounds:]
    heads = k_ref.shape[1] // HDIM
    eye = unit()
    grams = unfold_from(taken(refs[:rounds], False), heads)
    for h, b, i, rows, cols in places(k_ref, heads):
        ridged = grams[h] + jnp.where(eye, RIDGE, 0.0)
        scale = 1.0 / jnp.sqrt(jnp.sum(ridged * ridged, keepdims=True))
        a_ref[i] = ridged
        es[i] = ridged * scale
        xs[i] = jnp.where(eye, scale, 0.0)
        k = k_ref[rows, cols]
        grams[h] = grams[h] + dot(k, k, (0, 0))
    nil = jnp.zeros((HDIM, HDIM), BF16)

    def step(j, carry):
        for i in range(es.shape[0]):
            e, x = es[i], xs[i]
            eh, el = split(e)
            xh, xl = split(x)
            e_ref[j, i] = eh
            x_ref[j, i] = xh
            left = cat([cat([eh, el], 1), cat([xh, xl], 1)], 0)
            right = cat([cat([eh, el], 1), cat([eh, nil], 1)], 0)
            both = dot(left, right)
            both = both[:, :HDIM] + both[:, HDIM:]
            es[i] = 2.0 * e - both[:HDIM]
            xs[i] = 2.0 * x - both[HDIM:]
        return carry

    lax.fori_loop(0, NEWTON, step, 0)
    for i in range(xs.shape[0]):
        last_ref[i] = xs[i]


def inverses(keys, grams, count):
    stash = shape((NEWTON, count, HDIM, HDIM), BF16)
    state = shape((count, HDIM, HDIM))
    return pl.pallas_call(
        functools.partial(inverse_kernel, len(grams)),
        out_shape=(stash, stash, state, state),
        in_specs=[VMEM_SPEC] * (1 + len(grams)),
        out_specs=(VMEM_SPEC,) * 4,
        scratch_shapes=[pltpu.VMEM((count, HDIM, HDIM), F32)] * 2,
        compiler_params=params(),
        cost_estimate=cost(2_000_000_000, 8_000_000),
    )(keys, *grams)


def outputs_kernel(rounds, mark_ref, q_ref, k_ref, v_ref, last_ref, *refs):
    out_ref, pre_ref, s_ref, w_ref = refs[rounds:]
    prefix = taken(refs[:rounds], False)
    heads = q_ref.shape[1] // HDIM
    keep = causal()
    nil = jnp.zeros((HDIM, HDIM), BF16)
    pairs = [prefix[h * HDIM : (h + 1) * HDIM, :] for h in range(heads)]
    for h, b, i, rows, cols in places(q_ref, heads):
        q, k, v = q_ref[rows, cols], k_ref[rows, cols], v_ref[rows, cols]
        xh, xl = split(last_ref[i])
        sh, sl = split(dot(cat([q, q], 1), cat([xh, xl], 0)))
        both = cat([sh, sl], 1)
        s_ref[i] = both
        scores = dot(both, cat([k, k], 1), (1, 1))
        scores = jnp.where(keep, scores, 0.0).astype(BF16)
        w_ref[i] = scores
        nh, nl = split(pairs[h])
        pre_ref[i] = cat([nh.T, nl.T], 0)
        state = dot(both, cat([cat([nh, nl], 1), cat([nh, nil], 1)], 0))
        out = dot(scores, v) + state[:, :HDIM] + state[:, HDIM:]
        out_ref[rows, cols] = out.astype(BF16)
        pairs[h] = pairs[h] + dot(k, v, (0, 0))


def outputs(mark, queries, keys, values, last, pairs):
    count = last.shape[0]
    return pl.pallas_call(
        functools.partial(outputs_kernel, len(pairs)),
        out_shape=(
            shape(queries.shape, BF16),
            shape((count, 2 * HDIM, HDIM), BF16),
            shape((count, SPAN, 2 * HDIM), BF16),
            shape((count, SPAN, SPAN), BF16),
        ),
        in_specs=[VMEM_SPEC] * (5 + len(pairs)),
        out_specs=(VMEM_SPEC,) * 4,
        compiler_params=params(),
        cost_estimate=cost(2_000_000_000, 8_000_000),
    )(mark, queries, keys, values, last, *pairs)


def tangent_kernel(
    q_ref, k_ref, v_ref, do_ref, e_ref, x_ref, last_ref, a_ref, pre_ref, s_ref,
    p_ref, ds_ref, da_ref, dn_ref, sum_ref, send_ref, des, dxs, first,
):
    heads = q_ref.shape[1] // HDIM
    keep = causal()
    nil = jnp.zeros((HDIM, HDIM), BF16)
    for h, b, i, rows, cols in places(q_ref, heads):
        q, k, v, do = q_ref[rows, cols], k_ref[rows, cols], v_ref[rows, cols], do_ref[rows, cols]
        weights = jnp.where(keep, dot(do, v, (1, 1)), 0.0).astype(BF16)
        p_ref[i] = weights
        ds = dot(weights, k) + dot(cat([do, do], 1), pre_ref[i])
        ds = ds.astype(BF16)
        ds_ref[rows, cols] = ds
        state = dot(s_ref[i], do, (0, 0))
        dn_ref[i] = state[:HDIM] + state[HDIM:]
        bar = dot(q, ds, (0, 0))
        bar = bar + bar.T
        ridged = a_ref[i]
        scale = 1.0 / jnp.sqrt(jnp.sum(ridged * ridged, keepdims=True))
        first[i] = bar
        des[i] = bar * scale
        dxs[i] = jnp.zeros((HDIM, HDIM), F32)

    def step(j, carry):
        for i in range(des.shape[0]):
            e, x = e_ref[j, i], x_ref[j, i]
            de, dx = des[i], dxs[i]
            left = cat([cat([dx.astype(BF16), x], 1), cat([nil, e], 1)], 0)
            both = dot(left, cat([e, de.astype(BF16)], 0))
            turned = both[HDIM:]
            dxs[i] = 2.0 * dx - both[:HDIM]
            des[i] = 2.0 * de - (turned + turned.T)
        return carry

    lax.fori_loop(0, NEWTON, step, 0)
    sum_a = [jnp.zeros((HDIM, HDIM), F32) for _ in range(heads)]
    sum_n = [jnp.zeros((HDIM, HDIM), F32) for _ in range(heads)]
    for h, b, i, rows, cols in places(q_ref, heads):
        ridged, dx = a_ref[i], dxs[i]
        square = jnp.sum(ridged * ridged, keepdims=True)
        along = jnp.sum(first[i] * last_ref[i] + dx * ridged, keepdims=True)
        da = dx - (along / square) * ridged
        da_ref[i] = da
        sum_a[h] = sum_a[h] + da
        sum_n[h] = sum_n[h] + dn_ref[i]
    for h in range(heads):
        sum_ref[h * HDIM : (h + 1) * HDIM, :] = sum_n[h]
    fold_into(sum_ref, sum_a, heads * HDIM)
    send_ref[...] = sum_ref[...].astype(BF16)


def tangent(queries, keys, values, grads, stash):
    heads = queries.shape[1] // HDIM
    count = stash[-1].shape[0]
    state = shape((count, HDIM, HDIM))
    rows = heads * HDIM + folded(heads) * (HDIM + 8)
    return pl.pallas_call(
        tangent_kernel,
        out_shape=(
            shape((count, SPAN, SPAN), BF16), shape(queries.shape, BF16), state, state,
            shape((rows, HDIM)), shape((rows, HDIM), BF16),
        ),
        in_specs=[VMEM_SPEC] * 10,
        out_specs=(VMEM_SPEC,) * 6,
        scratch_shapes=[pltpu.VMEM((count, HDIM, HDIM), F32)] * 3,
        compiler_params=params(),
        cost_estimate=cost(4_000_000_000, 8_000_000),
    )(queries, keys, values, grads, *stash)


def rest_kernel(
    early_ref, k_ref, v_ref, do_ref, last_ref, s_ref, w_ref, p_ref, ds_ref, da_ref, dn_ref,
    dq_hbm, dk_ref, dv_ref, dq_ref, sems,
):
    heads = k_ref.shape[1] // HDIM
    sa, sn = [None] * heads, [None] * heads
    copies = []
    for h, b, i, rows, cols in reversed(list(places(k_ref, heads))):
        k, v, do, ds = k_ref[rows, cols], v_ref[rows, cols], do_ref[rows, cols], ds_ref[rows, cols]
        dq_ref[rows, cols] = dot(cat([ds, ds], 1), cat(split(last_ref[i]), 0)).astype(BF16)
        dk = dot(p_ref[i], s_ref[i, :, :HDIM], (0, 0))
        dv = dot(w_ref[i], do, (0, 0))
        if sa[h] is None:
            sa[h], sn[h] = da_ref[i], dn_ref[i]
        else:
            nh, nl = split(sn[h])
            dk = dk + dot(k, sa[h].astype(BF16)) + dot(cat([v, v], 1), cat([nh, nl], 1), (1, 1))
            dv = dv + dot(cat([k, k], 1), cat([nh, nl], 0))
            sa[h], sn[h] = sa[h] + da_ref[i], sn[h] + dn_ref[i]
        dk_ref[rows, cols] = dk
        dv_ref[rows, cols] = dv
        copies.append(
            pltpu.make_async_copy(dq_ref.at[rows, cols], dq_hbm.at[rows, cols], sems.at[i])
        )
        copies[-1].start()
    for copy in copies:
        copy.wait()


def rest(early, keys, values, grads, *stash):
    wide = shape(keys.shape)
    return pl.pallas_call(
        rest_kernel,
        out_shape=(shape(keys.shape, BF16), wide, wide),
        in_specs=[VMEM_SPEC] * 11,
        out_specs=(ANY_SPEC, VMEM_SPEC, VMEM_SPEC),
        scratch_shapes=[
            pltpu.VMEM(keys.shape, BF16),
            pltpu.SemaphoreType.DMA((stash[0].shape[0],)),
        ],
        compiler_params=params(),
        cost_estimate=cost(2_000_000_000, 6_000_000),
    )(early, keys, values, grads, *stash)


def finish_kernel(rounds, k_ref, v_ref, dk_ref, dv_ref, *refs):
    low_ref, pieces = refs[rounds], refs[rounds + 1 : -8]
    gk_hbm, gv_hbm, gw_hbm, gk_ref, gv_ref, gw_ref, sems, gw_sem = refs[-8:]
    gw_ref[...] = low_ref[...]
    for piece in pieces:
        gw_ref[...] += piece[...].astype(F32)
    gw_copy = pltpu.make_async_copy(gw_ref, gw_hbm, gw_sem)
    gw_copy.start()
    sums = taken(refs[:rounds], True)
    heads = k_ref.shape[1] // HDIM
    nil = jnp.zeros((HDIM, HDIM), BF16)
    right = []
    for h, sa in enumerate(unfold_from(sums, heads, heads * HDIM)):
        sn = sums[h * HDIM : (h + 1) * HDIM, :]
        top = cat([sa.astype(BF16), sn.astype(BF16)], 1)
        right.append(cat([top, cat([sn.T.astype(BF16), nil], 1)], 0))
    copies = []
    for b in range(k_ref.shape[0] // SPAN):
        rows = slice(b * SPAN, (b + 1) * SPAN)
        for h in range(heads):
            cols = slice(h * HDIM, (h + 1) * HDIM)
            total = dot(cat([k_ref[rows, cols], v_ref[rows, cols]], 1), right[h])
            gk_ref[rows, cols] = (dk_ref[rows, cols] + total[:, :HDIM]).astype(BF16)
            gv_ref[rows, cols] = (dv_ref[rows, cols] + total[:, HDIM:]).astype(BF16)
        for i, (ref, hbm) in enumerate(((gk_ref, gk_hbm), (gv_ref, gv_hbm))):
            copies.append(pltpu.make_async_copy(ref.at[rows], hbm.at[rows], sems.at[b, i]))
            copies[-1].start()
    for copy in copies:
        copy.wait()
    gw_copy.wait()


def finish(keys, values, dk, dv, sums, low, pieces):
    blocks = keys.shape[0] // SPAN
    return pl.pallas_call(
        functools.partial(finish_kernel, len(sums)),
        out_shape=(shape(keys.shape, BF16),) * 2 + (shape(low.shape),),
        in_specs=[VMEM_SPEC] * (5 + len(sums) + len(pieces)),
        out_specs=(ANY_SPEC,) * 3,
        scratch_shapes=[pltpu.VMEM(keys.shape, BF16)] * 2
        + [pltpu.VMEM(low.shape, F32)]
        + [pltpu.SemaphoreType.DMA((blocks, 2)), pltpu.SemaphoreType.DMA(())],
        compiler_params=params(),
        cost_estimate=cost(1_000_000_000, 6_000_000),
    )(keys, values, dk, dv, *sums, low, *pieces)


def lead_kernel(*refs):
    refs[-1][...] = jnp.zeros_like(refs[-1])


def lead(flops, *behind):
    return pl.pallas_call(
        lead_kernel,
        out_shape=shape((8, HDIM)),
        in_specs=[VMEM_SPEC] * len(behind),
        out_specs=VMEM_SPEC,
        compiler_params=params(),
        cost_estimate=cost(flops, 4096),
    )(*behind)


def grads_kernel(first, w_ref, *refs):
    out_ref = refs[-1]
    me = lax.axis_index("head")
    total = refs[0][...] if first else None
    for s, part in enumerate(refs[1:-1] if first else refs[:-1]):
        width = part.shape[1]
        cols = pl.ds(pl.multiple_of((me ^ (first + s)) * width, width), width)
        term = dot(part[...], w_ref[:, cols], (1, 1))
        total = term if total is None else total + term
    out_ref[...] = total.astype(out_ref.dtype)


def head_grads(w_out, parts, first, begun=None):
    rows = parts[0].shape[0]
    begun = [] if begun is None else [begun]
    return pl.pallas_call(
        functools.partial(grads_kernel, first),
        out_shape=shape((rows, w_out.shape[0]), BF16 if begun else F32),
        in_specs=[VMEM_SPEC] * (1 + len(parts) + len(begun)),
        out_specs=VMEM_SPEC,
        compiler_params=params(),
        cost_estimate=cost(rows * w_out.size, 4_000_000),
    )(w_out, *begun, *parts)


def columns_kernel(w_ref, *refs):
    me = lax.axis_index("head")
    for s, out_ref in enumerate(refs):
        width = out_ref.shape[2]
        for f in range(2):
            target = me ^ (2 * s + f)
            cols = pl.ds(pl.multiple_of(target * width, width), width)
            out_ref[f] = w_ref[:, cols]


def column_pieces(w_out, count):
    piece = shape((2, w_out.shape[0], w_out.shape[1] // count), BF16)
    return pl.pallas_call(
        columns_kernel,
        out_shape=(piece,) * (count // 2),
        in_specs=[VMEM_SPEC],
        out_specs=(VMEM_SPEC,) * (count // 2),
        compiler_params=params(),
        cost_estimate=cost(0, 4 * w_out.size),
    )(w_out)


def weights_kernel(h_ref, *refs):
    parts, outs, all_ref = refs[:-5], refs[-5:-1], refs[-1]
    me, mine = lax.axis_index("head"), lax.axis_index("ctx")
    count, _, width = all_ref.shape
    fold = parts[0].shape[1] // width
    for s, part in enumerate(parts):
        term = dot(h_ref[...], part[...], (0, 0)).astype(BF16)
        for f in range(fold):
            target = (me ^ s) * fold + f
            all_ref[target ^ mine] = term[:, f * width : (f + 1) * width]
    for t in range(count):
        ref = outs[2 * (t % 2) + (t >= count // 2)]
        ref[t % (count // 2) // 2] = all_ref[t]


def weight_terms(heads_out, parts, count):
    feats = sum(part.shape[1] for part in parts)
    piece = (heads_out.shape[1], feats // count)
    return pl.pallas_call(
        weights_kernel,
        out_shape=(shape((count // 4,) + piece, BF16),) * 4,
        in_specs=[VMEM_SPEC] * (1 + len(parts)),
        out_specs=(VMEM_SPEC,) * 4,
        scratch_shapes=[pltpu.VMEM((count,) + piece, BF16)],
        compiler_params=params(),
        cost_estimate=cost(2 * heads_out.size * feats, 6_000_000),
    )(heads_out, *parts)


def layer_kernel(mark_ref, *refs):
    hbm, ref, sems = refs[-3:]
    count = (len(refs) - 3) // 2
    step = ref.shape[0] // sems.shape[0]
    copies = []
    for b in range(sems.shape[0]):
        rows = slice(b * step, (b + 1) * step)
        total = None
        for s in range(count):
            term = dot(refs[s][rows, :], refs[count + s][...])
            total = term if total is None else total + term
        ref[rows, :] = total.astype(BF16)
        copies.append(pltpu.make_async_copy(ref.at[rows], hbm.at[rows], sems.at[b]))
        copies[-1].start()
    for copy in copies:
        copy.wait()


def layer(mark, parts, columns):
    rows, cols = parts[0].shape[0], columns[0].shape[1]
    return pl.pallas_call(
        layer_kernel,
        out_shape=shape((rows, cols), BF16),
        in_specs=[VMEM_SPEC] * (1 + len(parts) + len(columns)),
        out_specs=ANY_SPEC,
        scratch_shapes=[pltpu.VMEM((rows, cols), BF16), pltpu.SemaphoreType.DMA((4,))],
        compiler_params=params(),
        cost_estimate=cost(2 * rows * cols * sum(p.shape[1] for p in parts), 6_000_000),
    )(mark, *parts, *columns)


def swap(value, axis, distance):
    count = lax.axis_size(axis)
    return lax.ppermute(value, axis, [(i, i ^ distance) for i in range(count)])


def after(value, *others):
    return lax.optimization_barrier((value,) + others)[0]


def doublings(axis):
    return [1 << i for i in range((lax.axis_size(axis) - 1).bit_length())]


def shards(queries, keys, values, w_out, cotangent):
    heads = queries.shape[1] // HDIM
    count = heads * (queries.shape[0] // SPAN)
    head_count, ctx_count = lax.axis_size("head"), lax.axis_size("ctx")
    evens = range(2, head_count, 2)

    far = {s: swap(cotangent, "head", s) for s in evens}
    begin = lead(700_000_000)
    gram, pair = totals(begin, keys, values, heads)
    near = swap(after(cotangent, gram, pair), "head", 1)

    grams, pairs = [], []
    begun = None
    rounds = doublings("ctx")
    for r, distance in enumerate(rounds):
        grams.append(swap(gram, "ctx", distance))
        if begun is None:
            begun = head_grads(w_out, [cotangent, near], 0)
        if distance != rounds[-1]:
            gram = gram + grams[-1]
        if r:
            pairs[-1] = after(pairs[-1], gram)
            pair = pair + pairs[-1].astype(F32)
        pairs.append(swap(pair.astype(BF16), "ctx", distance))
    grams[-1] = after(grams[-1], begun)
    *stash, last, ridged = inverses(keys, grams, count)
    pairs[-1] = after(pairs[-1], last)
    parts = []
    for s in evens:
        parts += [far[s], swap(after(far[s], pairs[-1]), "head", 1)]
    columns = column_pieces(after(w_out, begun), head_count)
    columns = [after(c, pairs[-1]) for c in columns]
    columns = [swap(c, "head", 2 * s) if s else c for s, c in enumerate(columns)]
    mark = lead(1000, last)
    heads_out, states, solved, scores = outputs(mark, queries, keys, values, last, pairs)

    even_low, even_high, odd_low, odd_high = weight_terms(
        heads_out, [cotangent, near] + parts, ctx_count
    )
    high = swap(odd_high, "ctx", 1)
    grads = head_grads(w_out, parts, 2, after(begun, odd_low))

    weights, ds, da, dn, sums, send = tangent(
        queries, keys, values, grads, [*stash, last, ridged, states, solved]
    )

    low = swap(after(odd_low, send), "ctx", 1)
    outs_out = after(heads_out, send)
    outs_far = [swap(outs_out, "head", s) for s in evens]
    high = even_high.astype(F32) + after(high, send).astype(F32)
    half = ctx_count // 4
    aside = [swap(high[u].astype(BF16), "ctx", 2 * u) for u in range(1, half)]

    early = lead(1000, send)
    later, sends = [], []
    for distance in doublings("ctx"):
        sends.append(send)
        later.append(swap(send, "ctx", distance))
        sums = sums + later[-1].astype(F32)
        send = sums.astype(BF16)

    far_sum = high[0]
    for part in aside:
        far_sum = far_sum + after(part, sends[1]).astype(F32)
    moved = [swap(far_sum.astype(BF16), "ctx", 2 * half)]
    grad_queries, dk, dv = rest(
        early, keys, values, grads, last, solved, scores, weights, after(ds, sends[1]), da, dn
    )

    mark = lead(1000, dk)
    low = even_low.astype(F32) + after(low, dk).astype(F32)
    moved += [swap(low[u].astype(BF16), "ctx", 2 * u) for u in range(1, half)]
    outs = [heads_out, swap(outs_out, "head", 1)]
    for part in outs_far:
        outs += [part, swap(after(part, sends[-1]), "head", 1)]
    columns = [after(c, sends[1]) for c in columns]
    crossing = jnp.stack([c[1] for c in columns])
    crossing = swap(crossing, "head", 1)
    columns = [c for s in range(head_count // 2) for c in (columns[s][0], crossing[s])]
    layer_out = layer(mark, outs, columns)
    moved = [after(part, layer_out) for part in moved]
    grad_keys, grad_values, grad_weight = finish(keys, values, dk, dv, later, low[0], moved)
    return (layer_out, grad_queries, grad_keys, grad_values, grad_weight)


def solution(mesh):
    in_specs = (
        P("ctx", "head"),
        P("ctx", "head"),
        P("ctx", "head"),
        P("head", None),
        P("ctx", "head"),
    )
    out_specs = (
        P("ctx", "head"),
        P("ctx", "head"),
        P("ctx", "head"),
        P("ctx", "head"),
        P("head", "ctx"),
    )
    return jax.shard_map(shards, mesh=mesh, in_specs=in_specs, out_specs=out_specs, check_vma=False)
```
